32 devices in a mesh: groups: 2 (over y), frames: 4 (over z), rows: 4 (over x, core).
Axes of the slice: x: 2, y: 2, z: 4, core: 2. Of those that a mesh axis runs over, the one named last changes fastest.
Arguments:
- latents: bfloat16 [16, 8, 16, 1280], P('rows', ('groups', 'frames')), parts along dimension 1, may hold values from -6 to 6
- spatial_weight: bfloat16 [3, 3, 1280, 1280], P(None, None, None, 'rows'), may hold values from -0.0546875 to 0.0546875
- spatial_bias: float32 [1280], P('rows'), may hold values from -3 to 3
- norm_gain: float32 [1280], P('rows'), may hold values from 0.1 to 1.9
- norm_shift: float32 [1280], P('rows'), may hold values from -3 to 3
- temporal_weight: bfloat16 [3, 1280, 1280], P(None, 'rows'), may hold values from -0.09375 to 0.09375
- temporal_bias: float32 [1280], replicated, may hold values from -3 to 3
- token_gain: float32 [1280], replicated, may hold values from 0.1 to 1.9
- query_weight: bfloat16 [1280, 1024], P(None, 'rows'), may hold values from -4 to 4
- key_weight: bfloat16 [1280, 1024], P(None, 'rows'), may hold values from -4 to 4
- value_weight: bfloat16 [1280, 1024], P(None, 'rows'), may hold values from -0.15625 to 0.15625
- output_weight: bfloat16 [1024, 1280], P('rows'), may hold values from -0.1875 to 0.1875
Outputs:
- denoised: bfloat16 [16, 8, 16, 1280], P('rows', ('groups', 'frames')), parts along dimension 1
The draws below stay inside these ranges and needn't reach their ends.
There are 2 independent parts, one for each index of `groups`. The reference program is written for one: setup_inputs(seed, part) draws one part's arguments, and reference() takes and returns one part's arrays. A program takes and returns all parts, laid end to end along the dimension named above; an argument that names none is the same for every part. Nothing has to cross between parts.
All inputs are finite; a program needn't handle non-finite values.
Results may differ from the reference program's by a relative error of at most 0.034.
Values may be sent and summed in bfloat16 or wider, within the bound.
A program may use at most 128 MiB of HBM per device.

```python
import math
import jax
import jax.numpy as jnp
from jax import lax

C = 1280
HEADS = 16
HD = 64
NORM_GROUPS = 32
LAT_H = 16
LAT_W = 16
FRAMES = 4
TOKENS = 1024


def shared_basis(key):
    base = jax.random.normal(jax.random.fold_in(key, 101), (C, HEADS * HD), jnp.float32)
    return jnp.clip(base, -5.0, 5.0) / math.sqrt(C)


def own_part(key, salt):
    noise = jax.random.normal(jax.random.fold_in(key, salt), (C, HEADS * HD), jnp.float32)
    return jnp.clip(noise, -5.0, 5.0) / math.sqrt(C)


def draw_query_weight(key, part):
    mixed = 0.6 * shared_basis(key) + 0.8 * own_part(key, 102)
    return jnp.clip(mixed, -4.0, 4.0).astype(jnp.bfloat16)


def draw_key_weight(key, part):
    mixed = 0.6 * shared_basis(key) + 0.8 * own_part(key, 103)
    return jnp.clip(mixed, -4.0, 4.0).astype(jnp.bfloat16)


def shard_levels(rng, dims, pieces, smallest, high):
    loudness, own = 1.0, jax.random.fold_in(rng, 6)
    for dim, shards_of in pieces:
        steps = jnp.exp(jax.random.uniform(jax.random.fold_in(own, dim), (shards_of,), jnp.float32, smallest / len(pieces), high / len(pieces)))
        loudness = loudness * jnp.repeat(steps, dims[dim] // shards_of).reshape([-1 if axis == dim else 1 for axis in range(len(dims))])
    return loudness


def normal_values(rng, shape, width, most, shards=(), kind=jnp.bfloat16):
    entries = width * jax.random.normal(rng, shape, jnp.float32)
    if shards:
        entries = entries * shard_levels(rng, shape, shards, -0.22, 0.18)
    return jnp.clip(entries, -most, most).astype(kind)


def setup_inputs(seed: int = 0, part: int = 0) -> dict:
    splits = jax.random.split(jax.random.key(seed), 13)
    part_splits = jax.random.split(jax.random.fold_in(splits[12], part), 13)
    return {
        "latents": normal_values(part_splits[0], (LAT_H, FRAMES, LAT_W, C), 1.0, 6.0, ((0, 4), (1, 4))),
        "spatial_weight": normal_values(splits[1], (3, 3, C, C), (9 * C) ** -0.5, 0.0546875, ((3, 4),)),
        "spatial_bias": normal_values(splits[2], (C,), 0.5, 3.0, ((0, 4),), jnp.float32),
        "norm_gain": jnp.clip(1.0 + 0.18 * jax.random.normal(splits[3], (C,), jnp.float32), 0.1, 1.9),
        "norm_shift": normal_values(splits[4], (C,), 0.5, 3.0, ((0, 4),), jnp.float32),
        "temporal_weight": normal_values(splits[5], (3, C, C), (3 * C) ** -0.5, 0.09375, ((1, 4),)),
        "temporal_bias": normal_values(splits[6], (C,), 0.5, 3.0, (), jnp.float32),
        "token_gain": jnp.clip(1.0 + 0.18 * jax.random.normal(splits[7], (C,), jnp.float32), 0.1, 1.9),
        "query_weight": draw_query_weight(jax.random.fold_in(splits[12], 71), part),
        "key_weight": draw_key_weight(jax.random.fold_in(splits[12], 71), part),
        "value_weight": normal_values(splits[10], (C, HEADS * HD), C ** -0.5, 0.15625, ((1, 4),)),
        "output_weight": normal_values(splits[11], (HEADS * HD, C), (HEADS * HD) ** -0.5, 0.1875, ((0, 4),)),
    }


def conv_plane(field, weight, bias):
    rows_n, frames_n, cols_n, chans = field.shape
    padded = jnp.pad(field, ((1, 1), (0, 0), (1, 1), (0, 0)))
    total = jnp.zeros((rows_n * frames_n * cols_n, weight.shape[3]), jnp.float32)
    for row_off in range(3):
        for col_off in range(3):
            window = padded[row_off:row_off + rows_n, :, col_off:col_off + cols_n, :].reshape(-1, chans)
            total = total + jnp.dot(window, weight[row_off, col_off], preferred_element_type=jnp.float32)
    return total.reshape(rows_n, frames_n, cols_n, -1) + bias

def head_attention(query, keys, values):
    block = math.gcd(query.shape[0], 1024)
    scale = 1.0 / math.sqrt(HD)

    def one_block(query_block):
        scores = jnp.dot(query_block, keys.T, preferred_element_type=jnp.float32) * scale
        peak = lax.optimization_barrier(jnp.max(scores, axis=-1, keepdims=True))
        weights = jnp.exp(scores - peak)
        denominator = lax.optimization_barrier(jnp.sum(weights, axis=-1, keepdims=True))
        return jnp.dot(weights.astype(jnp.bfloat16), values, preferred_element_type=jnp.float32) / denominator
    return lax.map(one_block, query.reshape(-1, block, HD)).reshape(-1, HD)

def reference(latents, spatial_weight, spatial_bias, norm_gain, norm_shift, temporal_weight, temporal_bias, token_gain, query_weight, key_weight, value_weight, output_weight):
    spatial = conv_plane(latents, spatial_weight, spatial_bias)
    grouped = spatial.reshape(LAT_H, FRAMES, LAT_W, NORM_GROUPS, -1)
    group_mean = lax.optimization_barrier(jnp.mean(grouped, axis=(0, 2, 4), keepdims=True))
    centred = grouped - group_mean
    group_var = lax.optimization_barrier(jnp.mean(centred * centred, axis=(0, 2, 4), keepdims=True))
    scaled = (centred / jnp.sqrt(group_var + 1e-05)).reshape(LAT_H, FRAMES, LAT_W, C) * norm_gain + norm_shift
    activated = jax.nn.silu(scaled).astype(jnp.bfloat16)
    rim = jnp.pad(activated, ((0, 0), (1, 1), (0, 0), (0, 0)))
    temporal = jnp.zeros((LAT_H * FRAMES * LAT_W, C), jnp.float32)
    for lag_index in range(3):
        window = rim[:, lag_index:lag_index + FRAMES].reshape(-1, C)
        temporal = temporal + jnp.dot(window, temporal_weight[lag_index], preferred_element_type=jnp.float32)
    temporal = temporal.reshape(LAT_H, FRAMES, LAT_W, C) + temporal_bias
    hidden = (latents.astype(jnp.float32) + temporal).astype(jnp.bfloat16)
    flat = hidden.reshape(-1, C).astype(jnp.float32)
    token_mean = lax.optimization_barrier(jnp.mean(flat, axis=-1, keepdims=True))
    shifted = flat - token_mean
    token_var = lax.optimization_barrier(jnp.mean(shifted * shifted, axis=-1, keepdims=True))
    normed = (shifted / jnp.sqrt(token_var + 1e-05) * token_gain).astype(jnp.bfloat16)
    queries = jnp.dot(normed, query_weight, preferred_element_type=jnp.float32).astype(jnp.bfloat16)
    keys = jnp.dot(normed, key_weight, preferred_element_type=jnp.float32).astype(jnp.bfloat16)
    values = jnp.dot(normed, value_weight, preferred_element_type=jnp.float32).astype(jnp.bfloat16)

    def by_head(array):
        return array.reshape(TOKENS, HEADS, HD).transpose(1, 0, 2)
    per_head = lax.map(lambda trio: head_attention(trio[0], trio[1], trio[2]), (by_head(queries), by_head(keys), by_head(values)))
    attended = per_head.transpose(1, 0, 2).reshape(TOKENS, HEADS * HD).astype(jnp.bfloat16)
    projected = jnp.dot(attended, output_weight, preferred_element_type=jnp.float32)
    denoised = hidden.reshape(-1, C).astype(jnp.float32) + projected
    return denoised.reshape(LAT_H, FRAMES, LAT_W, C).astype(jnp.bfloat16)
```

```python
import functools
import math

import jax
import jax.numpy as jnp
from jax import lax
from jax.experimental import pallas as pl
from jax.experimental.pallas import tpu as pltpu
from jax.sharding import PartitionSpec as P

HD = 64
NORM_GROUPS = 32


def padded_2(array, sides, width):
    for axis, dim in sides:
        peers, length = (lax.axis_size(axis), array.shape[dim])
        up = [(i, (i + 1) % peers) for i in range(peers - 1)]
        down = [(j, i) for i, j in up]
        last = lax.slice_in_dim(array, length - width, length, axis=dim)
        leading = lax.slice_in_dim(array, 0, width, axis=dim)
        before = lax.ppermute(last, axis, up)
        after = lax.ppermute(leading, axis, down)
        array = jnp.concatenate([before, array, after], axis=dim)
    return array


def shifted_2(value, axis, steps):
    count = lax.axis_size(axis)
    pairs = [(source, (source + steps) % count) for source in range(count)]
    return lax.ppermute(value, axis, pairs)


def conv_plane(field, weight, bias):
    rows_n, frames_n, cols_n, chans = field.shape
    padded = jnp.pad(field, ((1, 1), (0, 0), (1, 1), (0, 0)))
    total = jnp.zeros((rows_n * frames_n * cols_n, weight.shape[3]), jnp.float32)
    for row_off in range(3):
        for col_off in range(3):
            window = padded[row_off : row_off + rows_n, :, col_off : col_off + cols_n, :].reshape(
                -1, chans
            )
            total = total + jnp.dot(
                window, weight[row_off, col_off], preferred_element_type=jnp.float32
            )
    return total.reshape(rows_n, frames_n, cols_n, -1) + bias


def layer_norm(field, token_gain):
    flat = field.astype(jnp.float32)
    token_mean = jnp.mean(flat, axis=-1, keepdims=True)
    shifted = flat - token_mean
    token_var = jnp.mean(shifted * shifted, axis=-1, keepdims=True)
    return (shifted / jnp.sqrt(token_var + 1e-05) * token_gain).astype(jnp.bfloat16)


def attend(queries, carried, keys, values):
    block = queries.shape[0]
    head_count = queries.shape[1]
    block_count = keys.shape[0] // block
    key_blocks = keys.reshape(block_count, block, head_count, HD)
    value_blocks = values.reshape(block_count, block, head_count, HD)
    scale = 1.0 / math.sqrt(HD)

    def visit_block(state, block_pair):
        running_max, denominator, numerator = state
        key_block, value_block = block_pair
        scores = (
            jnp.einsum("qhd,khd->qhk", queries, key_block, preferred_element_type=jnp.float32)
            * scale
        )
        new_max = jnp.maximum(running_max, jnp.max(scores, axis=-1))
        shrink = jnp.exp(running_max - new_max)
        weights = jnp.exp(scores - new_max[..., None])
        denominator = denominator * shrink + jnp.sum(weights, axis=-1)
        numerator = numerator * shrink[..., None] + jnp.einsum(
            "qhk,khd->qhd",
            weights.astype(jnp.bfloat16),
            value_block,
            preferred_element_type=jnp.float32,
        )
        return ((new_max, denominator, numerator), None)

    result, _ = lax.scan(visit_block, carried, (key_blocks, value_blocks))
    return result


def body(
    latents,
    spatial_weight,
    spatial_bias,
    norm_gain,
    norm_shift,
    temporal_weight,
    temporal_bias,
    token_gain,
    query_weight,
    key_weight,
    value_weight,
    output_weight,
):
    row_count, frame_count, width_cells, channels = latents.shape
    plane = lax.all_gather(latents, "rows", axis=0, tiled=True)
    plane_rows = plane.shape[0]
    local_out = spatial_weight.shape[3]
    spatial = conv_plane(plane, spatial_weight, spatial_bias)
    local_groups = NORM_GROUPS // lax.axis_size("rows")
    grouped = spatial.reshape(plane_rows, frame_count, width_cells, local_groups, -1)
    group_mean = jnp.mean(grouped, axis=(0, 2, 4), keepdims=True)
    centred = grouped - group_mean
    group_var = jnp.mean(centred * centred, axis=(0, 2, 4), keepdims=True)
    scaled = (centred / jnp.sqrt(group_var + 1e-05)).reshape(
        plane_rows, frame_count, width_cells, local_out
    ) * norm_gain + norm_shift
    activated = jax.nn.silu(scaled).astype(jnp.bfloat16)
    rim = padded_2(activated, (("frames", 1),), 1)
    row_total = row_count * lax.axis_size("rows")
    row_piece = rim
    total = jnp.zeros((row_total * frame_count * width_cells, channels), jnp.float32)
    for lag_index in range(3):
        window = row_piece[:, lag_index : lag_index + frame_count].reshape(-1, local_out)
        total = total + jnp.dot(
            window, temporal_weight[lag_index], preferred_element_type=jnp.float32
        )
    temporal = lax.psum_scatter(
        total.reshape(row_total, frame_count, width_cells, channels).astype(jnp.bfloat16),
        "rows",
        scatter_dimension=0,
        tiled=True,
    ).astype(jnp.float32)
    hidden = (latents.astype(jnp.float32) + temporal + temporal_bias).astype(jnp.bfloat16)
    normed_all = lax.all_gather(layer_norm(hidden, token_gain), "rows", axis=0, tiled=True)
    flat = normed_all.reshape(-1, channels)
    head_cols = query_weight.shape[1]
    head_count = head_cols // HD
    token_count = flat.shape[0]
    queries = jnp.dot(flat, query_weight, preferred_element_type=jnp.float32).astype(jnp.bfloat16)
    keys = jnp.dot(flat, key_weight, preferred_element_type=jnp.float32).astype(jnp.bfloat16)
    values = jnp.dot(flat, value_weight, preferred_element_type=jnp.float32).astype(jnp.bfloat16)
    start_state = (
        jnp.full((token_count, head_count), -1e30, jnp.float32),
        jnp.zeros((token_count, head_count), jnp.float32),
        jnp.zeros((token_count, head_count, HD), jnp.float32),
    )
    local_keys = keys.reshape(token_count, head_count, HD)
    local_values = values.reshape(token_count, head_count, HD)

    def travel(turn, state):
        query_moving, running_max, denominator, numerator = state
        running_max, denominator, numerator = attend(
            query_moving, (running_max, denominator, numerator), local_keys, local_values
        )
        return (
            shifted_2(query_moving, "frames", 1),
            shifted_2(running_max.astype(jnp.bfloat16), "frames", 1).astype(running_max.dtype),
            shifted_2(denominator.astype(jnp.bfloat16), "frames", 1).astype(denominator.dtype),
            shifted_2(numerator.astype(jnp.bfloat16), "frames", 1).astype(numerator.dtype),
        )

    start_moving = queries.reshape(token_count, head_count, HD)
    final = lax.fori_loop(0, lax.axis_size("frames"), travel, (start_moving,) + start_state)
    denominator, numerator = (final[2], final[3])
    attended = (
        (numerator / denominator[..., None])
        .astype(jnp.bfloat16)
        .reshape(plane_rows, frame_count, width_cells, head_cols)
    )
    row_piece = attended
    mixed = lax.psum_scatter(
        jnp.dot(row_piece.reshape(-1, head_cols), output_weight, preferred_element_type=jnp.float32)
        .reshape(row_count * lax.axis_size("rows"), frame_count, width_cells, channels)
        .astype(jnp.bfloat16),
        "rows",
        scatter_dimension=0,
        tiled=True,
    ).astype(jnp.float32)
    return (hidden.astype(jnp.float32) + mixed).astype(jnp.bfloat16)


MESH = pl.DeviceIdType.MESH
DMA = pltpu.SemaphoreType.DMA
VMEM_SPEC = pl.BlockSpec(memory_space=pltpu.VMEM)
ANY_SPEC = pl.BlockSpec(memory_space=pl.ANY)
BF16 = jnp.bfloat16
F32 = jnp.float32
VMEM_LIMIT = 54 << 20
PARTS = 2
CHUNK = 256


def remote(src, dst, send, recv, axis, peer):
    return pltpu.make_async_remote_copy(
        src_ref=src,
        dst_ref=dst,
        send_sem=send,
        recv_sem=recv,
        device_id={axis: peer},
        device_id_type=MESH,
    )


def greet(barrier, axis, peer):
    pl.semaphore_signal(barrier, inc=1, device_id={axis: peer}, device_id_type=MESH)


class Gather:
    def __init__(self, block, out, send, recv):
        me = lax.axis_index("rows")
        near, far = me ^ 1, me ^ 2
        step = block.shape[0] // PARTS
        self.far, self.onward = [], []
        for part in range(PARTS):
            piece = pl.ds(part * step, step)
            self.far.append(
                remote(
                    block.at[piece],
                    out.at[me, piece],
                    send.at[part],
                    recv.at[part],
                    "rows",
                    far,
                )
            )
            self.onward.append(
                remote(
                    out.at[far, piece],
                    out.at[far, piece],
                    send.at[PARTS + part],
                    recv.at[PARTS + part],
                    "rows",
                    near,
                )
            )
        self.near = remote(
            block, out.at[me], send.at[2 * PARTS], recv.at[2 * PARTS], "rows", near
        )

    def start(self):
        for copy in self.far:
            copy.start()
        self.near.start()

    def near_ready(self):
        self.near.wait_recv()

    def finish(self):
        for copy, onward in zip(self.far, self.onward):
            copy.wait_recv()
            onward.start()
        for copy in self.far:
            copy.wait_send()
        self.near.wait_send()
        for onward in self.onward:
            onward.wait()


def reduce_rows(term, sent, got_near, got_far, send, recv):
    me = lax.axis_index("rows")
    near, far = me ^ 1, me ^ 2

    def hand(slot, value):
        sent[slot] = value.astype(BF16)
        copy = remote(
            sent.at[slot], got_near.at[slot], send.at[slot], recv.at[slot], "rows", near
        )
        copy.start()
        return copy

    first = hand(0, term(far ^ 1, 0))
    mine = term(far, 1)
    first.wait_recv()
    sent[2] = (mine + got_near[0].astype(F32)).astype(BF16)
    across = remote(sent.at[2], got_far, send.at[2], recv.at[2], "rows", far)
    across.start()
    second = hand(1, term(near, 2))
    mine = term(me, 3)
    second.wait_recv()
    mine = mine + got_near[1].astype(F32)
    across.wait_recv()
    total = mine + got_far[...].astype(F32)
    for copy in (first, second, across):
        copy.wait_send()
    return total


def row(ref):
    return ref[...].reshape(1, -1)


def column(ref):
    value = jnp.broadcast_to(row(ref), (8, ref.shape[0]))
    return value.T[:, :1]


def convolve_chunk(plane, shifted, weight, chunk, width):
    blocks, size, depth = plane.shape
    tokens = blocks * size
    edge = jnp.zeros((width, depth), BF16)
    place = lax.broadcasted_iota(jnp.int32, (size, depth), 0) % width
    for offset in range(3):
        shifted[offset, :width, :] = edge
        shifted[offset, tokens + width :, :] = edge
    for block in range(blocks):
        rows = slice(width + block * size, width + (block + 1) * size)
        value = plane[block]
        wide = value.astype(F32)
        before = jnp.where(place == 0, 0.0, pltpu.roll(wide, 1, 0))
        after = jnp.where(place == width - 1, 0.0, pltpu.roll(wide, size - 1, 0))
        shifted[0, rows, :] = before.astype(BF16)
        shifted[1, rows, :] = value
        shifted[2, rows, :] = after.astype(BF16)
    total = None
    for row_off in range(3):
        for col_off in range(3):
            window = shifted[col_off, row_off * width : row_off * width + tokens, :]
            part = lax.dot_general(
                weight[row_off, col_off, :, chunk * depth : (chunk + 1) * depth],
                window,
                (((1,), (1,)), ((), ())),
                preferred_element_type=F32,
            )
            total = part if total is None else total + part
    return total


def group_norm_silu(spatial, gain, shift, groups):
    channels, tokens = spatial.shape

    def group_mean(value):
        return jnp.mean(value, axis=(1, 2), keepdims=True)

    grouped = spatial.reshape(groups, channels // groups, tokens)
    centred = grouped - group_mean(grouped)
    scale = 1.0 / jnp.sqrt(group_mean(centred * centred) + 1e-05)
    value = (centred * scale).reshape(channels, tokens) * gain + shift
    return (value / (1.0 + jnp.exp(-value))).T.astype(BF16)


def block_kernel(
    frames,
    width_cells,
    groups,
    latents_hbm,
    spatial_hbm,
    bias_hbm,
    gain_hbm,
    shift_hbm,
    temporal_hbm,
    temporal_bias_hbm,
    token_gain_hbm,
    query_hbm,
    key_hbm,
    value_hbm,
    output_hbm,
    out_ref,
    chunks,
    latents,
    spatial_bias,
    norm_gain,
    norm_shift,
    temporal_bias,
    token_gain,
    spatial_w,
    temporal_w,
    project_w,
    output_w,
    plane,
    shifted,
    act,
    halo,
    normed,
    normed_all,
    outgoing,
    got,
    keys,
    values,
    probs,
    done,
    back,
    att,
    sent,
    got_near,
    got_far,
    load_sem,
    ready,
    lat_send,
    lat_recv,
    halo_send,
    halo_recv,
    gat_send,
    gat_recv,
    in_send,
    in_recv,
    out_send,
    out_recv,
    sum_send,
    sum_recv,
):
    me = lax.axis_index("rows")
    frame = lax.axis_index("frames")
    near, far = me ^ 1, me ^ 2
    has_prev, has_next = frame > 0, frame < frames - 1
    prev = jnp.maximum(frame - 1, 0)
    later = jnp.minimum(frame + 1, frames - 1)
    barrier = pltpu.get_barrier_semaphore()
    greet(barrier, "rows", far)

    @pl.when(has_next)
    def _():
        greet(barrier, "frames", later)

    @pl.when(has_prev)
    def _():
        greet(barrier, "frames", prev)

    greet(barrier, "rows", near)
    count, size, depth = chunks.shape
    loads, pieces = [], []
    for index in range(count):
        load = pltpu.make_async_copy(
            latents_hbm.at[:, index * depth : (index + 1) * depth],
            chunks.at[index],
            load_sem.at[index],
        )
        load.start()
        pieces.append(load)
    for index, (src, dst) in enumerate(
        (
            (bias_hbm, spatial_bias),
            (spatial_hbm, spatial_w),
            (gain_hbm, norm_gain),
            (shift_hbm, norm_shift),
            (temporal_hbm, temporal_w),
            (latents_hbm, latents),
            (temporal_bias_hbm, temporal_bias),
            (token_gain_hbm, token_gain),
            (key_hbm, project_w.at[0]),
            (query_hbm, project_w.at[1]),
            (value_hbm, project_w.at[2]),
            (output_hbm, output_w),
        )
    ):
        load = pltpu.make_async_copy(src, dst, load_sem.at[count + index])
        load.start()
        loads.append(load)
    for load in pieces:
        load.wait()
    pl.semaphore_wait(
        barrier, 2 + has_prev.astype(jnp.int32) + has_next.astype(jnp.int32)
    )

    across, onward = [], []
    for index in range(count):
        across.append(
            remote(
                chunks.at[index],
                plane.at[index, me],
                lat_send.at[0, index],
                lat_recv.at[0, index],
                "rows",
                far,
            )
        )
        onward.append(
            remote(
                plane.at[index, far],
                plane.at[index, far],
                lat_send.at[1, index],
                lat_recv.at[1, index],
                "rows",
                near,
            )
        )
        across[index].start()
    beside = remote(
        chunks, plane.at[:, me], lat_send.at[2, 0], lat_recv.at[2, 0], "rows", near
    )
    beside.start()
    for index in range(count):
        plane[index, me] = chunks[index]
    for load in loads[:2]:
        load.wait()
    beside.wait_recv()
    spatial = column(spatial_bias)
    for index in range(count):
        if index == 0:
            across[0].wait_recv()
            onward[0].start()
        if index + 1 < count:
            across[index + 1].wait_recv()
            onward[index + 1].start()
        onward[index].wait_recv()
        spatial = spatial + convolve_chunk(
            plane.at[index], shifted.at[index], spatial_w, index, width_cells
        )
    for load in loads[2:4]:
        load.wait()
    act[...] = group_norm_silu(spatial, column(norm_gain), column(norm_shift), groups)
    for copy in across + onward + [beside]:
        copy.wait_send()


    def rows_of(block):
        return pl.ds(pl.multiple_of(block * size, size), size)

    up, down = [], []
    for turn, block in enumerate((far ^ 1, far, near, me)):
        rows = rows_of(block)
        for side, (copies, peer) in enumerate(((up, later), (down, prev))):
            copies.append(
                remote(
                    act.at[rows],
                    halo.at[side, rows],
                    halo_send.at[side, turn],
                    halo_recv.at[side, turn],
                    "frames",
                    peer,
                )
            )

    @pl.when(has_next)
    def _():
        for copy in up:
            copy.start()

    @pl.when(has_prev)
    def _():
        for copy in down:
            copy.start()

    @pl.when(jnp.logical_not(has_prev))
    def _():
        halo[0] = jnp.zeros(halo.shape[1:], halo.dtype)

    @pl.when(jnp.logical_not(has_next))
    def _():
        halo[1] = jnp.zeros(halo.shape[1:], halo.dtype)

    loads[4].wait()

    def temporal_term(block, turn):
        rows = rows_of(block)
        total = jnp.dot(act[rows, :], temporal_w[1], preferred_element_type=F32)

        @pl.when(has_prev)
        def _():
            up[turn].wait_recv()

        @pl.when(has_next)
        def _():
            down[turn].wait_recv()

        total += jnp.dot(halo[0, rows, :], temporal_w[0], preferred_element_type=F32)
        total += jnp.dot(halo[1, rows, :], temporal_w[2], preferred_element_type=F32)
        return total

    temporal = reduce_rows(
        temporal_term, sent.at[0], got_near.at[0], got_far.at[0], sum_send.at[0], sum_recv.at[0]
    )

    @pl.when(jnp.logical_and(has_prev, frame == frames - 3))
    def _():
        pl.semaphore_signal(ready, inc=1, device_id={"frames": prev}, device_id_type=MESH)

    @pl.when(jnp.logical_and(has_next, frame == 2))
    def _():
        pl.semaphore_signal(ready, inc=1, device_id={"frames": later}, device_id_type=MESH)

    @pl.when(has_next)
    def _():
        for copy in up:
            copy.wait_send()

    @pl.when(has_prev)
    def _():
        for copy in down:
            copy.wait_send()

    for load in loads[5:8]:
        load.wait()
    hidden = (latents[...].astype(F32) + temporal + row(temporal_bias)).astype(BF16)
    flat = hidden.astype(F32)
    centred = flat - jnp.mean(flat, axis=-1, keepdims=True)
    var = jnp.mean(centred * centred, axis=-1, keepdims=True)
    normed[...] = (centred / jnp.sqrt(var + 1e-05) * row(token_gain)).astype(BF16)
    gather = Gather(normed, normed_all, gat_send, gat_recv)
    gather.start()
    normed_all[me] = normed[...]

    @pl.when(jnp.logical_not(jnp.logical_and(has_prev, has_next)))
    def _():
        pl.semaphore_wait(ready, 1)

    tokens = act.shape[0]
    width, half = got.shape[3], got.shape[4]
    here = me // 2
    moves = [[], [], []]

    def project(pair):
        slab = normed_all[pl.ds(2 * pair, 2)].reshape(half, -1)
        for kind in range(3):
            cols = jnp.dot(slab, project_w[kind], preferred_element_type=F32)
            cols = cols.T.astype(BF16)
            for owner in range(frames):
                outgoing[kind, pair, owner] = cols[owner * width : (owner + 1) * width, :]
            for turn in range(1, frames):
                peer = lax.rem(frame + turn, frames)
                copy = remote(
                    outgoing.at[kind, pair, peer],
                    got.at[kind, pair, frame],
                    in_send.at[kind, pair, turn],
                    in_recv.at[kind, pair, turn],
                    "frames",
                    peer,
                )
                copy.start()
                moves[kind].append(copy)
            got[kind, pair, frame] = outgoing[kind, pair, frame]

    for kind in range(3):
        loads[8 + kind].wait()
    gather.near_ready()
    project(here)
    gather.finish()
    project(1 - here)

    for copy in moves[0]:
        copy.wait_recv()
    for source in range(frames):
        for pair in range(2):
            begin = source * tokens + pair * half
            keys[begin : begin + half, :] = got[0, pair, source].astype(F32).T.astype(BF16)
    for copy in moves[1]:
        copy.wait_recv()
    scale = 1.0 / math.sqrt(HD)
    heads = width // HD
    sums = []
    for turn in range(1, frames + 1):
        peer = lax.rem(frame + turn, frames)
        for head in range(heads):
            cols = slice(head * HD, (head + 1) * HD)
            query = jnp.concatenate(
                [got[1, 0, peer, cols, :], got[1, 1, peer, cols, :]], axis=1
            )
            scores = jnp.dot(keys[:, cols], query, preferred_element_type=F32) * scale
            weights = jnp.exp(scores - jnp.max(scores, axis=0, keepdims=True))
            sums.append(jnp.sum(weights, axis=0, keepdims=True))
            probs[(turn - 1) * heads + head] = weights.astype(BF16)
    for copy in moves[2]:
        copy.wait_recv()
    for source in range(frames):
        for pair in range(2):
            begin = source * tokens + pair * half
            values[:, begin : begin + half] = got[2, pair, source]
    returns = [[], []]

    def give_back(step, pair, turn):
        peer = lax.rem(frame + turn, frames)
        copy = remote(
            done.at[pair, peer],
            back.at[pair, frame],
            out_send.at[pair, turn],
            out_recv.at[pair, turn],
            "frames",
            peer,
        )
        copy.start()
        returns[step].append(copy)

    for turn in range(1, frames + 1):
        peer = lax.rem(frame + turn, frames)
        for head in range(heads):
            cols = slice(head * HD, (head + 1) * HD)
            place = (turn - 1) * heads + head
            numerator = jnp.dot(values[cols, :], probs[place], preferred_element_type=F32)
            result = (numerator / sums[place]).astype(BF16)
            for pair in range(2):
                done[pair, peer, cols, :] = result[:, pair * half : (pair + 1) * half]
        if turn < frames:
            give_back(0, 1 - here, turn)
    for turn in range(1, frames):
        give_back(1, here, turn)
    for pair in range(2):
        back[pair, frame] = done[pair, frame]
    loads[11].wait()

    def collect(step, pair):
        for copy in returns[step]:
            copy.wait_recv()
        rows = pl.ds(pl.multiple_of(pair * half, half), half)
        for source in range(frames):
            att[rows, source * width : (source + 1) * width] = (
                back[pair, source].astype(F32).T.astype(BF16)
            )

    def mixed_term(block, turn):
        if turn == 0:
            collect(0, 1 - here)
        if turn == 2:
            collect(1, here)
        return jnp.dot(att[rows_of(block), :], output_w[...], preferred_element_type=F32)

    mixed = reduce_rows(
        mixed_term, sent.at[1], got_near.at[1], got_far.at[1], sum_send.at[1], sum_recv.at[1]
    )
    out_ref[...] = (hidden.astype(F32) + mixed).astype(BF16)
    for batch in moves + returns:
        for copy in batch:
            copy.wait_send()


def body_fast(
    latents,
    spatial_weight,
    spatial_bias,
    norm_gain,
    norm_shift,
    temporal_weight,
    temporal_bias,
    token_gain,
    query_weight,
    key_weight,
    value_weight,
    output_weight,
):
    channels = latents.shape[3]
    peers, frames = lax.axis_size("rows"), lax.axis_size("frames")
    block = latents.reshape(-1, channels)
    size = block.shape[0]
    tokens = size * peers
    width_cells = latents.shape[2]
    local_out = spatial_weight.shape[3]
    width = query_weight.shape[1] // frames
    heads = width // HD
    links = 2 * PARTS + 1
    depth = CHUNK
    count = channels // depth
    denoised = pl.pallas_call(
        functools.partial(block_kernel, frames, width_cells, NORM_GROUPS // peers),
        out_shape=jax.ShapeDtypeStruct(block.shape, BF16),
        in_specs=[ANY_SPEC] * 12,
        out_specs=VMEM_SPEC,
        scratch_shapes=[
            pltpu.VMEM((count, size, depth), BF16),
            pltpu.VMEM(block.shape, BF16),
            pltpu.VMEM(spatial_bias.shape, F32),
            pltpu.VMEM(norm_gain.shape, F32),
            pltpu.VMEM(norm_shift.shape, F32),
            pltpu.VMEM(temporal_bias.shape, F32),
            pltpu.VMEM(token_gain.shape, F32),
            pltpu.VMEM(spatial_weight.shape[:2] + (local_out, channels), BF16),
            pltpu.VMEM(temporal_weight.shape, BF16),
            pltpu.VMEM((3,) + query_weight.shape, BF16),
            pltpu.VMEM(output_weight.shape, BF16),
            pltpu.VMEM((count, peers, size, depth), BF16),
            pltpu.VMEM((count, 3, tokens + 2 * width_cells, depth), BF16),
            pltpu.VMEM((tokens, local_out), BF16),
            pltpu.VMEM((2, tokens, local_out), BF16),
            pltpu.VMEM(block.shape, BF16),
            pltpu.VMEM((peers,) + block.shape, BF16),
            pltpu.VMEM((3, 2, frames, width, tokens // 2), BF16),
            pltpu.VMEM((3, 2, frames, width, tokens // 2), BF16),
            pltpu.VMEM((frames * tokens, width), BF16),
            pltpu.VMEM((width, frames * tokens), BF16),
            pltpu.VMEM((frames * heads, frames * tokens, tokens), BF16),
            pltpu.VMEM((2, frames, width, tokens // 2), BF16),
            pltpu.VMEM((2, frames, width, tokens // 2), BF16),
            pltpu.VMEM((tokens, frames * width), BF16),
            pltpu.VMEM((2, 3) + block.shape, BF16),
            pltpu.VMEM((2, 2) + block.shape, BF16),
            pltpu.VMEM((2,) + block.shape, BF16),
            DMA((12 + count,)),
            pltpu.SemaphoreType.REGULAR,
            DMA((3, count)),
            DMA((3, count)),
            DMA((2, peers)),
            DMA((2, peers)),
            DMA((links,)),
            DMA((links,)),
            DMA((3, 2, frames)),
            DMA((3, 2, frames)),
            DMA((2, frames)),
            DMA((2, frames)),
            DMA((2, 3)),
            DMA((2, 3)),
        ],
        compiler_params=pltpu.CompilerParams(
            collective_id=0, has_side_effects=True, vmem_limit_bytes=VMEM_LIMIT
        ),
    )(
        block,
        jnp.swapaxes(spatial_weight, 2, 3),
        spatial_bias,
        norm_gain,
        norm_shift,
        temporal_weight,
        temporal_bias,
        token_gain,
        query_weight,
        key_weight,
        value_weight,
        output_weight,
    )
    return denoised.reshape(latents.shape)


def fits(mesh):
    def choose(*args):
        latents, query_weight = args[0], args[8]
        peers, frames = mesh.shape["rows"], mesh.shape["frames"]
        heads = query_weight.shape[1] // HD
        tokens = latents.shape[0] * latents.shape[1] * latents.shape[2] * peers
        fast = (
            peers == 4
            and mesh.shape["frames"] == 4
            and latents.shape[3] % CHUNK == 0
            and args[1].shape[3] % (8 * (NORM_GROUPS // peers)) == 0
            and latents.shape[1] == 1
            and heads % frames == 0
            and tokens % 256 == 0
            and latents.shape[2] % 16 == 0
            and latents.shape[0] * latents.shape[2] % (16 * PARTS) == 0
        )
        return (body_fast if fast else body)(*args)

    return choose


def solution(mesh):
    in_specs = (
        P("rows", ("groups", "frames"), None, None),
        P(None, None, None, "rows"),
        P("rows"),
        P("rows"),
        P("rows"),
        P(None, "rows", None),
        P(),
        P(),
        P(None, "rows"),
        P(None, "rows"),
        P(None, "rows"),
        P("rows", None),
    )
    out_specs = P("rows", ("groups", "frames"), None, None)
    return jax.shard_map(
        fits(mesh), mesh=mesh, in_specs=in_specs, out_specs=out_specs, check_vma=False
    )
```

```python
import functools
import math

import jax
import jax.numpy as jnp
from jax import lax
from jax.experimental import pallas as pl
from jax.experimental.pallas import tpu as pltpu
from jax.sharding import PartitionSpec as P

HD = 64
NORM_GROUPS = 32


def padded_2(array, sides, width):
    for axis, dim in sides:
        peers, length = (lax.axis_size(axis), array.shape[dim])
        up = [(i, (i + 1) % peers) for i in range(peers - 1)]
        down = [(j, i) for i, j in up]
        last = lax.slice_in_dim(array, length - width, length, axis=dim)
        leading = lax.slice_in_dim(array, 0, width, axis=dim)
        before = lax.ppermute(last, axis, up)
        after = lax.ppermute(leading, axis, down)
        array = jnp.concatenate([before, array, after], axis=dim)
    return array


def shifted_2(value, axis, steps):
    count = lax.axis_size(axis)
    pairs = [(source, (source + steps) % count) for source in range(count)]
    return lax.ppermute(value, axis, pairs)


def conv_plane(field, weight, bias):
    rows_n, frames_n, cols_n, chans = field.shape
    padded = jnp.pad(field, ((1, 1), (0, 0), (1, 1), (0, 0)))
    total = jnp.zeros((rows_n * frames_n * cols_n, weight.shape[3]), jnp.float32)
    for row_off in range(3):
        for col_off in range(3):
            window = padded[row_off : row_off + rows_n, :, col_off : col_off + cols_n, :].reshape(
                -1, chans
            )
            total = total + jnp.dot(
                window, weight[row_off, col_off], preferred_element_type=jnp.float32
            )
    return total.reshape(rows_n, frames_n, cols_n, -1) + bias


def layer_norm(field, token_gain):
    flat = field.astype(jnp.float32)
    token_mean = jnp.mean(flat, axis=-1, keepdims=True)
    shifted = flat - token_mean
    token_var = jnp.mean(shifted * shifted, axis=-1, keepdims=True)
    return (shifted / jnp.sqrt(token_var + 1e-05) * token_gain).astype(jnp.bfloat16)


def attend(queries, carried, keys, values):
    block = queries.shape[0]
    head_count = queries.shape[1]
    block_count = keys.shape[0] // block
    key_blocks = keys.reshape(block_count, block, head_count, HD)
    value_blocks = values.reshape(block_count, block, head_count, HD)
    scale = 1.0 / math.sqrt(HD)

    def visit_block(state, block_pair):
        running_max, denominator, numerator = state
        key_block, value_block = block_pair
        scores = (
            jnp.einsum("qhd,khd->qhk", queries, key_block, preferred_element_type=jnp.float32)
            * scale
        )
        new_max = jnp.maximum(running_max, jnp.max(scores, axis=-1))
        shrink = jnp.exp(running_max - new_max)
        weights = jnp.exp(scores - new_max[..., None])
        denominator = denominator * shrink + jnp.sum(weights, axis=-1)
        numerator = numerator * shrink[..., None] + jnp.einsum(
            "qhk,khd->qhd",
            weights.astype(jnp.bfloat16),
            value_block,
            preferred_element_type=jnp.float32,
        )
        return ((new_max, denominator, numerator), None)

    result, _ = lax.scan(visit_block, carried, (key_blocks, value_blocks))
    return result


def body(
    latents,
    spatial_weight,
    spatial_bias,
    norm_gain,
    norm_shift,
    temporal_weight,
    temporal_bias,
    token_gain,
    query_weight,
    key_weight,
    value_weight,
    output_weight,
):
    row_count, frame_count, width_cells, channels = latents.shape
    plane = lax.all_gather(latents, "rows", axis=0, tiled=True)
    plane_rows = plane.shape[0]
    local_out = spatial_weight.shape[3]
    spatial = conv_plane(plane, spatial_weight, spatial_bias)
    local_groups = NORM_GROUPS // lax.axis_size("rows")
    grouped = spatial.reshape(plane_rows, frame_count, width_cells, local_groups, -1)
    group_mean = jnp.mean(grouped, axis=(0, 2, 4), keepdims=True)
    centred = grouped - group_mean
    group_var = jnp.mean(centred * centred, axis=(0, 2, 4), keepdims=True)
    scaled = (centred / jnp.sqrt(group_var + 1e-05)).reshape(
        plane_rows, frame_count, width_cells, local_out
    ) * norm_gain + norm_shift
    activated = jax.nn.silu(scaled).astype(jnp.bfloat16)
    rim = padded_2(activated, (("frames", 1),), 1)
    row_total = row_count * lax.axis_size("rows")
    row_piece = rim
    total = jnp.zeros((row_total * frame_count * width_cells, channels), jnp.float32)
    for lag_index in range(3):
        window = row_piece[:, lag_index : lag_index + frame_count].reshape(-1, local_out)
        total = total + jnp.dot(
            window, temporal_weight[lag_index], preferred_element_type=jnp.float32
        )
    temporal = lax.psum_scatter(
        total.reshape(row_total, frame_count, width_cells, channels).astype(jnp.bfloat16),
        "rows",
        scatter_dimension=0,
        tiled=True,
    ).astype(jnp.float32)
    hidden = (latents.astype(jnp.float32) + temporal + temporal_bias).astype(jnp.bfloat16)
    normed_all = lax.all_gather(layer_norm(hidden, token_gain), "rows", axis=0, tiled=True)
    flat = normed_all.reshape(-1, channels)
    head_cols = query_weight.shape[1]
    head_count = head_cols // HD
    token_count = flat.shape[0]
    queries = jnp.dot(flat, query_weight, preferred_element_type=jnp.float32).astype(jnp.bfloat16)
    keys = jnp.dot(flat, key_weight, preferred_element_type=jnp.float32).astype(jnp.bfloat16)
    values = jnp.dot(flat, value_weight, preferred_element_type=jnp.float32).astype(jnp.bfloat16)
    start_state = (
        jnp.full((token_count, head_count), -1e30, jnp.float32),
        jnp.zeros((token_count, head_count), jnp.float32),
        jnp.zeros((token_count, head_count, HD), jnp.float32),
    )
    local_keys = keys.reshape(token_count, head_count, HD)
    local_values = values.reshape(token_count, head_count, HD)

    def travel(turn, state):
        query_moving, running_max, denominator, numerator = state
        running_max, denominator, numerator = attend(
            query_moving, (running_max, denominator, numerator), local_keys, local_values
        )
        return (
            shifted_2(query_moving, "frames", 1),
            shifted_2(running_max.astype(jnp.bfloat16), "frames", 1).astype(running_max.dtype),
            shifted_2(denominator.astype(jnp.bfloat16), "frames", 1).astype(denominator.dtype),
            shifted_2(numerator.astype(jnp.bfloat16), "frames", 1).astype(numerator.dtype),
        )

    start_moving = queries.reshape(token_count, head_count, HD)
    final = lax.fori_loop(0, lax.axis_size("frames"), travel, (start_moving,) + start_state)
    denominator, numerator = (final[2], final[3])
    attended = (
        (numerator / denominator[..., None])
        .astype(jnp.bfloat16)
        .reshape(plane_rows, frame_count, width_cells, head_cols)
    )
    row_piece = attended
    mixed = lax.psum_scatter(
        jnp.dot(row_piece.reshape(-1, head_cols), output_weight, preferred_element_type=jnp.float32)
        .reshape(row_count * lax.axis_size("rows"), frame_count, width_cells, channels)
        .astype(jnp.bfloat16),
        "rows",
        scatter_dimension=0,
        tiled=True,
    ).astype(jnp.float32)
    return (hidden.astype(jnp.float32) + mixed).astype(jnp.bfloat16)


MESH = pl.DeviceIdType.MESH
DMA = pltpu.SemaphoreType.DMA
VMEM_SPEC = pl.BlockSpec(memory_space=pltpu.VMEM)
ANY_SPEC = pl.BlockSpec(memory_space=pl.ANY)
BF16 = jnp.bfloat16
F32 = jnp.float32
VMEM_LIMIT = 54 << 20
PARTS = 2
CHUNK = 256


def remote(src, dst, send, recv, axis, peer):
    return pltpu.make_async_remote_copy(
        src_ref=src,
        dst_ref=dst,
        send_sem=send,
        recv_sem=recv,
        device_id={axis: peer},
        device_id_type=MESH,
    )


def greet(barrier, axis, peer):
    pl.semaphore_signal(barrier, inc=1, device_id={axis: peer}, device_id_type=MESH)


class Gather:
    def __init__(self, block, out, send, recv):
        me = lax.axis_index("rows")
        near, far = me ^ 1, me ^ 2
        step = block.shape[0] // PARTS
        self.far, self.onward = [], []
        for part in range(PARTS):
            piece = pl.ds(part * step, step)
            self.far.append(
                remote(
                    block.at[piece],
                    out.at[me, piece],
                    send.at[part],
                    recv.at[part],
                    "rows",
                    far,
                )
            )
            self.onward.append(
                remote(
                    out.at[far, piece],
                    out.at[far, piece],
                    send.at[PARTS + part],
                    recv.at[PARTS + part],
                    "rows",
                    near,
                )
            )
        self.near = remote(
            block, out.at[me], send.at[2 * PARTS], recv.at[2 * PARTS], "rows", near
        )

    def start(self):
        for copy in self.far:
            copy.start()
        self.near.start()

    def near_ready(self):
        self.near.wait_recv()

    def finish(self):
        for copy, onward in zip(self.far, self.onward):
            copy.wait_recv()
            onward.start()
        for copy in self.far:
            copy.wait_send()
        self.near.wait_send()
        for onward in self.onward:
            onward.wait()


def reduce_rows(term, sent, got_near, got_far, send, recv):
    me = lax.axis_index("rows")
    near, far = me ^ 1, me ^ 2

    def hand(slot, value):
        sent[slot] = value.astype(BF16)
        copy = remote(
            sent.at[slot], got_near.at[slot], send.at[slot], recv.at[slot], "rows", near
        )
        copy.start()
        return copy

    first = hand(0, term(far ^ 1, 0))
    mine = term(far, 1)
    first.wait_recv()
    sent[2] = (mine + got_near[0].astype(F32)).astype(BF16)
    across = remote(sent.at[2], got_far, send.at[2], recv.at[2], "rows", far)
    across.start()
    second = hand(1, term(near, 2))
    mine = term(me, 3)
    second.wait_recv()
    mine = mine + got_near[1].astype(F32)
    across.wait_recv()
    total = mine + got_far[...].astype(F32)
    for copy in (first, second, across):
        copy.wait_send()
    return total


def row(ref):
    return ref[...].reshape(1, -1)


def column(ref):
    value = jnp.broadcast_to(row(ref), (8, ref.shape[0]))
    return value.T[:, :1]


def convolve_chunk(plane, shifted, weight, chunk, width):
    blocks, size, depth = plane.shape
    tokens = blocks * size
    edge = jnp.zeros((width, depth), BF16)
    place = lax.broadcasted_iota(jnp.int32, (size, depth), 0) % width
    for offset in range(3):
        shifted[offset, :width, :] = edge
        shifted[offset, tokens + width :, :] = edge
    for block in range(blocks):
        rows = slice(width + block * size, width + (block + 1) * size)
        value = plane[block]
        wide = value.astype(F32)
        before = jnp.where(place == 0, 0.0, pltpu.roll(wide, 1, 0))
        after = jnp.where(place == width - 1, 0.0, pltpu.roll(wide, size - 1, 0))
        shifted[0, rows, :] = before.astype(BF16)
        shifted[1, rows, :] = value
        shifted[2, rows, :] = after.astype(BF16)
    total = None
    for row_off in range(3):
        for col_off in range(3):
            window = shifted[col_off, row_off * width : row_off * width + tokens, :]
            part = lax.dot_general(
                weight[row_off, col_off, :, chunk * depth : (chunk + 1) * depth],
                window,
                (((1,), (1,)), ((), ())),
                preferred_element_type=F32,
            )
            total = part if total is None else total + part
    return total


def group_norm_silu(spatial, gain, shift, groups):
    channels, tokens = spatial.shape

    def group_mean(value):
        return jnp.mean(value, axis=(1, 2), keepdims=True)

    grouped = spatial.reshape(groups, channels // groups, tokens)
    centred = grouped - group_mean(grouped)
    scale = 1.0 / jnp.sqrt(group_mean(centred * centred) + 1e-05)
    value = (centred * scale).reshape(channels, tokens) * gain + shift
    return (value / (1.0 + jnp.exp(-value))).T.astype(BF16)


def block_kernel(
    frames,
    width_cells,
    groups,
    latents_hbm,
    spatial_hbm,
    bias_hbm,
    gain_hbm,
    shift_hbm,
    temporal_hbm,
    temporal_bias_hbm,
    token_gain_hbm,
    query_hbm,
    key_hbm,
    value_hbm,
    output_hbm,
    out_ref,
    chunks,
    latents,
    spatial_bias,
    norm_gain,
    norm_shift,
    temporal_bias,
    token_gain,
    spatial_w,
    temporal_w,
    project_w,
    output_w,
    plane,
    shifted,
    act,
    halo,
    normed,
    normed_all,
    outgoing,
    got,
    keys,
    values,
    probs,
    done,
    back,
    att,
    sent,
    got_near,
    got_far,
    load_sem,
    ready,
    lat_send,
    lat_recv,
    halo_send,
    halo_recv,
    gat_send,
    gat_recv,
    in_send,
    in_recv,
    out_send,
    out_recv,
    sum_send,
    sum_recv,
    lend_send,
    lend_recv,
):
    me = lax.axis_index("rows")
    frame = lax.axis_index("frames")
    near, far = me ^ 1, me ^ 2
    has_prev, has_next = frame > 0, frame < frames - 1
    prev = jnp.maximum(frame - 1, 0)
    later = jnp.minimum(frame + 1, frames - 1)
    barrier = pltpu.get_barrier_semaphore()
    greet(barrier, "rows", far)

    @pl.when(has_next)
    def _():
        greet(barrier, "frames", later)

    @pl.when(has_prev)
    def _():
        greet(barrier, "frames", prev)

    greet(barrier, "rows", near)
    count, size, depth = chunks.shape
    loads, pieces = [], []
    for index in range(count):
        load = pltpu.make_async_copy(
            latents_hbm.at[:, index * depth : (index + 1) * depth],
            chunks.at[index],
            load_sem.at[index],
        )
        load.start()
        pieces.append(load)
    for index, (src, dst) in enumerate(
        (
            (bias_hbm, spatial_bias),
            (spatial_hbm, spatial_w),
            (gain_hbm, norm_gain),
            (shift_hbm, norm_shift),
            (temporal_hbm, temporal_w),
            (latents_hbm, latents),
            (temporal_bias_hbm, temporal_bias),
            (token_gain_hbm, token_gain),
            (key_hbm, project_w.at[0]),
            (query_hbm, project_w.at[1]),
            (value_hbm, project_w.at[2]),
            (output_hbm, output_w.at[me // 2]),
        )
    ):
        load = pltpu.make_async_copy(src, dst, load_sem.at[count + index])
        load.start()
        loads.append(load)
    for load in pieces:
        load.wait()
    pl.semaphore_wait(
        barrier, 2 + has_prev.astype(jnp.int32) + has_next.astype(jnp.int32)
    )

    across, onward = [], []
    for index in range(count):
        across.append(
            remote(
                chunks.at[index],
                plane.at[index, me],
                lat_send.at[0, index],
                lat_recv.at[0, index],
                "rows",
                far,
            )
        )
        onward.append(
            remote(
                plane.at[index, far],
                plane.at[index, far],
                lat_send.at[1, index],
                lat_recv.at[1, index],
                "rows",
                near,
            )
        )
        across[index].start()
    beside = remote(
        chunks, plane.at[:, me], lat_send.at[2, 0], lat_recv.at[2, 0], "rows", near
    )
    beside.start()
    for index in range(count):
        plane[index, me] = chunks[index]
    for load in loads[:2]:
        load.wait()
    beside.wait_recv()
    spatial = column(spatial_bias)
    for index in range(count):
        across[index].wait_recv()
        onward[index].start()
    here = me // 2
    depth_out = output_w.shape[1]
    early = depth_out * 7 // 16 // 16 * 16
    loads[11].wait()
    lent = []
    for index, rows in enumerate((pl.ds(0, early), pl.ds(early, depth_out - early))):
        lent.append(
            remote(
                output_w.at[here, rows],
                output_w.at[here, rows],
                lend_send.at[index],
                lend_recv.at[index],
                "rows",
                far,
            )
        )
    lent[0].start()
    for index in range(count):
        onward[index].wait_recv()
    for index in range(count):
        spatial = spatial + convolve_chunk(
            plane.at[index], shifted.at[index], spatial_w, index, width_cells
        )
    for load in loads[2:4]:
        load.wait()
    act[...] = group_norm_silu(spatial, column(norm_gain), column(norm_shift), groups)
    for copy in across + onward + [beside]:
        copy.wait_send()


    def rows_of(block):
        return pl.ds(pl.multiple_of(block * size, size), size)

    up, down = [], []
    for turn, block in enumerate((far ^ 1, far, near, me)):
        rows = rows_of(block)
        for side, (copies, peer) in enumerate(((up, later), (down, prev))):
            copies.append(
                remote(
                    act.at[rows],
                    halo.at[side, rows],
                    halo_send.at[side, turn],
                    halo_recv.at[side, turn],
                    "frames",
                    peer,
                )
            )

    @pl.when(has_next)
    def _():
        for copy in up:
            copy.start()

    @pl.when(has_prev)
    def _():
        for copy in down:
            copy.start()

    @pl.when(jnp.logical_not(has_prev))
    def _():
        halo[0] = jnp.zeros(halo.shape[1:], halo.dtype)

    @pl.when(jnp.logical_not(has_next))
    def _():
        halo[1] = jnp.zeros(halo.shape[1:], halo.dtype)

    loads[4].wait()

    def temporal_term(block, turn):
        rows = rows_of(block)
        total = jnp.dot(act[rows, :], temporal_w[1], preferred_element_type=F32)

        @pl.when(has_prev)
        def _():
            up[turn].wait_recv()

        @pl.when(has_next)
        def _():
            down[turn].wait_recv()

        total += jnp.dot(halo[0, rows, :], temporal_w[0], preferred_element_type=F32)
        total += jnp.dot(halo[1, rows, :], temporal_w[2], preferred_element_type=F32)
        return total

    temporal = reduce_rows(
        temporal_term, sent.at[0], got_near.at[0], got_far.at[0], sum_send.at[0], sum_recv.at[0]
    )

    @pl.when(jnp.logical_and(has_prev, frame == frames - 3))
    def _():
        pl.semaphore_signal(ready, inc=1, device_id={"frames": prev}, device_id_type=MESH)

    @pl.when(jnp.logical_and(has_next, frame == 2))
    def _():
        pl.semaphore_signal(ready, inc=1, device_id={"frames": later}, device_id_type=MESH)

    @pl.when(has_next)
    def _():
        for copy in up:
            copy.wait_send()

    @pl.when(has_prev)
    def _():
        for copy in down:
            copy.wait_send()

    for load in loads[5:8]:
        load.wait()
    hidden = (latents[...].astype(F32) + temporal + row(temporal_bias)).astype(BF16)
    flat = hidden.astype(F32)
    centred = flat - jnp.mean(flat, axis=-1, keepdims=True)
    var = jnp.mean(centred * centred, axis=-1, keepdims=True)
    normed[...] = (centred / jnp.sqrt(var + 1e-05) * row(token_gain)).astype(BF16)
    gather = Gather(normed, normed_all, gat_send, gat_recv)
    gather.start()
    normed_all[me] = normed[...]

    @pl.when(jnp.logical_not(jnp.logical_and(has_prev, has_next)))
    def _():
        pl.semaphore_wait(ready, 1)

    tokens = act.shape[0]
    width, half = got.shape[3], got.shape[4]
    moves = [[], [], []]

    def project(pair):
        slab = normed_all[pl.ds(2 * pair, 2)].reshape(half, -1)
        for kind in range(3):
            cols = jnp.dot(slab, project_w[kind], preferred_element_type=F32)
            cols = cols.T.astype(BF16)
            for owner in range(frames):
                outgoing[kind, pair, owner] = cols[owner * width : (owner + 1) * width, :]
            for turn in range(1, frames):
                peer = lax.rem(frame + turn, frames)
                copy = remote(
                    outgoing.at[kind, pair, peer],
                    got.at[kind, pair, frame],
                    in_send.at[kind, pair, turn],
                    in_recv.at[kind, pair, turn],
                    "frames",
                    peer,
                )
                copy.start()
                moves[kind].append(copy)
            got[kind, pair, frame] = outgoing[kind, pair, frame]

    for kind in range(3):
        loads[8 + kind].wait()
    gather.near_ready()
    project(here)
    gather.finish()
    lent[1].start()
    project(1 - here)

    for copy in moves[0]:
        copy.wait_recv()
    for source in range(frames):
        for pair in range(2):
            begin = source * tokens + pair * half
            keys[begin : begin + half, :] = got[0, pair, source].astype(F32).T.astype(BF16)
    for copy in moves[1]:
        copy.wait_recv()
    scale = 1.0 / math.sqrt(HD)
    heads = width // HD
    sums = []
    for turn in range(1, frames + 1):
        peer = lax.rem(frame + turn, frames)
        for head in range(heads):
            cols = slice(head * HD, (head + 1) * HD)
            query = jnp.concatenate(
                [got[1, 0, peer, cols, :], got[1, 1, peer, cols, :]], axis=1
            )
            scores = jnp.dot(keys[:, cols], query, preferred_element_type=F32) * scale
            weights = jnp.exp(scores - jnp.max(scores, axis=0, keepdims=True))
            sums.append(jnp.sum(weights, axis=0, keepdims=True))
            probs[(turn - 1) * heads + head] = weights.astype(BF16)
    for copy in moves[2]:
        copy.wait_recv()
    for source in range(frames):
        for pair in range(2):
            begin = source * tokens + pair * half
            values[:, begin : begin + half] = got[2, pair, source]
    returns = []

    def give_back(turn):
        peer = lax.rem(frame + turn, frames)
        for side, (pair, target) in enumerate(((1 - here, far), (here, me))):
            if side == 1 and turn == frames:
                continue
            copy = pltpu.make_async_remote_copy(
                src_ref=done.at[pair, peer],
                dst_ref=back.at[here, frame],
                send_sem=out_send.at[side, turn],
                recv_sem=out_recv.at[side, turn],
                device_id={"rows": target, "frames": peer},
                device_id_type=MESH,
            )
            copy.start()
            returns.append(copy)

    for turn in range(1, frames + 1):
        peer = lax.rem(frame + turn, frames)
        for head in range(heads):
            cols = slice(head * HD, (head + 1) * HD)
            place = (turn - 1) * heads + head
            numerator = jnp.dot(values[cols, :], probs[place], preferred_element_type=F32)
            result = (numerator / sums[place]).astype(BF16)
            for pair in range(2):
                done[pair, peer, cols, :] = result[:, pair * half : (pair + 1) * half]
        give_back(turn)
    back[here, frame] = done[here, frame]
    for copy in lent:
        copy.wait_recv()
    for copy in returns:
        copy.wait_recv()
    att[...] = back[...].reshape(-1, half).astype(F32).T.astype(BF16)
    mix = output_w[...].reshape(-1, output_w.shape[2])
    core = lax.rem(me, 2)

    def mixed_term(owner):
        rows = pl.ds(pl.multiple_of(owner * size, size), size)
        return jnp.dot(att[rows, :], mix, preferred_element_type=F32)

    sent[1, 0] = mixed_term(1 - core).astype(BF16)
    share = remote(
        sent.at[1, 0], got_near.at[1, 0], sum_send.at[1, 0], sum_recv.at[1, 0], "rows", near
    )
    share.start()
    mixed = mixed_term(core)
    share.wait_recv()
    out_ref[...] = (hidden.astype(F32) + mixed + got_near[1, 0].astype(F32)).astype(BF16)
    share.wait_send()
    for copy in lent + returns:
        copy.wait_send()
    for batch in moves:
        for copy in batch:
            copy.wait_send()


def body_fast(
    latents,
    spatial_weight,
    spatial_bias,
    norm_gain,
    norm_shift,
    temporal_weight,
    temporal_bias,
    token_gain,
    query_weight,
    key_weight,
    value_weight,
    output_weight,
):
    channels = latents.shape[3]
    peers, frames = lax.axis_size("rows"), lax.axis_size("frames")
    block = latents.reshape(-1, channels)
    size = block.shape[0]
    tokens = size * peers
    width_cells = latents.shape[2]
    local_out = spatial_weight.shape[3]
    width = query_weight.shape[1] // frames
    heads = width // HD
    links = 2 * PARTS + 1
    depth = CHUNK
    count = channels // depth
    denoised = pl.pallas_call(
        functools.partial(block_kernel, frames, width_cells, NORM_GROUPS // peers),
        out_shape=jax.ShapeDtypeStruct(block.shape, BF16),
        in_specs=[ANY_SPEC] * 12,
        out_specs=VMEM_SPEC,
        scratch_shapes=[
            pltpu.VMEM((count, size, depth), BF16),
            pltpu.VMEM(block.shape, BF16),
            pltpu.VMEM(spatial_bias.shape, F32),
            pltpu.VMEM(norm_gain.shape, F32),
            pltpu.VMEM(norm_shift.shape, F32),
            pltpu.VMEM(temporal_bias.shape, F32),
            pltpu.VMEM(token_gain.shape, F32),
            pltpu.VMEM(spatial_weight.shape[:2] + (local_out, channels), BF16),
            pltpu.VMEM(temporal_weight.shape, BF16),
            pltpu.VMEM((3,) + query_weight.shape, BF16),
            pltpu.VMEM((2,) + output_weight.shape, BF16),
            pltpu.VMEM((count, peers, size, depth), BF16),
            pltpu.VMEM((count, 3, tokens + 2 * width_cells, depth), BF16),
            pltpu.VMEM((tokens, local_out), BF16),
            pltpu.VMEM((2, tokens, local_out), BF16),
            pltpu.VMEM(block.shape, BF16),
            pltpu.VMEM((peers,) + block.shape, BF16),
            pltpu.VMEM((3, 2, frames, width, tokens // 2), BF16),
            pltpu.VMEM((3, 2, frames, width, tokens // 2), BF16),
            pltpu.VMEM((frames * tokens, width), BF16),
            pltpu.VMEM((width, frames * tokens), BF16),
            pltpu.VMEM((frames * heads, frames * tokens, tokens), BF16),
            pltpu.VMEM((2, frames, width, tokens // 2), BF16),
            pltpu.VMEM((2, frames, width, tokens // 2), BF16),
            pltpu.VMEM((tokens // 2, 2 * frames * width), BF16),
            pltpu.VMEM((2, 3) + block.shape, BF16),
            pltpu.VMEM((2, 2) + block.shape, BF16),
            pltpu.VMEM((2,) + block.shape, BF16),
            DMA((12 + count,)),
            pltpu.SemaphoreType.REGULAR,
            DMA((3, count)),
            DMA((3, count)),
            DMA((2, peers)),
            DMA((2, peers)),
            DMA((links,)),
            DMA((links,)),
            DMA((3, 2, frames)),
            DMA((3, 2, frames)),
            DMA((2, frames + 1)),
            DMA((2, frames + 1)),
            DMA((2, 3)),
            DMA((2, 3)),
            DMA((2,)),
            DMA((2,)),
        ],
        compiler_params=pltpu.CompilerParams(
            collective_id=0, has_side_effects=True, vmem_limit_bytes=VMEM_LIMIT
        ),
    )(
        block,
        jnp.swapaxes(spatial_weight, 2, 3),
        spatial_bias,
        norm_gain,
        norm_shift,
        temporal_weight,
        temporal_bias,
        token_gain,
        query_weight,
        key_weight,
        value_weight,
        output_weight,
    )
    return denoised.reshape(latents.shape)


def fits(mesh):
    def choose(*args):
        latents, query_weight = args[0], args[8]
        peers, frames = mesh.shape["rows"], mesh.shape["frames"]
        heads = query_weight.shape[1] // HD
        tokens = latents.shape[0] * latents.shape[1] * latents.shape[2] * peers
        fast = (
            peers == 4
            and mesh.shape["frames"] == 4
            and latents.shape[3] % CHUNK == 0
            and args[1].shape[3] % (8 * (NORM_GROUPS // peers)) == 0
            and latents.shape[1] == 1
            and heads % frames == 0
            and tokens % 256 == 0
            and latents.shape[2] % 16 == 0
            and latents.shape[0] * latents.shape[2] % (16 * PARTS) == 0
        )
        return (body_fast if fast else body)(*args)

    return choose


def solution(mesh):
    in_specs = (
        P("rows", ("groups", "frames"), None, None),
        P(None, None, None, "rows"),
        P("rows"),
        P("rows"),
        P("rows"),
        P(None, "rows", None),
        P(),
        P(),
        P(None, "rows"),
        P(None, "rows"),
        P(None, "rows"),
        P("rows", None),
    )
    out_specs = P("rows", ("groups", "frames"), None, None)
    return jax.shard_map(
        fits(mesh), mesh=mesh, in_specs=in_specs, out_specs=out_specs, check_vma=False
    )
```

```python
import functools
import math

import jax
import jax.numpy as jnp
from jax import lax
from jax.experimental import pallas as pl
from jax.experimental.pallas import tpu as pltpu
from jax.sharding import PartitionSpec as P

HD = 64
NORM_GROUPS = 32


def padded_2(array, sides, width):
    for axis, dim in sides:
        peers, length = (lax.axis_size(axis), array.shape[dim])
        up = [(i, (i + 1) % peers) for i in range(peers - 1)]
        down = [(j, i) for i, j in up]
        last = lax.slice_in_dim(array, length - width, length, axis=dim)
        leading = lax.slice_in_dim(array, 0, width, axis=dim)
        before = lax.ppermute(last, axis, up)
        after = lax.ppermute(leading, axis, down)
        array = jnp.concatenate([before, array, after], axis=dim)
    return array


def shifted_2(value, axis, steps):
    count = lax.axis_size(axis)
    pairs = [(source, (source + steps) % count) for source in range(count)]
    return lax.ppermute(value, axis, pairs)


def conv_plane(field, weight, bias):
    rows_n, frames_n, cols_n, chans = field.shape
    padded = jnp.pad(field, ((1, 1), (0, 0), (1, 1), (0, 0)))
    total = jnp.zeros((rows_n * frames_n * cols_n, weight.shape[3]), jnp.float32)
    for row_off in range(3):
        for col_off in range(3):
            window = padded[row_off : row_off + rows_n, :, col_off : col_off + cols_n, :].reshape(
                -1, chans
            )
            total = total + jnp.dot(
                window, weight[row_off, col_off], preferred_element_type=jnp.float32
            )
    return total.reshape(rows_n, frames_n, cols_n, -1) + bias


def layer_norm(field, token_gain):
    flat = field.astype(jnp.float32)
    token_mean = jnp.mean(flat, axis=-1, keepdims=True)
    shifted = flat - token_mean
    token_var = jnp.mean(shifted * shifted, axis=-1, keepdims=True)
    return (shifted / jnp.sqrt(token_var + 1e-05) * token_gain).astype(jnp.bfloat16)


def attend(queries, carried, keys, values):
    block = queries.shape[0]
    head_count = queries.shape[1]
    block_count = keys.shape[0] // block
    key_blocks = keys.reshape(block_count, block, head_count, HD)
    value_blocks = values.reshape(block_count, block, head_count, HD)
    scale = 1.0 / math.sqrt(HD)

    def visit_block(state, block_pair):
        running_max, denominator, numerator = state
        key_block, value_block = block_pair
        scores = (
            jnp.einsum("qhd,khd->qhk", queries, key_block, preferred_element_type=jnp.float32)
            * scale
        )
        new_max = jnp.maximum(running_max, jnp.max(scores, axis=-1))
        shrink = jnp.exp(running_max - new_max)
        weights = jnp.exp(scores - new_max[..., None])
        denominator = denominator * shrink + jnp.sum(weights, axis=-1)
        numerator = numerator * shrink[..., None] + jnp.einsum(
            "qhk,khd->qhd",
            weights.astype(jnp.bfloat16),
            value_block,
            preferred_element_type=jnp.float32,
        )
        return ((new_max, denominator, numerator), None)

    result, _ = lax.scan(visit_block, carried, (key_blocks, value_blocks))
    return result


def body(
    latents,
    spatial_weight,
    spatial_bias,
    norm_gain,
    norm_shift,
    temporal_weight,
    temporal_bias,
    token_gain,
    query_weight,
    key_weight,
    value_weight,
    output_weight,
):
    row_count, frame_count, width_cells, channels = latents.shape
    plane = lax.all_gather(latents, "rows", axis=0, tiled=True)
    plane_rows = plane.shape[0]
    local_out = spatial_weight.shape[3]
    spatial = conv_plane(plane, spatial_weight, spatial_bias)
    local_groups = NORM_GROUPS // lax.axis_size("rows")
    grouped = spatial.reshape(plane_rows, frame_count, width_cells, local_groups, -1)
    group_mean = jnp.mean(grouped, axis=(0, 2, 4), keepdims=True)
    centred = grouped - group_mean
    group_var = jnp.mean(centred * centred, axis=(0, 2, 4), keepdims=True)
    scaled = (centred / jnp.sqrt(group_var + 1e-05)).reshape(
        plane_rows, frame_count, width_cells, local_out
    ) * norm_gain + norm_shift
    activated = jax.nn.silu(scaled).astype(jnp.bfloat16)
    rim = padded_2(activated, (("frames", 1),), 1)
    row_total = row_count * lax.axis_size("rows")
    row_piece = rim
    total = jnp.zeros((row_total * frame_count * width_cells, channels), jnp.float32)
    for lag_index in range(3):
        window = row_piece[:, lag_index : lag_index + frame_count].reshape(-1, local_out)
        total = total + jnp.dot(
            window, temporal_weight[lag_index], preferred_element_type=jnp.float32
        )
    temporal = lax.psum_scatter(
        total.reshape(row_total, frame_count, width_cells, channels).astype(jnp.bfloat16),
        "rows",
        scatter_dimension=0,
        tiled=True,
    ).astype(jnp.float32)
    hidden = (latents.astype(jnp.float32) + temporal + temporal_bias).astype(jnp.bfloat16)
    normed_all = lax.all_gather(layer_norm(hidden, token_gain), "rows", axis=0, tiled=True)
    flat = normed_all.reshape(-1, channels)
    head_cols = query_weight.shape[1]
    head_count = head_cols // HD
    token_count = flat.shape[0]
    queries = jnp.dot(flat, query_weight, preferred_element_type=jnp.float32).astype(jnp.bfloat16)
    keys = jnp.dot(flat, key_weight, preferred_element_type=jnp.float32).astype(jnp.bfloat16)
    values = jnp.dot(flat, value_weight, preferred_element_type=jnp.float32).astype(jnp.bfloat16)
    start_state = (
        jnp.full((token_count, head_count), -1e30, jnp.float32),
        jnp.zeros((token_count, head_count), jnp.float32),
        jnp.zeros((token_count, head_count, HD), jnp.float32),
    )
    local_keys = keys.reshape(token_count, head_count, HD)
    local_values = values.reshape(token_count, head_count, HD)

    def travel(turn, state):
        query_moving, running_max, denominator, numerator = state
        running_max, denominator, numerator = attend(
            query_moving, (running_max, denominator, numerator), local_keys, local_values
        )
        return (
            shifted_2(query_moving, "frames", 1),
            shifted_2(running_max.astype(jnp.bfloat16), "frames", 1).astype(running_max.dtype),
            shifted_2(denominator.astype(jnp.bfloat16), "frames", 1).astype(denominator.dtype),
            shifted_2(numerator.astype(jnp.bfloat16), "frames", 1).astype(numerator.dtype),
        )

    start_moving = queries.reshape(token_count, head_count, HD)
    final = lax.fori_loop(0, lax.axis_size("frames"), travel, (start_moving,) + start_state)
    denominator, numerator = (final[2], final[3])
    attended = (
        (numerator / denominator[..., None])
        .astype(jnp.bfloat16)
        .reshape(plane_rows, frame_count, width_cells, head_cols)
    )
    row_piece = attended
    mixed = lax.psum_scatter(
        jnp.dot(row_piece.reshape(-1, head_cols), output_weight, preferred_element_type=jnp.float32)
        .reshape(row_count * lax.axis_size("rows"), frame_count, width_cells, channels)
        .astype(jnp.bfloat16),
        "rows",
        scatter_dimension=0,
        tiled=True,
    ).astype(jnp.float32)
    return (hidden.astype(jnp.float32) + mixed).astype(jnp.bfloat16)


MESH = pl.DeviceIdType.MESH
DMA = pltpu.SemaphoreType.DMA
VMEM_SPEC = pl.BlockSpec(memory_space=pltpu.VMEM)
ANY_SPEC = pl.BlockSpec(memory_space=pl.ANY)
BF16 = jnp.bfloat16
F32 = jnp.float32
VMEM_LIMIT = 54 << 20
PARTS = 2
CHUNK = 256
LANES = 128


def remote(src, dst, send, recv, axis, peer):
    return pltpu.make_async_remote_copy(
        src_ref=src,
        dst_ref=dst,
        send_sem=send,
        recv_sem=recv,
        device_id={axis: peer},
        device_id_type=MESH,
    )


def greet(barrier, axis, peer):
    pl.semaphore_signal(barrier, inc=1, device_id={axis: peer}, device_id_type=MESH)


class Gather:
    def __init__(self, block, out, send, recv):
        me = lax.axis_index("rows")
        near, far = me ^ 1, me ^ 2
        step = block.shape[0] // PARTS
        self.far, self.onward = [], []
        for part in range(PARTS):
            piece = pl.ds(part * step, step)
            self.far.append(
                remote(
                    block.at[piece],
                    out.at[me, piece],
                    send.at[part],
                    recv.at[part],
                    "rows",
                    far,
                )
            )
            self.onward.append(
                remote(
                    out.at[far, piece],
                    out.at[far, piece],
                    send.at[PARTS + part],
                    recv.at[PARTS + part],
                    "rows",
                    near,
                )
            )
        self.near = remote(
            block, out.at[me], send.at[2 * PARTS], recv.at[2 * PARTS], "rows", near
        )

    def start(self):
        for copy in self.far:
            copy.start()
        self.near.start()

    def near_ready(self):
        self.near.wait_recv()

    def finish(self):
        for copy, onward in zip(self.far, self.onward):
            copy.wait_recv()
            onward.start()
        for copy in self.far:
            copy.wait_send()
        self.near.wait_send()
        for onward in self.onward:
            onward.wait()


def reduce_pairs(term, terms, sent, got_near, got_far, send, recv):
    me = lax.axis_index("rows")
    near, far = me ^ 1, me ^ 2
    here, core = me // 2, lax.rem(me, 2)
    size = got_far.shape[0]

    def part(slot, owner):
        return terms[slot, pl.ds(pl.multiple_of(owner * size, size), size), :]

    def hand(slot, pair):
        terms[slot] = term(pair, slot)
        sent[slot] = part(slot, 1 - core).astype(BF16)
        copy = remote(
            sent.at[slot], got_near.at[slot], send.at[slot], recv.at[slot], "rows", near
        )
        copy.start()
        return copy

    first = hand(0, 1 - here)
    first.wait_recv()
    sent[2] = (part(0, core) + got_near[0].astype(F32)).astype(BF16)
    across = remote(sent.at[2], got_far, send.at[2], recv.at[2], "rows", far)
    across.start()
    second = hand(1, here)
    second.wait_recv()
    mine = part(1, core) + got_near[1].astype(F32)
    across.wait_recv()
    total = mine + got_far[...].astype(F32)
    for copy in (first, second, across):
        copy.wait_send()
    return total


def row(ref):
    return ref[...].reshape(1, -1)


def column(ref):
    value = jnp.broadcast_to(row(ref), (8, ref.shape[0]))
    return value.T[:, :1]


def convolve_chunk(plane, shifted, weight, chunk, width):
    blocks, size, depth = plane.shape
    tokens = blocks * size
    edge = jnp.zeros((width, depth), BF16)
    place = lax.broadcasted_iota(jnp.int32, (size, depth), 0) % width
    for offset in range(3):
        shifted[offset, :width, :] = edge
        shifted[offset, tokens + width :, :] = edge
    for block in range(blocks):
        rows = slice(width + block * size, width + (block + 1) * size)
        value = plane[block]
        wide = value.astype(F32)
        before = jnp.where(place == 0, 0.0, pltpu.roll(wide, 1, 0))
        after = jnp.where(place == width - 1, 0.0, pltpu.roll(wide, size - 1, 0))
        shifted[0, rows, :] = before.astype(BF16)
        shifted[1, rows, :] = value
        shifted[2, rows, :] = after.astype(BF16)
    total = None
    for row_off in range(3):
        for col_off in range(3):
            window = shifted[col_off, row_off * width : row_off * width + tokens, :]
            part = lax.dot_general(
                weight[row_off, col_off, :, chunk * depth : (chunk + 1) * depth],
                window,
                (((1,), (1,)), ((), ())),
                preferred_element_type=F32,
            )
            total = part if total is None else total + part
    return total


def group_norm_silu(spatial, gain, shift, groups):
    channels, tokens = spatial.shape

    def group_mean(value):
        return jnp.mean(value, axis=(1, 2), keepdims=True)

    grouped = spatial.reshape(groups, channels // groups, tokens)
    centred = grouped - group_mean(grouped)
    scale = 1.0 / jnp.sqrt(group_mean(centred * centred) + 1e-05)
    value = (centred * scale).reshape(channels, tokens) * gain + shift
    return value / (1.0 + jnp.exp(-value))


def block_kernel(
    frames,
    width_cells,
    groups,
    latents_hbm,
    spatial_hbm,
    bias_hbm,
    gain_hbm,
    shift_hbm,
    temporal_hbm,
    temporal_bias_hbm,
    token_gain_hbm,
    query_hbm,
    key_hbm,
    value_hbm,
    output_hbm,
    out_ref,
    chunks,
    latents,
    spatial_bias,
    norm_gain,
    norm_shift,
    temporal_bias,
    token_gain,
    spatial_w,
    temporal_w,
    project_w,
    output_w,
    plane,
    shifted,
    act,
    act_rest,
    halo,
    halo_rest,
    terms,
    normed,
    normed_all,
    outgoing,
    got,
    keys,
    values,
    probs,
    done,
    back,
    att,
    sent,
    got_near,
    got_far,
    load_sem,
    tap_sem,
    ready,
    lat_send,
    lat_recv,
    halo_send,
    halo_recv,
    gat_send,
    gat_recv,
    in_send,
    in_recv,
    out_send,
    out_recv,
    sum_send,
    sum_recv,
    lend_send,
    lend_recv,
):
    me = lax.axis_index("rows")
    frame = lax.axis_index("frames")
    near, far = me ^ 1, me ^ 2
    has_prev, has_next = frame > 0, frame < frames - 1
    prev = jnp.maximum(frame - 1, 0)
    later = jnp.minimum(frame + 1, frames - 1)
    barrier = pltpu.get_barrier_semaphore()
    greet(barrier, "rows", far)

    @pl.when(has_next)
    def _():
        greet(barrier, "frames", later)

    @pl.when(has_prev)
    def _():
        greet(barrier, "frames", prev)

    greet(barrier, "rows", near)
    count, size, depth = chunks.shape
    main, rest = act.shape[1], act_rest.shape[1]
    loads, pieces = [], []
    for index in range(count):
        load = pltpu.make_async_copy(
            latents_hbm.at[:, index * depth : (index + 1) * depth],
            chunks.at[index],
            load_sem.at[index],
        )
        load.start()
        pieces.append(load)
    for index, (src, dst) in enumerate(
        (
            (bias_hbm, spatial_bias),
            (spatial_hbm, spatial_w),
            (gain_hbm, norm_gain),
            (shift_hbm, norm_shift),
            (latents_hbm, latents),
            (temporal_bias_hbm, temporal_bias),
            (token_gain_hbm, token_gain),
            (key_hbm, project_w.at[0]),
            (query_hbm, project_w.at[1]),
            (value_hbm, project_w.at[2]),
            (output_hbm, output_w.at[me // 2]),
        )
    ):
        load = pltpu.make_async_copy(src, dst, load_sem.at[count + index])
        load.start()
        loads.append(load)
        if index == 3:
            taps = []
            for tap in range(3):
                for start, stop, place in (
                    (0, main, tap * main),
                    (main, main + rest, 3 * main + tap * rest),
                ):
                    load = pltpu.make_async_copy(
                        temporal_hbm.at[tap, start:stop],
                        temporal_w.at[place : place + stop - start],
                        tap_sem.at[len(taps)],
                    )
                    load.start()
                    taps.append(load)
    for load in pieces:
        load.wait()
    pl.semaphore_wait(
        barrier, 2 + has_prev.astype(jnp.int32) + has_next.astype(jnp.int32)
    )

    across, onward = [], []
    for index in range(count):
        across.append(
            remote(
                chunks.at[index],
                plane.at[index, me],
                lat_send.at[0, index],
                lat_recv.at[0, index],
                "rows",
                far,
            )
        )
        onward.append(
            remote(
                plane.at[index, far],
                plane.at[index, far],
                lat_send.at[1, index],
                lat_recv.at[1, index],
                "rows",
                near,
            )
        )
        across[index].start()
    beside = remote(
        chunks, plane.at[:, me], lat_send.at[2, 0], lat_recv.at[2, 0], "rows", near
    )
    beside.start()
    for index in range(count):
        plane[index, me] = chunks[index]
    for load in loads[:2]:
        load.wait()
    beside.wait_recv()
    spatial = column(spatial_bias)
    for index in range(count):
        across[index].wait_recv()
        onward[index].start()
    here = me // 2
    depth_out = output_w.shape[1]
    early = depth_out * 7 // 16 // 16 * 16
    loads[10].wait()
    lent = []
    for index, rows in enumerate((pl.ds(0, early), pl.ds(early, depth_out - early))):
        lent.append(
            remote(
                output_w.at[here, rows],
                output_w.at[here, rows],
                lend_send.at[index],
                lend_recv.at[index],
                "rows",
                far,
            )
        )
    lent[0].start()
    for index in range(count):
        onward[index].wait_recv()
    for index in range(count):
        spatial = spatial + convolve_chunk(
            plane.at[index], shifted.at[index], spatial_w, index, width_cells
        )
    for load in loads[2:4]:
        load.wait()
    value = group_norm_silu(spatial, column(norm_gain), column(norm_shift), groups)
    half = act_rest.shape[2]
    act[...] = value[:main].T.astype(BF16)
    for pair in range(2):
        act_rest[pair] = value[main:, pair * half : (pair + 1) * half].astype(BF16)
    for copy in across + onward + [beside]:
        copy.wait_send()


    up, down = [], []
    for turn, pair in enumerate((1 - here, here)):
        rows = pl.ds(pl.multiple_of(pair * half, half), half)
        for side, (copies, peer) in enumerate(((up, later), (down, prev))):
            for index, (src, dst) in enumerate(
                ((act.at[rows], halo.at[side, rows]), (act_rest.at[pair], halo_rest.at[side, pair]))
            ):
                copies.append(
                    remote(
                        src,
                        dst,
                        halo_send.at[side, 2 * turn + index],
                        halo_recv.at[side, 2 * turn + index],
                        "frames",
                        peer,
                    )
                )

    for turn in range(2):
        for exists, copies in ((has_next, up), (has_prev, down)):

            @pl.when(exists)
            def _(part=copies[2 * turn : 2 * turn + 2]):
                for copy in part:
                    copy.start()

    @pl.when(jnp.logical_not(has_prev))
    def _():
        halo[0] = jnp.zeros(halo.shape[1:], halo.dtype)
        halo_rest[0] = jnp.zeros(halo_rest.shape[1:], halo.dtype)

    @pl.when(jnp.logical_not(has_next))
    def _():
        halo[1] = jnp.zeros(halo.shape[1:], halo.dtype)
        halo_rest[1] = jnp.zeros(halo_rest.shape[1:], halo.dtype)

    for load in taps:
        load.wait()

    def temporal_term(pair, turn):
        rows = pl.ds(pl.multiple_of(pair * half, half), half)

        @pl.when(has_prev)
        def _():
            for copy in up[2 * turn : 2 * turn + 2]:
                copy.wait_recv()

        @pl.when(has_next)
        def _():
            for copy in down[2 * turn : 2 * turn + 2]:
                copy.wait_recv()

        left = jnp.concatenate([halo_rest[0, pair], act_rest[pair], halo_rest[1, pair]], axis=0)
        window = jnp.concatenate(
            [halo[0, rows, :], act[rows, :], halo[1, rows, :], left.astype(F32).T.astype(BF16)],
            axis=1,
        )
        return jnp.dot(window, temporal_w[...], preferred_element_type=F32)

    temporal = reduce_pairs(
        temporal_term,
        terms,
        sent.at[0],
        got_near.at[0],
        got_far.at[0],
        sum_send.at[0],
        sum_recv.at[0],
    )

    @pl.when(jnp.logical_and(has_prev, frame == frames - 3))
    def _():
        pl.semaphore_signal(ready, inc=1, device_id={"frames": prev}, device_id_type=MESH)

    @pl.when(jnp.logical_and(has_next, frame == 2))
    def _():
        pl.semaphore_signal(ready, inc=1, device_id={"frames": later}, device_id_type=MESH)

    @pl.when(has_next)
    def _():
        for copy in up:
            copy.wait_send()

    @pl.when(has_prev)
    def _():
        for copy in down:
            copy.wait_send()

    for load in loads[4:7]:
        load.wait()
    hidden = (latents[...].astype(F32) + temporal + row(temporal_bias)).astype(BF16)
    flat = hidden.astype(F32)
    centred = flat - jnp.mean(flat, axis=-1, keepdims=True)
    var = jnp.mean(centred * centred, axis=-1, keepdims=True)
    normed[...] = (centred / jnp.sqrt(var + 1e-05) * row(token_gain)).astype(BF16)
    gather = Gather(normed, normed_all, gat_send, gat_recv)
    gather.start()
    normed_all[me] = normed[...]

    @pl.when(jnp.logical_not(jnp.logical_and(has_prev, has_next)))
    def _():
        pl.semaphore_wait(ready, 1)

    tokens = act.shape[0]
    width = got.shape[3]
    moves = [[], [], []]

    def project(pair):
        slab = normed_all[pl.ds(2 * pair, 2)].reshape(half, -1)
        for kind in range(3):
            cols = jnp.dot(slab, project_w[kind], preferred_element_type=F32)
            cols = cols.T.astype(BF16)
            for owner in range(frames):
                outgoing[kind, pair, owner] = cols[owner * width : (owner + 1) * width, :]
            for turn in range(1, frames):
                peer = lax.rem(frame + turn, frames)
                copy = remote(
                    outgoing.at[kind, pair, peer],
                    got.at[kind, pair, frame],
                    in_send.at[kind, pair, turn],
                    in_recv.at[kind, pair, turn],
                    "frames",
                    peer,
                )
                copy.start()
                moves[kind].append(copy)
            got[kind, pair, frame] = outgoing[kind, pair, frame]

    for kind in range(3):
        loads[7 + kind].wait()
    gather.near_ready()
    project(here)
    gather.finish()
    project(1 - here)

    lent[1].start()
    for copy in moves[0]:
        copy.wait_recv()
    for source in range(frames):
        for pair in range(2):
            begin = source * tokens + pair * half
            keys[begin : begin + half, :] = got[0, pair, source].astype(F32).T.astype(BF16)
    for copy in moves[1]:
        copy.wait_recv()
    scale = 1.0 / math.sqrt(HD)
    heads = width // HD
    sums = []
    for turn in range(1, frames + 1):
        peer = lax.rem(frame + turn, frames)
        for head in range(heads):
            cols = slice(head * HD, (head + 1) * HD)
            query = jnp.concatenate(
                [got[1, 0, peer, cols, :], got[1, 1, peer, cols, :]], axis=1
            )
            scores = jnp.dot(keys[:, cols], query, preferred_element_type=F32) * scale
            weights = jnp.exp(scores - jnp.max(scores, axis=0, keepdims=True))
            sums.append(jnp.sum(weights, axis=0, keepdims=True))
            probs[(turn - 1) * heads + head] = weights.astype(BF16)
    for copy in moves[2]:
        copy.wait_recv()
    for source in range(frames):
        for pair in range(2):
            begin = source * tokens + pair * half
            values[:, begin : begin + half] = got[2, pair, source]
    returns = []

    def give_back(turn):
        peer = lax.rem(frame + turn, frames)
        for side, (pair, target) in enumerate(((1 - here, far), (here, me))):
            if side == 1 and turn == frames:
                continue
            copy = pltpu.make_async_remote_copy(
                src_ref=done.at[pair, peer],
                dst_ref=back.at[here, frame],
                send_sem=out_send.at[side, turn],
                recv_sem=out_recv.at[side, turn],
                device_id={"rows": target, "frames": peer},
                device_id_type=MESH,
            )
            copy.start()
            returns.append(copy)

    for turn in range(1, frames + 1):
        peer = lax.rem(frame + turn, frames)
        for head in range(heads):
            cols = slice(head * HD, (head + 1) * HD)
            place = (turn - 1) * heads + head
            numerator = jnp.dot(values[cols, :], probs[place], preferred_element_type=F32)
            result = (numerator / sums[place]).astype(BF16)
            for pair in range(2):
                done[pair, peer, cols, :] = result[:, pair * half : (pair + 1) * half]
        give_back(turn)
    back[here, frame] = done[here, frame]
    for copy in lent:
        copy.wait_recv()
    for copy in returns:
        copy.wait_recv()
    att[...] = back[...].reshape(-1, half).astype(F32).T.astype(BF16)
    mix = output_w[...].reshape(-1, output_w.shape[2])
    core = lax.rem(me, 2)

    def mixed_term(owner):
        rows = pl.ds(pl.multiple_of(owner * size, size), size)
        return jnp.dot(att[rows, :], mix, preferred_element_type=F32)

    sent[1, 0] = mixed_term(1 - core).astype(BF16)
    share = remote(
        sent.at[1, 0], got_near.at[1, 0], sum_send.at[1, 0], sum_recv.at[1, 0], "rows", near
    )
    share.start()
    mixed = mixed_term(core)
    share.wait_recv()
    out_ref[...] = (hidden.astype(F32) + mixed + got_near[1, 0].astype(F32)).astype(BF16)
    share.wait_send()
    for copy in lent + returns:
        copy.wait_send()
    for batch in moves:
        for copy in batch:
            copy.wait_send()


def body_fast(
    latents,
    spatial_weight,
    spatial_bias,
    norm_gain,
    norm_shift,
    temporal_weight,
    temporal_bias,
    token_gain,
    query_weight,
    key_weight,
    value_weight,
    output_weight,
):
    channels = latents.shape[3]
    peers, frames = lax.axis_size("rows"), lax.axis_size("frames")
    block = latents.reshape(-1, channels)
    size = block.shape[0]
    tokens = size * peers
    width_cells = latents.shape[2]
    local_out = spatial_weight.shape[3]
    width = query_weight.shape[1] // frames
    main = local_out // LANES * LANES
    rest = local_out - main
    heads = width // HD
    links = 2 * PARTS + 1
    depth = CHUNK
    count = channels // depth
    denoised = pl.pallas_call(
        functools.partial(block_kernel, frames, width_cells, NORM_GROUPS // peers),
        out_shape=pltpu.VMEM(block.shape, BF16),
        in_specs=[ANY_SPEC] * 12,
        out_specs=VMEM_SPEC,
        scratch_shapes=[
            pltpu.VMEM((count, size, depth), BF16),
            pltpu.VMEM(block.shape, BF16),
            pltpu.VMEM(spatial_bias.shape, F32),
            pltpu.VMEM(norm_gain.shape, F32),
            pltpu.VMEM(norm_shift.shape, F32),
            pltpu.VMEM(temporal_bias.shape, F32),
            pltpu.VMEM(token_gain.shape, F32),
            pltpu.VMEM(spatial_weight.shape[:2] + (local_out, channels), BF16),
            pltpu.VMEM((3 * local_out, channels), BF16),
            pltpu.VMEM((3,) + query_weight.shape, BF16),
            pltpu.VMEM((2,) + output_weight.shape, BF16),
            pltpu.VMEM((count, peers, size, depth), BF16),
            pltpu.VMEM((count, 3, tokens + 2 * width_cells, depth), BF16),
            pltpu.VMEM((tokens, main), BF16),
            pltpu.VMEM((2, rest, tokens // 2), BF16),
            pltpu.VMEM((2, tokens, main), BF16),
            pltpu.VMEM((2, 2, rest, tokens // 2), BF16),
            pltpu.VMEM((2, tokens // 2, channels), F32),
            pltpu.VMEM(block.shape, BF16),
            pltpu.VMEM((peers,) + block.shape, BF16),
            pltpu.VMEM((3, 2, frames, width, tokens // 2), BF16),
            pltpu.VMEM((3, 2, frames, width, tokens // 2), BF16),
            pltpu.VMEM((frames * tokens, width), BF16),
            pltpu.VMEM((width, frames * tokens), BF16),
            pltpu.VMEM((frames * heads, frames * tokens, tokens), BF16),
            pltpu.VMEM((2, frames, width, tokens // 2), BF16),
            pltpu.VMEM((2, frames, width, tokens // 2), BF16),
            pltpu.VMEM((tokens // 2, 2 * frames * width), BF16),
            pltpu.VMEM((2, 3) + block.shape, BF16),
            pltpu.VMEM((2, 2) + block.shape, BF16),
            pltpu.VMEM((2,) + block.shape, BF16),
            DMA((11 + count,)),
            DMA((6,)),
            pltpu.SemaphoreType.REGULAR,
            DMA((3, count)),
            DMA((3, count)),
            DMA((2, peers)),
            DMA((2, peers)),
            DMA((links,)),
            DMA((links,)),
            DMA((3, 2, frames)),
            DMA((3, 2, frames)),
            DMA((2, frames + 1)),
            DMA((2, frames + 1)),
            DMA((2, 3)),
            DMA((2, 3)),
            DMA((2,)),
            DMA((2,)),
        ],
        compiler_params=pltpu.CompilerParams(
            collective_id=0, has_side_effects=True, vmem_limit_bytes=VMEM_LIMIT
        ),
    )(
        block,
        jnp.swapaxes(spatial_weight, 2, 3),
        spatial_bias,
        norm_gain,
        norm_shift,
        temporal_weight,
        temporal_bias,
        token_gain,
        query_weight,
        key_weight,
        value_weight,
        output_weight,
    )
    return denoised.reshape(latents.shape)


def fits(mesh):
    def choose(*args):
        latents, query_weight = args[0], args[8]
        peers, frames = mesh.shape["rows"], mesh.shape["frames"]
        heads = query_weight.shape[1] // HD
        tokens = latents.shape[0] * latents.shape[1] * latents.shape[2] * peers
        fast = (
            peers == 4
            and mesh.shape["frames"] == 4
            and latents.shape[3] % CHUNK == 0
            and args[1].shape[3] > LANES
            and args[1].shape[3] % LANES >= 16
            and args[1].shape[3] % 16 == 0
            and args[1].shape[3] % (8 * (NORM_GROUPS // peers)) == 0
            and latents.shape[1] == 1
            and heads % frames == 0
            and tokens % 256 == 0
            and latents.shape[2] % 16 == 0
            and latents.shape[0] * latents.shape[2] % (16 * PARTS) == 0
        )
        return (body_fast if fast else body)(*args)

    return choose


def solution(mesh):
    in_specs = (
        P("rows", ("groups", "frames"), None, None),
        P(None, None, None, "rows"),
        P("rows"),
        P("rows"),
        P("rows"),
        P(None, "rows", None),
        P(),
        P(),
        P(None, "rows"),
        P(None, "rows"),
        P(None, "rows"),
        P("rows", None),
    )
    out_specs = P("rows", ("groups", "frames"), None, None)
    return jax.shard_map(
        fits(mesh), mesh=mesh, in_specs=in_specs, out_specs=out_specs, check_vma=False
    )
```

```python
import functools
import math

import jax
import jax.numpy as jnp
from jax import lax
from jax.experimental import pallas as pl
from jax.experimental.pallas import tpu as pltpu
from jax.sharding import PartitionSpec as P

HD = 64
NORM_GROUPS = 32


def padded_2(array, sides, width):
    for axis, dim in sides:
        peers, length = (lax.axis_size(axis), array.shape[dim])
        up = [(i, (i + 1) % peers) for i in range(peers - 1)]
        down = [(j, i) for i, j in up]
        last = lax.slice_in_dim(array, length - width, length, axis=dim)
        leading = lax.slice_in_dim(array, 0, width, axis=dim)
        before = lax.ppermute(last, axis, up)
        after = lax.ppermute(leading, axis, down)
        array = jnp.concatenate([before, array, after], axis=dim)
    return array


def shifted_2(value, axis, steps):
    count = lax.axis_size(axis)
    pairs = [(source, (source + steps) % count) for source in range(count)]
    return lax.ppermute(value, axis, pairs)


def conv_plane(field, weight, bias):
    rows_n, frames_n, cols_n, chans = field.shape
    padded = jnp.pad(field, ((1, 1), (0, 0), (1, 1), (0, 0)))
    total = jnp.zeros((rows_n * frames_n * cols_n, weight.shape[3]), jnp.float32)
    for row_off in range(3):
        for col_off in range(3):
            window = padded[row_off : row_off + rows_n, :, col_off : col_off + cols_n, :].reshape(
                -1, chans
            )
            total = total + jnp.dot(
                window, weight[row_off, col_off], preferred_element_type=jnp.float32
            )
    return total.reshape(rows_n, frames_n, cols_n, -1) + bias


def layer_norm(field, token_gain):
    flat = field.astype(jnp.float32)
    token_mean = jnp.mean(flat, axis=-1, keepdims=True)
    shifted = flat - token_mean
    token_var = jnp.mean(shifted * shifted, axis=-1, keepdims=True)
    return (shifted / jnp.sqrt(token_var + 1e-05) * token_gain).astype(jnp.bfloat16)


def attend(queries, carried, keys, values):
    block = queries.shape[0]
    head_count = queries.shape[1]
    block_count = keys.shape[0] // block
    key_blocks = keys.reshape(block_count, block, head_count, HD)
    value_blocks = values.reshape(block_count, block, head_count, HD)
    scale = 1.0 / math.sqrt(HD)

    def visit_block(state, block_pair):
        running_max, denominator, numerator = state
        key_block, value_block = block_pair
        scores = (
            jnp.einsum("qhd,khd->qhk", queries, key_block, preferred_element_type=jnp.float32)
            * scale
        )
        new_max = jnp.maximum(running_max, jnp.max(scores, axis=-1))
        shrink = jnp.exp(running_max - new_max)
        weights = jnp.exp(scores - new_max[..., None])
        denominator = denominator * shrink + jnp.sum(weights, axis=-1)
        numerator = numerator * shrink[..., None] + jnp.einsum(
            "qhk,khd->qhd",
            weights.astype(jnp.bfloat16),
            value_block,
            preferred_element_type=jnp.float32,
        )
        return ((new_max, denominator, numerator), None)

    result, _ = lax.scan(visit_block, carried, (key_blocks, value_blocks))
    return result


def body(
    latents,
    spatial_weight,
    spatial_bias,
    norm_gain,
    norm_shift,
    temporal_weight,
    temporal_bias,
    token_gain,
    query_weight,
    key_weight,
    value_weight,
    output_weight,
):
    row_count, frame_count, width_cells, channels = latents.shape
    plane = lax.all_gather(latents, "rows", axis=0, tiled=True)
    plane_rows = plane.shape[0]
    local_out = spatial_weight.shape[3]
    spatial = conv_plane(plane, spatial_weight, spatial_bias)
    local_groups = NORM_GROUPS // lax.axis_size("rows")
    grouped = spatial.reshape(plane_rows, frame_count, width_cells, local_groups, -1)
    group_mean = jnp.mean(grouped, axis=(0, 2, 4), keepdims=True)
    centred = grouped - group_mean
    group_var = jnp.mean(centred * centred, axis=(0, 2, 4), keepdims=True)
    scaled = (centred / jnp.sqrt(group_var + 1e-05)).reshape(
        plane_rows, frame_count, width_cells, local_out
    ) * norm_gain + norm_shift
    activated = jax.nn.silu(scaled).astype(jnp.bfloat16)
    rim = padded_2(activated, (("frames", 1),), 1)
    row_total = row_count * lax.axis_size("rows")
    row_piece = rim
    total = jnp.zeros((row_total * frame_count * width_cells, channels), jnp.float32)
    for lag_index in range(3):
        window = row_piece[:, lag_index : lag_index + frame_count].reshape(-1, local_out)
        total = total + jnp.dot(
            window, temporal_weight[lag_index], preferred_element_type=jnp.float32
        )
    temporal = lax.psum_scatter(
        total.reshape(row_total, frame_count, width_cells, channels).astype(jnp.bfloat16),
        "rows",
        scatter_dimension=0,
        tiled=True,
    ).astype(jnp.float32)
    hidden = (latents.astype(jnp.float32) + temporal + temporal_bias).astype(jnp.bfloat16)
    normed_all = lax.all_gather(layer_norm(hidden, token_gain), "rows", axis=0, tiled=True)
    flat = normed_all.reshape(-1, channels)
    head_cols = query_weight.shape[1]
    head_count = head_cols // HD
    token_count = flat.shape[0]
    queries = jnp.dot(flat, query_weight, preferred_element_type=jnp.float32).astype(jnp.bfloat16)
    keys = jnp.dot(flat, key_weight, preferred_element_type=jnp.float32).astype(jnp.bfloat16)
    values = jnp.dot(flat, value_weight, preferred_element_type=jnp.float32).astype(jnp.bfloat16)
    start_state = (
        jnp.full((token_count, head_count), -1e30, jnp.float32),
        jnp.zeros((token_count, head_count), jnp.float32),
        jnp.zeros((token_count, head_count, HD), jnp.float32),
    )
    local_keys = keys.reshape(token_count, head_count, HD)
    local_values = values.reshape(token_count, head_count, HD)

    def travel(turn, state):
        query_moving, running_max, denominator, numerator = state
        running_max, denominator, numerator = attend(
            query_moving, (running_max, denominator, numerator), local_keys, local_values
        )
        return (
            shifted_2(query_moving, "frames", 1),
            shifted_2(running_max.astype(jnp.bfloat16), "frames", 1).astype(running_max.dtype),
            shifted_2(denominator.astype(jnp.bfloat16), "frames", 1).astype(denominator.dtype),
            shifted_2(numerator.astype(jnp.bfloat16), "frames", 1).astype(numerator.dtype),
        )

    start_moving = queries.reshape(token_count, head_count, HD)
    final = lax.fori_loop(0, lax.axis_size("frames"), travel, (start_moving,) + start_state)
    denominator, numerator = (final[2], final[3])
    attended = (
        (numerator / denominator[..., None])
        .astype(jnp.bfloat16)
        .reshape(plane_rows, frame_count, width_cells, head_cols)
    )
    row_piece = attended
    mixed = lax.psum_scatter(
        jnp.dot(row_piece.reshape(-1, head_cols), output_weight, preferred_element_type=jnp.float32)
        .reshape(row_count * lax.axis_size("rows"), frame_count, width_cells, channels)
        .astype(jnp.bfloat16),
        "rows",
        scatter_dimension=0,
        tiled=True,
    ).astype(jnp.float32)
    return (hidden.astype(jnp.float32) + mixed).astype(jnp.bfloat16)


MESH = pl.DeviceIdType.MESH
DMA = pltpu.SemaphoreType.DMA
VMEM_SPEC = pl.BlockSpec(memory_space=pltpu.VMEM)
ANY_SPEC = pl.BlockSpec(memory_space=pl.ANY)
BF16 = jnp.bfloat16
F32 = jnp.float32
VMEM_LIMIT = 54 << 20
PARTS = 2
CHUNK = 256
LANES = 128


def remote(src, dst, send, recv, axis, peer):
    return pltpu.make_async_remote_copy(
        src_ref=src,
        dst_ref=dst,
        send_sem=send,
        recv_sem=recv,
        device_id={axis: peer},
        device_id_type=MESH,
    )


def greet(barrier, axis, peer):
    pl.semaphore_signal(barrier, inc=1, device_id={axis: peer}, device_id_type=MESH)


def row(ref):
    return ref[...].reshape(1, -1)


def column(ref):
    value = jnp.broadcast_to(row(ref), (8, ref.shape[0]))
    return value.T[:, :1]


def convolve_chunk(plane, shifted, weight, chunk, width):
    blocks, size, depth = plane.shape
    tokens = blocks * size
    edge = jnp.zeros((width, depth), BF16)
    place = lax.broadcasted_iota(jnp.int32, (size, depth), 0) % width
    for offset in range(3):
        shifted[offset, :width, :] = edge
        shifted[offset, tokens + width :, :] = edge
    for block in range(blocks):
        rows = slice(width + block * size, width + (block + 1) * size)
        value = plane[block]
        wide = value.astype(F32)
        before = jnp.where(place == 0, 0.0, pltpu.roll(wide, 1, 0))
        after = jnp.where(place == width - 1, 0.0, pltpu.roll(wide, size - 1, 0))
        shifted[0, rows, :] = before.astype(BF16)
        shifted[1, rows, :] = value
        shifted[2, rows, :] = after.astype(BF16)
    total = None
    for row_off in range(3):
        for col_off in range(3):
            window = shifted[col_off, row_off * width : row_off * width + tokens, :]
            part = lax.dot_general(
                weight[row_off, col_off, :, chunk * depth : (chunk + 1) * depth],
                window,
                (((1,), (1,)), ((), ())),
                preferred_element_type=F32,
            )
            total = part if total is None else total + part
    return total


def group_norm_silu(spatial, gain, shift, groups):
    channels, tokens = spatial.shape

    def group_mean(value):
        return jnp.mean(value, axis=(1, 2), keepdims=True)

    grouped = spatial.reshape(groups, channels // groups, tokens)
    centred = grouped - group_mean(grouped)
    scale = 1.0 / jnp.sqrt(group_mean(centred * centred) + 1e-05)
    value = (centred * scale).reshape(channels, tokens) * gain + shift
    return value / (1.0 + jnp.exp(-value))


def block_kernel(
    frames,
    width_cells,
    groups,
    latents_hbm,
    spatial_hbm,
    bias_hbm,
    gain_hbm,
    shift_hbm,
    temporal_hbm,
    temporal_bias_hbm,
    token_gain_hbm,
    query_hbm,
    key_hbm,
    value_hbm,
    output_hbm,
    out_ref,
    chunks,
    latents,
    spatial_bias,
    norm_gain,
    norm_shift,
    temporal_bias,
    token_gain,
    spatial_w,
    temporal_w,
    project_w,
    output_w,
    plane,
    shifted,
    act,
    act_rest,
    halo,
    halo_rest,
    terms,
    hidden,
    normed_all,
    outgoing,
    got,
    values,
    probs,
    done,
    back,
    att,
    sent,
    got_near,
    got_far,
    got_own,
    partial,
    final,
    load_sem,
    tap_sem,
    ready,
    lat_send,
    lat_recv,
    halo_send,
    halo_recv,
    gat_send,
    gat_recv,
    in_send,
    in_recv,
    out_send,
    out_recv,
    sum_send,
    sum_recv,
    lend_send,
    lend_recv,
):
    me = lax.axis_index("rows")
    frame = lax.axis_index("frames")
    near, far = me ^ 1, me ^ 2
    has_prev, has_next = frame > 0, frame < frames - 1
    prev = jnp.maximum(frame - 1, 0)
    later = jnp.minimum(frame + 1, frames - 1)
    barrier = pltpu.get_barrier_semaphore()
    greet(barrier, "rows", far)

    @pl.when(has_next)
    def _():
        greet(barrier, "frames", later)

    @pl.when(has_prev)
    def _():
        greet(barrier, "frames", prev)

    greet(barrier, "rows", near)
    count, size, depth = chunks.shape
    main, rest = act.shape[1], act_rest.shape[1]
    loads, pieces = [], []
    for index in range(count):
        load = pltpu.make_async_copy(
            latents_hbm.at[:, index * depth : (index + 1) * depth],
            chunks.at[index],
            load_sem.at[index],
        )
        load.start()
        pieces.append(load)
    for index, (src, dst) in enumerate(
        (
            (bias_hbm, spatial_bias),
            (spatial_hbm, spatial_w),
            (gain_hbm, norm_gain),
            (shift_hbm, norm_shift),
            (latents_hbm, latents),
            (temporal_bias_hbm, temporal_bias),
            (token_gain_hbm, token_gain),
            (key_hbm, project_w.at[0]),
            (query_hbm, project_w.at[1]),
            (value_hbm, project_w.at[2]),
            (output_hbm, output_w.at[me // 2]),
        )
    ):
        load = pltpu.make_async_copy(src, dst, load_sem.at[count + index])
        load.start()
        loads.append(load)
        if index == 3:
            taps = []
            for tap in range(3):
                for start, stop, place in (
                    (0, main, tap * main),
                    (main, main + rest, 3 * main + tap * rest),
                ):
                    load = pltpu.make_async_copy(
                        temporal_hbm.at[tap, start:stop],
                        temporal_w.at[place : place + stop - start],
                        tap_sem.at[len(taps)],
                    )
                    load.start()
                    taps.append(load)
    for load in pieces:
        load.wait()
    pl.semaphore_wait(
        barrier, 2 + has_prev.astype(jnp.int32) + has_next.astype(jnp.int32)
    )

    across, onward = [], []
    for index in range(count):
        across.append(
            remote(
                chunks.at[index],
                plane.at[index, me],
                lat_send.at[0, index],
                lat_recv.at[0, index],
                "rows",
                far,
            )
        )
        onward.append(
            remote(
                plane.at[index, far],
                plane.at[index, far],
                lat_send.at[1, index],
                lat_recv.at[1, index],
                "rows",
                near,
            )
        )
        across[index].start()
    beside = remote(
        chunks, plane.at[:, me], lat_send.at[2, 0], lat_recv.at[2, 0], "rows", near
    )
    beside.start()
    for index in range(count):
        plane[index, me] = chunks[index]
    for load in loads[:2]:
        load.wait()
    beside.wait_recv()
    spatial = column(spatial_bias)
    for index in range(count):
        across[index].wait_recv()
        onward[index].start()
    here = me // 2
    depth_out = output_w.shape[1]
    early = depth_out * 9 // 16 // 16 * 16
    loads[10].wait()
    lent = []
    for index, rows in enumerate((pl.ds(0, early), pl.ds(early, depth_out - early))):
        lent.append(
            remote(
                output_w.at[here, rows],
                output_w.at[here, rows],
                lend_send.at[index],
                lend_recv.at[index],
                "rows",
                far,
            )
        )
    lent[0].start()
    for index in range(count):
        onward[index].wait_recv()
    for index in range(count):
        spatial = spatial + convolve_chunk(
            plane.at[index], shifted.at[index], spatial_w, index, width_cells
        )
    for load in loads[2:4]:
        load.wait()
    value = group_norm_silu(spatial, column(norm_gain), column(norm_shift), groups)
    half = act_rest.shape[2]
    act[...] = value[:main].T.astype(BF16)
    for pair in range(2):
        act_rest[pair] = value[main:, pair * half : (pair + 1) * half].astype(BF16)
    for copy in across + onward + [beside]:
        copy.wait_send()


    up, down = [], []
    for turn, pair in enumerate((1 - here, here)):
        rows = pl.ds(pl.multiple_of(pair * half, half), half)
        for side, (copies, peer) in enumerate(((up, later), (down, prev))):
            for index, (src, dst) in enumerate(
                ((act.at[rows], halo.at[side, rows]), (act_rest.at[pair], halo_rest.at[side, pair]))
            ):
                copies.append(
                    remote(
                        src,
                        dst,
                        halo_send.at[side, 2 * turn + index],
                        halo_recv.at[side, 2 * turn + index],
                        "frames",
                        peer,
                    )
                )

    for turn in range(2):
        for exists, copies in ((has_next, up), (has_prev, down)):

            @pl.when(exists)
            def _(part=copies[2 * turn : 2 * turn + 2]):
                for copy in part:
                    copy.start()

    @pl.when(jnp.logical_not(has_prev))
    def _():
        halo[0] = jnp.zeros(halo.shape[1:], halo.dtype)
        halo_rest[0] = jnp.zeros(halo_rest.shape[1:], halo.dtype)

    @pl.when(jnp.logical_not(has_next))
    def _():
        halo[1] = jnp.zeros(halo.shape[1:], halo.dtype)
        halo_rest[1] = jnp.zeros(halo_rest.shape[1:], halo.dtype)

    for load in taps:
        load.wait()

    def temporal_term(pair, turn):
        rows = pl.ds(pl.multiple_of(pair * half, half), half)

        @pl.when(has_prev)
        def _():
            for copy in up[2 * turn : 2 * turn + 2]:
                copy.wait_recv()

        @pl.when(has_next)
        def _():
            for copy in down[2 * turn : 2 * turn + 2]:
                copy.wait_recv()

        left = jnp.concatenate([halo_rest[0, pair], act_rest[pair], halo_rest[1, pair]], axis=0)
        window = jnp.concatenate(
            [halo[0, rows, :], act[rows, :], halo[1, rows, :], left.astype(F32).T.astype(BF16)],
            axis=1,
        )
        return jnp.dot(window, temporal_w[...], preferred_element_type=F32)

    core = lax.rem(me, 2)
    step = size // PARTS
    spans = [slice(part * step, (part + 1) * step) for part in range(PARTS)]

    def share(slot, owner, part):
        start = pl.multiple_of(owner * size + part * step, step)
        return terms[slot, pl.ds(start, step), :]

    def hand(slot, pair):
        terms[slot] = temporal_term(pair, slot)
        for part, span in enumerate(spans):
            sent[slot, span, :] = share(slot, 1 - core, part).astype(BF16)
        copy = remote(
            sent.at[slot], got_near.at[slot], sum_send.at[slot], sum_recv.at[slot], "rows", near
        )
        copy.start()
        return copy

    first = hand(0, 1 - here)
    first.wait_recv()
    over = []
    for part, span in enumerate(spans):
        value = share(0, core, part) + got_near[0, span, :].astype(F32)
        partial[0, span, :] = value
        sent[2, span, :] = value.astype(BF16)
        copy = remote(
            sent.at[2, span],
            got_far.at[span],
            sum_send.at[2 + part],
            sum_recv.at[2 + part],
            "rows",
            far,
        )
        copy.start()
        over.append(copy)
    second = hand(1, here)
    second.wait_recv()
    for part, span in enumerate(spans):
        value = share(1, core, part) + got_near[1, span, :].astype(F32)
        partial[1, span, :] = value
        sent[3, span, :] = value.astype(BF16)
        copy = remote(
            sent.at[3, span],
            got_own.at[span],
            sum_send.at[2 + PARTS + part],
            sum_recv.at[2 + PARTS + part],
            "rows",
            far,
        )
        copy.start()
        over.append(copy)
    lent[1].start()
    for load in loads[4:7]:
        load.wait()

    @pl.when(jnp.logical_and(has_prev, frame == frames - 3))
    def _():
        pl.semaphore_signal(ready, inc=1, device_id={"frames": prev}, device_id_type=MESH)

    @pl.when(jnp.logical_and(has_next, frame == 2))
    def _():
        pl.semaphore_signal(ready, inc=1, device_id={"frames": later}, device_id_type=MESH)

    @pl.when(has_next)
    def _():
        for copy in up:
            copy.wait_send()

    @pl.when(has_prev)
    def _():
        for copy in down:
            copy.wait_send()

    tokens = act.shape[0]
    moves = []

    def project(pair, start, length, slot):
        slab = normed_all[pl.ds(2 * pair, 2), start : start + length, :]
        slab = slab.reshape(2 * length, slab.shape[2])
        span = pl.ds(start, length)
        for kind in range(3):
            cols = jnp.dot(slab, project_w[kind], preferred_element_type=F32)
            for owner in range(frames):
                head = cols[:, owner * HD : (owner + 1) * HD]
                outgoing[pair, owner, kind, span, :] = jnp.concatenate(
                    [head[:length], head[length:]], axis=1
                ).astype(BF16)
        for turn in range(1, frames):
            peer = lax.rem(frame + turn, frames)
            copy = remote(
                outgoing.at[pair, peer, :, span],
                got.at[pair, frame, :, span],
                in_send.at[slot, turn],
                in_recv.at[slot, turn],
                "frames",
                peer,
            )
            copy.start()
            moves.append(copy)
        got[pair, frame, :, span, :] = outgoing[pair, frame, :, span, :]

    def normalise(slot, part, base, other):
        span = spans[part]
        total = partial[slot, span, :] + other[span, :].astype(F32) + row(temporal_bias)
        value = (base.astype(F32) + total).astype(BF16)
        flat = value.astype(F32)
        centred = flat - jnp.mean(flat, axis=-1, keepdims=True)
        var = jnp.mean(centred * centred, axis=-1, keepdims=True)
        return value, (centred / jnp.sqrt(var + 1e-05) * row(token_gain)).astype(BF16)

    gathers = []

    def give(block, slot, part, value):
        place = normed_all.at[block, spans[part]]
        normed_all[block, spans[part], :] = value
        copy = remote(
            place, place, gat_send.at[slot, part], gat_recv.at[slot, part], "rows", near
        )
        copy.start()
        gathers.append(copy)
        return copy

    def ready_part(index):
        slot, part = index // PARTS, index % PARTS
        span = spans[part]
        over[index].wait_recv()
        if slot == 0:
            hidden[span, :], value = normalise(1, part, latents[span, :], got_far)
            return give(me, 0, part, value)
        base = jnp.concatenate([plane[index, far, span, :] for index in range(count)], axis=1)
        _, value = normalise(0, part, base, got_own)
        return give(far, 1, part, value)

    pending = ready_part(0)
    for load in loads[7:10]:
        load.wait()

    @pl.when(jnp.logical_not(jnp.logical_and(has_prev, has_next)))
    def _():
        pl.semaphore_wait(ready, 1)

    for index in range(2 * PARTS):
        pending.wait_recv()
        project(here if index < PARTS else 1 - here, index % PARTS * step, step, index)
        if index + 1 < 2 * PARTS:
            pending = ready_part(index + 1)

    for copy in moves:
        copy.wait_recv()
    scale = 1.0 / math.sqrt(HD)
    keys = got[:, :, 0].reshape(-1, LANES)
    values[...] = got[:, :, 2].reshape(-1, LANES).astype(F32).T.astype(BF16)
    sums = []
    for turn in range(1, frames + 1):
        peer = lax.rem(frame + turn, frames)
        pieces = []
        for pair in range(2):
            flipped = got[pair, peer, 1].astype(F32).T
            pieces += [flipped[:HD], flipped[HD:]]
        query = (jnp.concatenate(pieces, axis=1) * scale).astype(BF16)
        zero = jnp.zeros_like(query)
        block = jnp.concatenate(
            [jnp.concatenate([query, zero], axis=1), jnp.concatenate([zero, query], axis=1)],
            axis=0,
        )
        scores = jnp.dot(keys, block, preferred_element_type=F32)
        peak = jnp.max(scores, axis=0, keepdims=True)
        peak = jnp.maximum(peak[:, :tokens], peak[:, tokens:])
        weights = jnp.exp(scores - jnp.concatenate([peak, peak], axis=1))
        total = jnp.sum(weights, axis=0, keepdims=True)
        sums.append(total[:, :tokens] + total[:, tokens:])
        probs[turn - 1] = weights.astype(BF16)
    returns = []

    def give_back(turn):
        peer = lax.rem(frame + turn, frames)
        for side, (pair, target) in enumerate(((1 - here, far), (here, me))):
            if side == 1 and turn == frames:
                continue
            copy = pltpu.make_async_remote_copy(
                src_ref=done.at[pair, peer],
                dst_ref=back.at[here, frame],
                send_sem=out_send.at[side, turn],
                recv_sem=out_recv.at[side, turn],
                device_id={"rows": target, "frames": peer},
                device_id_type=MESH,
            )
            copy.start()
            returns.append(copy)

    for turn in range(1, frames + 1):
        peer = lax.rem(frame + turn, frames)
        numerator = jnp.dot(
            values[:HD, :], probs[turn - 1, :, :tokens], preferred_element_type=F32
        ) + jnp.dot(values[HD:, :], probs[turn - 1, :, tokens:], preferred_element_type=F32)
        result = (numerator / sums[turn - 1]).astype(BF16)
        for pair in range(2):
            done[pair, peer] = result[:, pair * half : (pair + 1) * half]
        give_back(turn)
    back[here, frame] = done[here, frame]
    for copy in lent:
        copy.wait_recv()
    for copy in returns:
        copy.wait_recv()
    att[...] = back[...].reshape(-1, half).astype(F32).T.astype(BF16)
    mix = output_w[...].reshape(-1, output_w.shape[2])
    def mixed_term(owner):
        rows = pl.ds(pl.multiple_of(owner * size, size), size)
        return jnp.dot(att[rows, :], mix, preferred_element_type=F32)

    final[0] = mixed_term(1 - core).astype(BF16)
    swap = remote(
        final.at[0], final.at[1], sum_send.at[2 + 2 * PARTS], sum_recv.at[2 + 2 * PARTS], "rows", near
    )
    swap.start()
    mixed = mixed_term(core)
    swap.wait_recv()
    out_ref[...] = (hidden[...].astype(F32) + mixed + final[1].astype(F32)).astype(BF16)
    for copy in [first, second, swap] + over + gathers:
        copy.wait_send()
    for copy in lent + returns:
        copy.wait_send()
    for copy in moves:
        copy.wait_send()


def body_fast(
    latents,
    spatial_weight,
    spatial_bias,
    norm_gain,
    norm_shift,
    temporal_weight,
    temporal_bias,
    token_gain,
    query_weight,
    key_weight,
    value_weight,
    output_weight,
):
    channels = latents.shape[3]
    peers, frames = lax.axis_size("rows"), lax.axis_size("frames")
    block = latents.reshape(-1, channels)
    size = block.shape[0]
    tokens = size * peers
    width_cells = latents.shape[2]
    local_out = spatial_weight.shape[3]
    width = query_weight.shape[1] // frames
    main = local_out // LANES * LANES
    rest = local_out - main
    depth = CHUNK
    count = channels // depth
    denoised = pl.pallas_call(
        functools.partial(block_kernel, frames, width_cells, NORM_GROUPS // peers),
        out_shape=pltpu.VMEM(block.shape, BF16),
        in_specs=[ANY_SPEC] * 12,
        out_specs=VMEM_SPEC,
        scratch_shapes=[
            pltpu.VMEM((count, size, depth), BF16),
            pltpu.VMEM(block.shape, BF16),
            pltpu.VMEM(spatial_bias.shape, F32),
            pltpu.VMEM(norm_gain.shape, F32),
            pltpu.VMEM(norm_shift.shape, F32),
            pltpu.VMEM(temporal_bias.shape, F32),
            pltpu.VMEM(token_gain.shape, F32),
            pltpu.VMEM(spatial_weight.shape[:2] + (local_out, channels), BF16),
            pltpu.VMEM((3 * local_out, channels), BF16),
            pltpu.VMEM((3,) + query_weight.shape, BF16),
            pltpu.VMEM((2,) + output_weight.shape, BF16),
            pltpu.VMEM((count, peers, size, depth), BF16),
            pltpu.VMEM((count, 3, tokens + 2 * width_cells, depth), BF16),
            pltpu.VMEM((tokens, main), BF16),
            pltpu.VMEM((2, rest, tokens // 2), BF16),
            pltpu.VMEM((2, tokens, main), BF16),
            pltpu.VMEM((2, 2, rest, tokens // 2), BF16),
            pltpu.VMEM((2, tokens // 2, channels), F32),
            pltpu.VMEM(block.shape, BF16),
            pltpu.VMEM((peers,) + block.shape, BF16),
            pltpu.VMEM((2, frames, 3, size, LANES), BF16),
            pltpu.VMEM((2, frames, 3, size, LANES), BF16),
            pltpu.VMEM((LANES, 2 * frames * size), BF16),
            pltpu.VMEM((frames, 2 * frames * size, 2 * tokens), BF16),
            pltpu.VMEM((2, frames, width, tokens // 2), BF16),
            pltpu.VMEM((2, frames, width, tokens // 2), BF16),
            pltpu.VMEM((tokens // 2, 2 * frames * width), BF16),
            pltpu.VMEM((4,) + block.shape, BF16),
            pltpu.VMEM((2,) + block.shape, BF16),
            pltpu.VMEM(block.shape, BF16),
            pltpu.VMEM(block.shape, BF16),
            pltpu.VMEM((2,) + block.shape, F32),
            pltpu.VMEM((2,) + block.shape, BF16),
            DMA((11 + count,)),
            DMA((6,)),
            pltpu.SemaphoreType.REGULAR,
            DMA((3, count)),
            DMA((3, count)),
            DMA((2, peers)),
            DMA((2, peers)),
            DMA((2, PARTS)),
            DMA((2, PARTS)),
            DMA((2 * PARTS, frames)),
            DMA((2 * PARTS, frames)),
            DMA((2, frames + 1)),
            DMA((2, frames + 1)),
            DMA((3 + 2 * PARTS,)),
            DMA((3 + 2 * PARTS,)),
            DMA((2,)),
            DMA((2,)),
        ],
        compiler_params=pltpu.CompilerParams(
            collective_id=0, has_side_effects=True, vmem_limit_bytes=VMEM_LIMIT
        ),
    )(
        block,
        jnp.swapaxes(spatial_weight, 2, 3),
        spatial_bias,
        norm_gain,
        norm_shift,
        temporal_weight,
        temporal_bias,
        token_gain,
        query_weight,
        key_weight,
        value_weight,
        output_weight,
    )
    return denoised.reshape(latents.shape)


def fits(mesh):
    def choose(*args):
        latents, query_weight = args[0], args[8]
        peers, frames = mesh.shape["rows"], mesh.shape["frames"]
        heads = query_weight.shape[1] // HD
        tokens = latents.shape[0] * latents.shape[1] * latents.shape[2] * peers
        fast = (
            peers == 4
            and mesh.shape["frames"] == 4
            and latents.shape[3] % CHUNK == 0
            and args[1].shape[3] > LANES
            and args[1].shape[3] % LANES >= 16
            and args[1].shape[3] % 16 == 0
            and args[1].shape[3] % (8 * (NORM_GROUPS // peers)) == 0
            and latents.shape[1] == 1
            and heads == frames
            and 2 * HD == LANES
            and tokens % 256 == 0
            and latents.shape[2] % 16 == 0
            and latents.shape[0] * latents.shape[2] % (16 * PARTS) == 0
        )
        return (body_fast if fast else body)(*args)

    return choose


def solution(mesh):
    in_specs = (
        P("rows", ("groups", "frames"), None, None),
        P(None, None, None, "rows"),
        P("rows"),
        P("rows"),
        P("rows"),
        P(None, "rows", None),
        P(),
        P(),
        P(None, "rows"),
        P(None, "rows"),
        P(None, "rows"),
        P("rows", None),
    )
    out_specs = P("rows", ("groups", "frames"), None, None)
    return jax.shard_map(
        fits(mesh), mesh=mesh, in_specs=in_specs, out_specs=out_specs, check_vma=False
    )
```

```python
import functools
import math

import jax
import jax.numpy as jnp
from jax import lax
from jax.experimental import pallas as pl
from jax.experimental.pallas import tpu as pltpu
from jax.sharding import PartitionSpec as P

HD = 64
NORM_GROUPS = 32


def padded_2(array, sides, width):
    for axis, dim in sides:
        peers, length = (lax.axis_size(axis), array.shape[dim])
        up = [(i, (i + 1) % peers) for i in range(peers - 1)]
        down = [(j, i) for i, j in up]
        last = lax.slice_in_dim(array, length - width, length, axis=dim)
        leading = lax.slice_in_dim(array, 0, width, axis=dim)
        before = lax.ppermute(last, axis, up)
        after = lax.ppermute(leading, axis, down)
        array = jnp.concatenate([before, array, after], axis=dim)
    return array


def shifted_2(value, axis, steps):
    count = lax.axis_size(axis)
    pairs = [(source, (source + steps) % count) for source in range(count)]
    return lax.ppermute(value, axis, pairs)


def conv_plane(field, weight, bias):
    rows_n, frames_n, cols_n, chans = field.shape
    padded = jnp.pad(field, ((1, 1), (0, 0), (1, 1), (0, 0)))
    total = jnp.zeros((rows_n * frames_n * cols_n, weight.shape[3]), jnp.float32)
    for row_off in range(3):
        for col_off in range(3):
            window = padded[row_off : row_off + rows_n, :, col_off : col_off + cols_n, :].reshape(
                -1, chans
            )
            total = total + jnp.dot(
                window, weight[row_off, col_off], preferred_element_type=jnp.float32
            )
    return total.reshape(rows_n, frames_n, cols_n, -1) + bias


def layer_norm(field, token_gain):
    flat = field.astype(jnp.float32)
    token_mean = jnp.mean(flat, axis=-1, keepdims=True)
    shifted = flat - token_mean
    token_var = jnp.mean(shifted * shifted, axis=-1, keepdims=True)
    return (shifted / jnp.sqrt(token_var + 1e-05) * token_gain).astype(jnp.bfloat16)


def attend(queries, carried, keys, values):
    block = queries.shape[0]
    head_count = queries.shape[1]
    block_count = keys.shape[0] // block
    key_blocks = keys.reshape(block_count, block, head_count, HD)
    value_blocks = values.reshape(block_count, block, head_count, HD)
    scale = 1.0 / math.sqrt(HD)

    def visit_block(state, block_pair):
        running_max, denominator, numerator = state
        key_block, value_block = block_pair
        scores = (
            jnp.einsum("qhd,khd->qhk", queries, key_block, preferred_element_type=jnp.float32)
            * scale
        )
        new_max = jnp.maximum(running_max, jnp.max(scores, axis=-1))
        shrink = jnp.exp(running_max - new_max)
        weights = jnp.exp(scores - new_max[..., None])
        denominator = denominator * shrink + jnp.sum(weights, axis=-1)
        numerator = numerator * shrink[..., None] + jnp.einsum(
            "qhk,khd->qhd",
            weights.astype(jnp.bfloat16),
            value_block,
            preferred_element_type=jnp.float32,
        )
        return ((new_max, denominator, numerator), None)

    result, _ = lax.scan(visit_block, carried, (key_blocks, value_blocks))
    return result


def body(
    latents,
    spatial_weight,
    spatial_bias,
    norm_gain,
    norm_shift,
    temporal_weight,
    temporal_bias,
    token_gain,
    query_weight,
    key_weight,
    value_weight,
    output_weight,
):
    row_count, frame_count, width_cells, channels = latents.shape
    plane = lax.all_gather(latents, "rows", axis=0, tiled=True)
    plane_rows = plane.shape[0]
    local_out = spatial_weight.shape[3]
    spatial = conv_plane(plane, spatial_weight, spatial_bias)
    local_groups = NORM_GROUPS // lax.axis_size("rows")
    grouped = spatial.reshape(plane_rows, frame_count, width_cells, local_groups, -1)
    group_mean = jnp.mean(grouped, axis=(0, 2, 4), keepdims=True)
    centred = grouped - group_mean
    group_var = jnp.mean(centred * centred, axis=(0, 2, 4), keepdims=True)
    scaled = (centred / jnp.sqrt(group_var + 1e-05)).reshape(
        plane_rows, frame_count, width_cells, local_out
    ) * norm_gain + norm_shift
    activated = jax.nn.silu(scaled).astype(jnp.bfloat16)
    rim = padded_2(activated, (("frames", 1),), 1)
    row_total = row_count * lax.axis_size("rows")
    row_piece = rim
    total = jnp.zeros((row_total * frame_count * width_cells, channels), jnp.float32)
    for lag_index in range(3):
        window = row_piece[:, lag_index : lag_index + frame_count].reshape(-1, local_out)
        total = total + jnp.dot(
            window, temporal_weight[lag_index], preferred_element_type=jnp.float32
        )
    temporal = lax.psum_scatter(
        total.reshape(row_total, frame_count, width_cells, channels).astype(jnp.bfloat16),
        "rows",
        scatter_dimension=0,
        tiled=True,
    ).astype(jnp.float32)
    hidden = (latents.astype(jnp.float32) + temporal + temporal_bias).astype(jnp.bfloat16)
    normed_all = lax.all_gather(layer_norm(hidden, token_gain), "rows", axis=0, tiled=True)
    flat = normed_all.reshape(-1, channels)
    head_cols = query_weight.shape[1]
    head_count = head_cols // HD
    token_count = flat.shape[0]
    queries = jnp.dot(flat, query_weight, preferred_element_type=jnp.float32).astype(jnp.bfloat16)
    keys = jnp.dot(flat, key_weight, preferred_element_type=jnp.float32).astype(jnp.bfloat16)
    values = jnp.dot(flat, value_weight, preferred_element_type=jnp.float32).astype(jnp.bfloat16)
    start_state = (
        jnp.full((token_count, head_count), -1e30, jnp.float32),
        jnp.zeros((token_count, head_count), jnp.float32),
        jnp.zeros((token_count, head_count, HD), jnp.float32),
    )
    local_keys = keys.reshape(token_count, head_count, HD)
    local_values = values.reshape(token_count, head_count, HD)

    def travel(turn, state):
        query_moving, running_max, denominator, numerator = state
        running_max, denominator, numerator = attend(
            query_moving, (running_max, denominator, numerator), local_keys, local_values
        )
        return (
            shifted_2(query_moving, "frames", 1),
            shifted_2(running_max.astype(jnp.bfloat16), "frames", 1).astype(running_max.dtype),
            shifted_2(denominator.astype(jnp.bfloat16), "frames", 1).astype(denominator.dtype),
            shifted_2(numerator.astype(jnp.bfloat16), "frames", 1).astype(numerator.dtype),
        )

    start_moving = queries.reshape(token_count, head_count, HD)
    final = lax.fori_loop(0, lax.axis_size("frames"), travel, (start_moving,) + start_state)
    denominator, numerator = (final[2], final[3])
    attended = (
        (numerator / denominator[..., None])
        .astype(jnp.bfloat16)
        .reshape(plane_rows, frame_count, width_cells, head_cols)
    )
    row_piece = attended
    mixed = lax.psum_scatter(
        jnp.dot(row_piece.reshape(-1, head_cols), output_weight, preferred_element_type=jnp.float32)
        .reshape(row_count * lax.axis_size("rows"), frame_count, width_cells, channels)
        .astype(jnp.bfloat16),
        "rows",
        scatter_dimension=0,
        tiled=True,
    ).astype(jnp.float32)
    return (hidden.astype(jnp.float32) + mixed).astype(jnp.bfloat16)


MESH = pl.DeviceIdType.MESH
DMA = pltpu.SemaphoreType.DMA
VMEM_SPEC = pl.BlockSpec(memory_space=pltpu.VMEM)
ANY_SPEC = pl.BlockSpec(memory_space=pl.ANY)
BF16 = jnp.bfloat16
F32 = jnp.float32
VMEM_LIMIT = 54 << 20
PARTS = 2
CHUNK = 256
LANES = 128


def remote(src, dst, send, recv, axis, peer):
    return pltpu.make_async_remote_copy(
        src_ref=src,
        dst_ref=dst,
        send_sem=send,
        recv_sem=recv,
        device_id={axis: peer},
        device_id_type=MESH,
    )


def greet(barrier, axis, peer):
    pl.semaphore_signal(barrier, inc=1, device_id={axis: peer}, device_id_type=MESH)


def row(ref):
    return ref[...].reshape(1, -1)


def column(ref):
    value = jnp.broadcast_to(row(ref), (8, ref.shape[0]))
    return value.T[:, :1]


def convolve_chunk(plane, shifted, weight, chunk, width):
    blocks, size, depth = plane.shape
    tokens = blocks * size
    edge = jnp.zeros((width, depth), BF16)
    place = lax.broadcasted_iota(jnp.int32, (size, depth), 0) % width
    for offset in range(3):
        shifted[offset, :width, :] = edge
        shifted[offset, tokens + width :, :] = edge
    for block in range(blocks):
        rows = slice(width + block * size, width + (block + 1) * size)
        value = plane[block]
        wide = value.astype(F32)
        before = jnp.where(place == 0, 0.0, pltpu.roll(wide, 1, 0))
        after = jnp.where(place == width - 1, 0.0, pltpu.roll(wide, size - 1, 0))
        shifted[0, rows, :] = before.astype(BF16)
        shifted[1, rows, :] = value
        shifted[2, rows, :] = after.astype(BF16)
    total = None
    for row_off in range(3):
        for col_off in range(3):
            window = shifted[col_off, row_off * width : row_off * width + tokens, :]
            part = lax.dot_general(
                weight[row_off, col_off, :, chunk * depth : (chunk + 1) * depth],
                window,
                (((1,), (1,)), ((), ())),
                preferred_element_type=F32,
            )
            total = part if total is None else total + part
    return total


def group_norm_silu(spatial, gain, shift, groups):
    channels, tokens = spatial.shape

    def group_mean(value):
        return jnp.mean(value, axis=(1, 2), keepdims=True)

    grouped = spatial.reshape(groups, channels // groups, tokens)
    centred = grouped - group_mean(grouped)
    scale = 1.0 / jnp.sqrt(group_mean(centred * centred) + 1e-05)
    value = (centred * scale).reshape(channels, tokens) * gain + shift
    return value / (1.0 + jnp.exp(-value))


def block_kernel(
    frames,
    width_cells,
    groups,
    latents_hbm,
    spatial_hbm,
    bias_hbm,
    gain_hbm,
    shift_hbm,
    temporal_hbm,
    temporal_bias_hbm,
    token_gain_hbm,
    query_hbm,
    key_hbm,
    value_hbm,
    output_hbm,
    out_ref,
    chunks,
    latents,
    spatial_bias,
    norm_gain,
    norm_shift,
    temporal_bias,
    token_gain,
    spatial_w,
    temporal_w,
    project_w,
    output_w,
    plane,
    shifted,
    act,
    act_rest,
    halo,
    halo_rest,
    terms,
    hidden,
    normed_all,
    outgoing,
    got,
    values,
    probs,
    done,
    back,
    att,
    sent,
    got_near,
    got_far,
    got_own,
    partial,
    final,
    load_sem,
    tap_sem,
    ready,
    lat_send,
    lat_recv,
    halo_send,
    halo_recv,
    gat_send,
    gat_recv,
    in_send,
    in_recv,
    out_send,
    out_recv,
    sum_send,
    sum_recv,
    lend_send,
    lend_recv,
):
    me = lax.axis_index("rows")
    frame = lax.axis_index("frames")
    near, far = me ^ 1, me ^ 2
    has_prev, has_next = frame > 0, frame < frames - 1
    prev = jnp.maximum(frame - 1, 0)
    later = jnp.minimum(frame + 1, frames - 1)
    barrier = pltpu.get_barrier_semaphore()
    greet(barrier, "rows", far)

    @pl.when(has_next)
    def _():
        greet(barrier, "frames", later)

    @pl.when(has_prev)
    def _():
        greet(barrier, "frames", prev)

    greet(barrier, "rows", near)
    count, size, depth = chunks.shape
    main, rest = act.shape[1], act_rest.shape[1]
    loads, pieces = [], []
    for index in range(count):
        load = pltpu.make_async_copy(
            latents_hbm.at[:, index * depth : (index + 1) * depth],
            chunks.at[index],
            load_sem.at[index],
        )
        load.start()
        pieces.append(load)
    for index, (src, dst) in enumerate(
        (
            (bias_hbm, spatial_bias),
            (spatial_hbm, spatial_w),
            (gain_hbm, norm_gain),
            (shift_hbm, norm_shift),
            (latents_hbm, latents),
            (temporal_bias_hbm, temporal_bias),
            (token_gain_hbm, token_gain),
            (key_hbm, project_w.at[0]),
            (query_hbm, project_w.at[1]),
            (value_hbm, project_w.at[2]),
            (output_hbm, output_w.at[me // 2]),
        )
    ):
        load = pltpu.make_async_copy(src, dst, load_sem.at[count + index])
        load.start()
        loads.append(load)
        if index == 3:
            taps = []
            for tap in range(3):
                for start, stop, place in (
                    (0, main, tap * main),
                    (main, main + rest, 3 * main + tap * rest),
                ):
                    load = pltpu.make_async_copy(
                        temporal_hbm.at[tap, start:stop],
                        temporal_w.at[place : place + stop - start],
                        tap_sem.at[len(taps)],
                    )
                    load.start()
                    taps.append(load)
    for load in pieces:
        load.wait()
    pl.semaphore_wait(
        barrier, 2 + has_prev.astype(jnp.int32) + has_next.astype(jnp.int32)
    )

    across, onward = [], []
    for index in range(count):
        across.append(
            remote(
                chunks.at[index],
                plane.at[index, me],
                lat_send.at[0, index],
                lat_recv.at[0, index],
                "rows",
                far,
            )
        )
        onward.append(
            remote(
                plane.at[index, far],
                plane.at[index, far],
                lat_send.at[1, index],
                lat_recv.at[1, index],
                "rows",
                near,
            )
        )
        across[index].start()
    beside = remote(
        chunks, plane.at[:, me], lat_send.at[2, 0], lat_recv.at[2, 0], "rows", near
    )
    beside.start()
    for index in range(count):
        plane[index, me] = chunks[index]
    for load in loads[:2]:
        load.wait()
    beside.wait_recv()
    spatial = column(spatial_bias)
    for index in range(count):
        across[index].wait_recv()
        onward[index].start()
    here = me // 2
    depth_out = output_w.shape[1]
    early = depth_out * 4 // 16 // 16 * 16
    loads[10].wait()
    lent = []
    for index, rows in enumerate((pl.ds(0, early), pl.ds(early, depth_out - early))):
        lent.append(
            remote(
                output_w.at[here, rows],
                output_w.at[here, rows],
                lend_send.at[index],
                lend_recv.at[index],
                "rows",
                far,
            )
        )
    lent[0].start()
    for index in range(count):
        onward[index].wait_recv()
    for index in range(count):
        spatial = spatial + convolve_chunk(
            plane.at[index], shifted.at[index], spatial_w, index, width_cells
        )
    for load in loads[2:4]:
        load.wait()
    value = group_norm_silu(spatial, column(norm_gain), column(norm_shift), groups)
    half = act_rest.shape[2]
    act[...] = value[:main].T.astype(BF16)
    for pair in range(2):
        act_rest[pair] = value[main:, pair * half : (pair + 1) * half].astype(BF16)
    for copy in across + onward + [beside]:
        copy.wait_send()


    up, down = [], []
    for turn, pair in enumerate((1 - here, here)):
        rows = pl.ds(pl.multiple_of(pair * half, half), half)
        for side, (copies, peer) in enumerate(((up, later), (down, prev))):
            for index, (src, dst) in enumerate(
                ((act.at[rows], halo.at[side, rows]), (act_rest.at[pair], halo_rest.at[side, pair]))
            ):
                copies.append(
                    remote(
                        src,
                        dst,
                        halo_send.at[side, 2 * turn + index],
                        halo_recv.at[side, 2 * turn + index],
                        "frames",
                        peer,
                    )
                )

    sides = ((has_next, up), (has_prev, down))

    def launch(turn):
        for exists, copies in sides:

            @pl.when(exists)
            def _(part=copies[2 * turn : 2 * turn + 2]):
                for copy in part:
                    copy.start()

    def settle(turn):
        for exists, copies in sides:

            @pl.when(exists)
            def _(part=copies[2 * turn : 2 * turn + 2]):
                for copy in part:
                    copy.wait_send()

    launch(0)

    @pl.when(jnp.logical_not(has_prev))
    def _():
        halo[0] = jnp.zeros(halo.shape[1:], halo.dtype)
        halo_rest[0] = jnp.zeros(halo_rest.shape[1:], halo.dtype)

    @pl.when(jnp.logical_not(has_next))
    def _():
        halo[1] = jnp.zeros(halo.shape[1:], halo.dtype)
        halo_rest[1] = jnp.zeros(halo_rest.shape[1:], halo.dtype)

    settle(0)
    launch(1)
    for load in taps:
        load.wait()

    def temporal_term(pair, turn):
        rows = pl.ds(pl.multiple_of(pair * half, half), half)

        @pl.when(has_prev)
        def _():
            for copy in up[2 * turn : 2 * turn + 2]:
                copy.wait_recv()

        @pl.when(has_next)
        def _():
            for copy in down[2 * turn : 2 * turn + 2]:
                copy.wait_recv()

        left = jnp.concatenate([halo_rest[0, pair], act_rest[pair], halo_rest[1, pair]], axis=0)
        window = jnp.concatenate(
            [halo[0, rows, :], act[rows, :], halo[1, rows, :], left.astype(F32).T.astype(BF16)],
            axis=1,
        )
        return jnp.dot(window, temporal_w[...], preferred_element_type=F32)

    core = lax.rem(me, 2)
    step = size // PARTS
    spans = [slice(part * step, (part + 1) * step) for part in range(PARTS)]

    def share(slot, owner, part):
        start = pl.multiple_of(owner * size + part * step, step)
        return terms[slot, pl.ds(start, step), :]

    def hand(slot, pair):
        terms[slot] = temporal_term(pair, slot)
        for part, span in enumerate(spans):
            sent[slot, span, :] = share(slot, 1 - core, part).astype(BF16)
        copy = remote(
            sent.at[slot], got_near.at[slot], sum_send.at[slot], sum_recv.at[slot], "rows", near
        )
        copy.start()
        return copy

    first = hand(0, 1 - here)
    first.wait_recv()
    over = []
    for part, span in enumerate(spans):
        value = share(0, core, part) + got_near[0, span, :].astype(F32)
        partial[0, span, :] = value
        sent[2, span, :] = value.astype(BF16)
        copy = remote(
            sent.at[2, span],
            got_far.at[span],
            sum_send.at[2 + part],
            sum_recv.at[2 + part],
            "rows",
            far,
        )
        copy.start()
        over.append(copy)
    second = hand(1, here)
    second.wait_recv()
    for part, span in enumerate(spans):
        value = share(1, core, part) + got_near[1, span, :].astype(F32)
        partial[1, span, :] = value
        sent[3, span, :] = value.astype(BF16)
        copy = remote(
            sent.at[3, span],
            got_own.at[span],
            sum_send.at[2 + PARTS + part],
            sum_recv.at[2 + PARTS + part],
            "rows",
            far,
        )
        copy.start()
        over.append(copy)
    lent[1].start()
    for load in loads[4:7]:
        load.wait()

    @pl.when(jnp.logical_and(has_prev, frame == frames - 3))
    def _():
        pl.semaphore_signal(ready, inc=1, device_id={"frames": prev}, device_id_type=MESH)

    @pl.when(jnp.logical_and(has_next, frame == 2))
    def _():
        pl.semaphore_signal(ready, inc=1, device_id={"frames": later}, device_id_type=MESH)

    settle(1)
    tokens = act.shape[0]
    moves = []

    def project(pair, start, length, slot):
        slab = normed_all[pl.ds(2 * pair, 2), start : start + length, :]
        slab = slab.reshape(2 * length, slab.shape[2])
        span = pl.ds(start, length)
        for kind in range(3):
            cols = jnp.dot(slab, project_w[kind], preferred_element_type=F32)
            for owner in range(frames):
                head = cols[:, owner * HD : (owner + 1) * HD]
                outgoing[pair, owner, kind, span, :] = jnp.concatenate(
                    [head[:length], head[length:]], axis=1
                ).astype(BF16)
        for turn in range(1, frames):
            peer = lax.rem(frame + turn, frames)
            copy = remote(
                outgoing.at[pair, peer, :, span],
                got.at[pair, frame, :, span],
                in_send.at[slot, turn],
                in_recv.at[slot, turn],
                "frames",
                peer,
            )
            copy.start()
            moves.append(copy)
        got[pair, frame, :, span, :] = outgoing[pair, frame, :, span, :]

    def normalise(slot, part, base, other):
        span = spans[part]
        total = partial[slot, span, :] + other[span, :].astype(F32) + row(temporal_bias)
        value = (base.astype(F32) + total).astype(BF16)
        flat = value.astype(F32)
        centred = flat - jnp.mean(flat, axis=-1, keepdims=True)
        var = jnp.mean(centred * centred, axis=-1, keepdims=True)
        return value, (centred / jnp.sqrt(var + 1e-05) * row(token_gain)).astype(BF16)

    gathers = []

    def give(block, slot, part, value):
        place = normed_all.at[block, spans[part]]
        normed_all[block, spans[part], :] = value
        copy = remote(
            place, place, gat_send.at[slot, part], gat_recv.at[slot, part], "rows", near
        )
        copy.start()
        gathers.append(copy)
        return copy

    def ready_part(index):
        slot, part = index // PARTS, index % PARTS
        span = spans[part]
        over[index].wait_recv()
        if slot == 0:
            hidden[span, :], value = normalise(1, part, latents[span, :], got_far)
            return give(me, 0, part, value)
        base = jnp.concatenate([plane[index, far, span, :] for index in range(count)], axis=1)
        _, value = normalise(0, part, base, got_own)
        return give(far, 1, part, value)

    pending = ready_part(0)
    for load in loads[7:10]:
        load.wait()

    @pl.when(jnp.logical_not(jnp.logical_and(has_prev, has_next)))
    def _():
        pl.semaphore_wait(ready, 1)

    for index in range(2 * PARTS):
        pending.wait_recv()
        project(here if index < PARTS else 1 - here, index % PARTS * step, step, index)
        if index + 1 < 2 * PARTS:
            pending = ready_part(index + 1)

    for copy in moves:
        copy.wait_recv()
    scale = 1.0 / math.sqrt(HD)
    keys = got[:, :, 0].reshape(-1, LANES)
    values[...] = got[:, :, 2].reshape(-1, LANES).astype(F32).T.astype(BF16)
    sums = []
    for turn in range(1, frames + 1):
        peer = lax.rem(frame + turn, frames)
        pieces = []
        for pair in range(2):
            flipped = got[pair, peer, 1].astype(F32).T
            pieces += [flipped[:HD], flipped[HD:]]
        query = (jnp.concatenate(pieces, axis=1) * scale).astype(BF16)
        zero = jnp.zeros_like(query)
        block = jnp.concatenate(
            [jnp.concatenate([query, zero], axis=1), jnp.concatenate([zero, query], axis=1)],
            axis=0,
        )
        scores = jnp.dot(keys, block, preferred_element_type=F32)
        peak = jnp.max(scores, axis=0, keepdims=True)
        peak = jnp.maximum(peak[:, :tokens], peak[:, tokens:])
        weights = jnp.exp(scores - jnp.concatenate([peak, peak], axis=1))
        total = jnp.sum(weights, axis=0, keepdims=True)
        sums.append(total[:, :tokens] + total[:, tokens:])
        probs[turn - 1] = weights.astype(BF16)
    returns = []

    def give_back(turn):
        peer = lax.rem(frame + turn, frames)
        for side, (pair, target) in enumerate(((1 - here, far), (here, me))):
            if side == 1 and turn == frames:
                continue
            copy = pltpu.make_async_remote_copy(
                src_ref=done.at[pair, peer],
                dst_ref=back.at[here, frame],
                send_sem=out_send.at[side, turn],
                recv_sem=out_recv.at[side, turn],
                device_id={"rows": target, "frames": peer},
                device_id_type=MESH,
            )
            copy.start()
            returns.append(copy)

    for turn in range(1, frames + 1):
        peer = lax.rem(frame + turn, frames)
        numerator = jnp.dot(
            values[:HD, :], probs[turn - 1, :, :tokens], preferred_element_type=F32
        ) + jnp.dot(values[HD:, :], probs[turn - 1, :, tokens:], preferred_element_type=F32)
        result = (numerator / sums[turn - 1]).astype(BF16)
        for pair in range(2):
            done[pair, peer] = result[:, pair * half : (pair + 1) * half]
        give_back(turn)
    back[here, frame] = done[here, frame]
    for copy in lent:
        copy.wait_recv()
    for copy in returns:
        copy.wait_recv()
    att[...] = back[...].reshape(-1, half).astype(F32).T.astype(BF16)
    mix = output_w[...].reshape(-1, output_w.shape[2])
    def mixed_term(owner):
        rows = pl.ds(pl.multiple_of(owner * size, size), size)
        return jnp.dot(att[rows, :], mix, preferred_element_type=F32)

    final[0] = mixed_term(1 - core).astype(BF16)
    swap = remote(
        final.at[0], final.at[1], sum_send.at[2 + 2 * PARTS], sum_recv.at[2 + 2 * PARTS], "rows", near
    )
    swap.start()
    mixed = mixed_term(core)
    swap.wait_recv()
    out_ref[...] = (hidden[...].astype(F32) + mixed + final[1].astype(F32)).astype(BF16)
    for copy in [first, second, swap] + over + gathers:
        copy.wait_send()
    for copy in lent + returns:
        copy.wait_send()
    for copy in moves:
        copy.wait_send()


def body_fast(
    latents,
    spatial_weight,
    spatial_bias,
    norm_gain,
    norm_shift,
    temporal_weight,
    temporal_bias,
    token_gain,
    query_weight,
    key_weight,
    value_weight,
    output_weight,
):
    channels = latents.shape[3]
    peers, frames = lax.axis_size("rows"), lax.axis_size("frames")
    block = latents.reshape(-1, channels)
    size = block.shape[0]
    tokens = size * peers
    width_cells = latents.shape[2]
    local_out = spatial_weight.shape[3]
    width = query_weight.shape[1] // frames
    main = local_out // LANES * LANES
    rest = local_out - main
    depth = CHUNK
    count = channels // depth
    denoised = pl.pallas_call(
        functools.partial(block_kernel, frames, width_cells, NORM_GROUPS // peers),
        out_shape=pltpu.VMEM(block.shape, BF16),
        in_specs=[ANY_SPEC] * 12,
        out_specs=VMEM_SPEC,
        scratch_shapes=[
            pltpu.VMEM((count, size, depth), BF16),
            pltpu.VMEM(block.shape, BF16),
            pltpu.VMEM(spatial_bias.shape, F32),
            pltpu.VMEM(norm_gain.shape, F32),
            pltpu.VMEM(norm_shift.shape, F32),
            pltpu.VMEM(temporal_bias.shape, F32),
            pltpu.VMEM(token_gain.shape, F32),
            pltpu.VMEM(spatial_weight.shape[:2] + (local_out, channels), BF16),
            pltpu.VMEM((3 * local_out, channels), BF16),
            pltpu.VMEM((3,) + query_weight.shape, BF16),
            pltpu.VMEM((2,) + output_weight.shape, BF16),
            pltpu.VMEM((count, peers, size, depth), BF16),
            pltpu.VMEM((count, 3, tokens + 2 * width_cells, depth), BF16),
            pltpu.VMEM((tokens, main), BF16),
            pltpu.VMEM((2, rest, tokens // 2), BF16),
            pltpu.VMEM((2, tokens, main), BF16),
            pltpu.VMEM((2, 2, rest, tokens // 2), BF16),
            pltpu.VMEM((2, tokens // 2, channels), F32),
            pltpu.VMEM(block.shape, BF16),
            pltpu.VMEM((peers,) + block.shape, BF16),
            pltpu.VMEM((2, frames, 3, size, LANES), BF16),
            pltpu.VMEM((2, frames, 3, size, LANES), BF16),
            pltpu.VMEM((LANES, 2 * frames * size), BF16),
            pltpu.VMEM((frames, 2 * frames * size, 2 * tokens), BF16),
            pltpu.VMEM((2, frames, width, tokens // 2), BF16),
            pltpu.VMEM((2, frames, width, tokens // 2), BF16),
            pltpu.VMEM((tokens // 2, 2 * frames * width), BF16),
            pltpu.VMEM((4,) + block.shape, BF16),
            pltpu.VMEM((2,) + block.shape, BF16),
            pltpu.VMEM(block.shape, BF16),
            pltpu.VMEM(block.shape, BF16),
            pltpu.VMEM((2,) + block.shape, F32),
            pltpu.VMEM((2,) + block.shape, BF16),
            DMA((11 + count,)),
            DMA((6,)),
            pltpu.SemaphoreType.REGULAR,
            DMA((3, count)),
            DMA((3, count)),
            DMA((2, peers)),
            DMA((2, peers)),
            DMA((2, PARTS)),
            DMA((2, PARTS)),
            DMA((2 * PARTS, frames)),
            DMA((2 * PARTS, frames)),
            DMA((2, frames + 1)),
            DMA((2, frames + 1)),
            DMA((3 + 2 * PARTS,)),
            DMA((3 + 2 * PARTS,)),
            DMA((2,)),
            DMA((2,)),
        ],
        compiler_params=pltpu.CompilerParams(
            collective_id=0, has_side_effects=True, vmem_limit_bytes=VMEM_LIMIT
        ),
    )(
        block,
        jnp.swapaxes(spatial_weight, 2, 3),
        spatial_bias,
        norm_gain,
        norm_shift,
        temporal_weight,
        temporal_bias,
        token_gain,
        query_weight,
        key_weight,
        value_weight,
        output_weight,
    )
    return denoised.reshape(latents.shape)


def fits(mesh):
    def choose(*args):
        latents, query_weight = args[0], args[8]
        peers, frames = mesh.shape["rows"], mesh.shape["frames"]
        heads = query_weight.shape[1] // HD
        tokens = latents.shape[0] * latents.shape[1] * latents.shape[2] * peers
        fast = (
            peers == 4
            and mesh.shape["frames"] == 4
            and latents.shape[3] % CHUNK == 0
            and args[1].shape[3] > LANES
            and args[1].shape[3] % LANES >= 16
            and args[1].shape[3] % 16 == 0
            and args[1].shape[3] % (8 * (NORM_GROUPS // peers)) == 0
            and latents.shape[1] == 1
            and heads == frames
            and 2 * HD == LANES
            and tokens % 256 == 0
            and latents.shape[2] % 16 == 0
            and latents.shape[0] * latents.shape[2] % (16 * PARTS) == 0
        )
        return (body_fast if fast else body)(*args)

    return choose


def solution(mesh):
    in_specs = (
        P("rows", ("groups", "frames"), None, None),
        P(None, None, None, "rows"),
        P("rows"),
        P("rows"),
        P("rows"),
        P(None, "rows", None),
        P(),
        P(),
        P(None, "rows"),
        P(None, "rows"),
        P(None, "rows"),
        P("rows", None),
    )
    out_specs = P("rows", ("groups", "frames"), None, None)
    return jax.shard_map(
        fits(mesh), mesh=mesh, in_specs=in_specs, out_specs=out_specs, check_vma=False
    )
```

```python
import functools
import math

import jax
import jax.numpy as jnp
from jax import lax
from jax.experimental import pallas as pl
from jax.experimental.pallas import tpu as pltpu
from jax.sharding import PartitionSpec as P

HD = 64
NORM_GROUPS = 32


def padded_2(array, sides, width):
    for axis, dim in sides:
        peers, length = (lax.axis_size(axis), array.shape[dim])
        up = [(i, (i + 1) % peers) for i in range(peers - 1)]
        down = [(j, i) for i, j in up]
        last = lax.slice_in_dim(array, length - width, length, axis=dim)
        leading = lax.slice_in_dim(array, 0, width, axis=dim)
        before = lax.ppermute(last, axis, up)
        after = lax.ppermute(leading, axis, down)
        array = jnp.concatenate([before, array, after], axis=dim)
    return array


def shifted_2(value, axis, steps):
    count = lax.axis_size(axis)
    pairs = [(source, (source + steps) % count) for source in range(count)]
    return lax.ppermute(value, axis, pairs)


def conv_plane(field, weight, bias):
    rows_n, frames_n, cols_n, chans = field.shape
    padded = jnp.pad(field, ((1, 1), (0, 0), (1, 1), (0, 0)))
    total = jnp.zeros((rows_n * frames_n * cols_n, weight.shape[3]), jnp.float32)
    for row_off in range(3):
        for col_off in range(3):
            window = padded[row_off : row_off + rows_n, :, col_off : col_off + cols_n, :].reshape(
                -1, chans
            )
            total = total + jnp.dot(
                window, weight[row_off, col_off], preferred_element_type=jnp.float32
            )
    return total.reshape(rows_n, frames_n, cols_n, -1) + bias


def layer_norm(field, token_gain):
    flat = field.astype(jnp.float32)
    token_mean = jnp.mean(flat, axis=-1, keepdims=True)
    shifted = flat - token_mean
    token_var = jnp.mean(shifted * shifted, axis=-1, keepdims=True)
    return (shifted / jnp.sqrt(token_var + 1e-05) * token_gain).astype(jnp.bfloat16)


def attend(queries, carried, keys, values):
    block = queries.shape[0]
    head_count = queries.shape[1]
    block_count = keys.shape[0] // block
    key_blocks = keys.reshape(block_count, block, head_count, HD)
    value_blocks = values.reshape(block_count, block, head_count, HD)
    scale = 1.0 / math.sqrt(HD)

    def visit_block(state, block_pair):
        running_max, denominator, numerator = state
        key_block, value_block = block_pair
        scores = (
            jnp.einsum("qhd,khd->qhk", queries, key_block, preferred_element_type=jnp.float32)
            * scale
        )
        new_max = jnp.maximum(running_max, jnp.max(scores, axis=-1))
        shrink = jnp.exp(running_max - new_max)
        weights = jnp.exp(scores - new_max[..., None])
        denominator = denominator * shrink + jnp.sum(weights, axis=-1)
        numerator = numerator * shrink[..., None] + jnp.einsum(
            "qhk,khd->qhd",
            weights.astype(jnp.bfloat16),
            value_block,
            preferred_element_type=jnp.float32,
        )
        return ((new_max, denominator, numerator), None)

    result, _ = lax.scan(visit_block, carried, (key_blocks, value_blocks))
    return result


def body(
    latents,
    spatial_weight,
    spatial_bias,
    norm_gain,
    norm_shift,
    temporal_weight,
    temporal_bias,
    token_gain,
    query_weight,
    key_weight,
    value_weight,
    output_weight,
):
    row_count, frame_count, width_cells, channels = latents.shape
    plane = lax.all_gather(latents, "rows", axis=0, tiled=True)
    plane_rows = plane.shape[0]
    local_out = spatial_weight.shape[3]
    spatial = conv_plane(plane, spatial_weight, spatial_bias)
    local_groups = NORM_GROUPS // lax.axis_size("rows")
    grouped = spatial.reshape(plane_rows, frame_count, width_cells, local_groups, -1)
    group_mean = jnp.mean(grouped, axis=(0, 2, 4), keepdims=True)
    centred = grouped - group_mean
    group_var = jnp.mean(centred * centred, axis=(0, 2, 4), keepdims=True)
    scaled = (centred / jnp.sqrt(group_var + 1e-05)).reshape(
        plane_rows, frame_count, width_cells, local_out
    ) * norm_gain + norm_shift
    activated = jax.nn.silu(scaled).astype(jnp.bfloat16)
    rim = padded_2(activated, (("frames", 1),), 1)
    row_total = row_count * lax.axis_size("rows")
    row_piece = rim
    total = jnp.zeros((row_total * frame_count * width_cells, channels), jnp.float32)
    for lag_index in range(3):
        window = row_piece[:, lag_index : lag_index + frame_count].reshape(-1, local_out)
        total = total + jnp.dot(
            window, temporal_weight[lag_index], preferred_element_type=jnp.float32
        )
    temporal = lax.psum_scatter(
        total.reshape(row_total, frame_count, width_cells, channels).astype(jnp.bfloat16),
        "rows",
        scatter_dimension=0,
        tiled=True,
    ).astype(jnp.float32)
    hidden = (latents.astype(jnp.float32) + temporal + temporal_bias).astype(jnp.bfloat16)
    normed_all = lax.all_gather(layer_norm(hidden, token_gain), "rows", axis=0, tiled=True)
    flat = normed_all.reshape(-1, channels)
    head_cols = query_weight.shape[1]
    head_count = head_cols // HD
    token_count = flat.shape[0]
    queries = jnp.dot(flat, query_weight, preferred_element_type=jnp.float32).astype(jnp.bfloat16)
    keys = jnp.dot(flat, key_weight, preferred_element_type=jnp.float32).astype(jnp.bfloat16)
    values = jnp.dot(flat, value_weight, preferred_element_type=jnp.float32).astype(jnp.bfloat16)
    start_state = (
        jnp.full((token_count, head_count), -1e30, jnp.float32),
        jnp.zeros((token_count, head_count), jnp.float32),
        jnp.zeros((token_count, head_count, HD), jnp.float32),
    )
    local_keys = keys.reshape(token_count, head_count, HD)
    local_values = values.reshape(token_count, head_count, HD)

    def travel(turn, state):
        query_moving, running_max, denominator, numerator = state
        running_max, denominator, numerator = attend(
            query_moving, (running_max, denominator, numerator), local_keys, local_values
        )
        return (
            shifted_2(query_moving, "frames", 1),
            shifted_2(running_max.astype(jnp.bfloat16), "frames", 1).astype(running_max.dtype),
            shifted_2(denominator.astype(jnp.bfloat16), "frames", 1).astype(denominator.dtype),
            shifted_2(numerator.astype(jnp.bfloat16), "frames", 1).astype(numerator.dtype),
        )

    start_moving = queries.reshape(token_count, head_count, HD)
    final = lax.fori_loop(0, lax.axis_size("frames"), travel, (start_moving,) + start_state)
    denominator, numerator = (final[2], final[3])
    attended = (
        (numerator / denominator[..., None])
        .astype(jnp.bfloat16)
        .reshape(plane_rows, frame_count, width_cells, head_cols)
    )
    row_piece = attended
    mixed = lax.psum_scatter(
        jnp.dot(row_piece.reshape(-1, head_cols), output_weight, preferred_element_type=jnp.float32)
        .reshape(row_count * lax.axis_size("rows"), frame_count, width_cells, channels)
        .astype(jnp.bfloat16),
        "rows",
        scatter_dimension=0,
        tiled=True,
    ).astype(jnp.float32)
    return (hidden.astype(jnp.float32) + mixed).astype(jnp.bfloat16)


MESH = pl.DeviceIdType.MESH
DMA = pltpu.SemaphoreType.DMA
VMEM_SPEC = pl.BlockSpec(memory_space=pltpu.VMEM)
ANY_SPEC = pl.BlockSpec(memory_space=pl.ANY)
BF16 = jnp.bfloat16
F32 = jnp.float32
VMEM_LIMIT = 54 << 20
PARTS = 2
CHUNK = 256
LANES = 128


def remote(src, dst, send, recv, axis, peer):
    return pltpu.make_async_remote_copy(
        src_ref=src,
        dst_ref=dst,
        send_sem=send,
        recv_sem=recv,
        device_id={axis: peer},
        device_id_type=MESH,
    )


def greet(barrier, axis, peer):
    pl.semaphore_signal(barrier, inc=1, device_id={axis: peer}, device_id_type=MESH)


def row(ref):
    return ref[...].reshape(1, -1)


def column(ref):
    value = jnp.broadcast_to(row(ref), (8, ref.shape[0]))
    return value.T[:, :1]


def convolve_chunk(plane, shifted, weight, chunk, width):
    blocks, size, depth = plane.shape
    tokens = blocks * size
    edge = jnp.zeros((width, depth), BF16)
    place = lax.broadcasted_iota(jnp.int32, (size, depth), 0) % width
    for offset in range(3):
        shifted[offset, :width, :] = edge
        shifted[offset, tokens + width :, :] = edge
    for block in range(blocks):
        rows = slice(width + block * size, width + (block + 1) * size)
        value = plane[block]
        wide = value.astype(F32)
        before = jnp.where(place == 0, 0.0, pltpu.roll(wide, 1, 0))
        after = jnp.where(place == width - 1, 0.0, pltpu.roll(wide, size - 1, 0))
        shifted[0, rows, :] = before.astype(BF16)
        shifted[1, rows, :] = value
        shifted[2, rows, :] = after.astype(BF16)
    total = None
    for row_off in range(3):
        for col_off in range(3):
            window = shifted[col_off, row_off * width : row_off * width + tokens, :]
            part = lax.dot_general(
                weight[row_off, col_off, :, chunk * depth : (chunk + 1) * depth],
                window,
                (((1,), (1,)), ((), ())),
                preferred_element_type=F32,
            )
            total = part if total is None else total + part
    return total


def group_norm_silu(spatial, gain, shift, groups):
    channels, tokens = spatial.shape

    def group_mean(value):
        return jnp.mean(value, axis=(1, 2), keepdims=True)

    grouped = spatial.reshape(groups, channels // groups, tokens)
    centred = grouped - group_mean(grouped)
    scale = 1.0 / jnp.sqrt(group_mean(centred * centred) + 1e-05)
    value = (centred * scale).reshape(channels, tokens) * gain + shift
    return value / (1.0 + jnp.exp(-value))


def block_kernel(
    frames,
    width_cells,
    groups,
    latents_hbm,
    spatial_hbm,
    bias_hbm,
    gain_hbm,
    shift_hbm,
    temporal_hbm,
    temporal_bias_hbm,
    token_gain_hbm,
    query_hbm,
    key_hbm,
    value_hbm,
    output_hbm,
    out_ref,
    chunks,
    latents,
    spatial_bias,
    norm_gain,
    norm_shift,
    temporal_bias,
    token_gain,
    spatial_w,
    temporal_w,
    project_w,
    output_w,
    plane,
    shifted,
    act,
    act_rest,
    halo,
    halo_rest,
    terms,
    hidden,
    normed_all,
    outgoing,
    got,
    values,
    probs,
    done,
    back,
    att,
    sent,
    got_near,
    got_far,
    got_own,
    partial,
    final,
    load_sem,
    tap_sem,
    ready,
    lat_send,
    lat_recv,
    halo_send,
    halo_recv,
    gat_send,
    gat_recv,
    in_send,
    in_recv,
    out_send,
    out_recv,
    sum_send,
    sum_recv,
    lend_send,
    lend_recv,
):
    me = lax.axis_index("rows")
    frame = lax.axis_index("frames")
    near, far = me ^ 1, me ^ 2
    has_prev, has_next = frame > 0, frame < frames - 1
    prev = jnp.maximum(frame - 1, 0)
    later = jnp.minimum(frame + 1, frames - 1)
    barrier = pltpu.get_barrier_semaphore()
    greet(barrier, "rows", far)

    @pl.when(has_next)
    def _():
        greet(barrier, "frames", later)

    @pl.when(has_prev)
    def _():
        greet(barrier, "frames", prev)

    greet(barrier, "rows", near)
    count, size, depth = chunks.shape
    main, rest = act.shape[1], act_rest.shape[1]
    loads, pieces = [], []
    for index in range(count):
        load = pltpu.make_async_copy(
            latents_hbm.at[:, index * depth : (index + 1) * depth],
            chunks.at[index],
            load_sem.at[index],
        )
        load.start()
        pieces.append(load)
    for index, (src, dst) in enumerate(
        (
            (bias_hbm, spatial_bias),
            (spatial_hbm, spatial_w),
            (gain_hbm, norm_gain),
            (shift_hbm, norm_shift),
            (latents_hbm, latents),
            (temporal_bias_hbm, temporal_bias),
            (token_gain_hbm, token_gain),
            (key_hbm, project_w.at[0]),
            (query_hbm, project_w.at[1]),
            (value_hbm, project_w.at[2]),
            (output_hbm, output_w.at[me // 2]),
        )
    ):
        load = pltpu.make_async_copy(src, dst, load_sem.at[count + index])
        load.start()
        loads.append(load)
        if index == 3:
            taps = []
            for tap in range(3):
                for start, stop, place in (
                    (0, main, tap * main),
                    (main, main + rest, 3 * main + tap * rest),
                ):
                    load = pltpu.make_async_copy(
                        temporal_hbm.at[tap, start:stop],
                        temporal_w.at[place : place + stop - start],
                        tap_sem.at[len(taps)],
                    )
                    load.start()
                    taps.append(load)
    for load in pieces:
        load.wait()
    pl.semaphore_wait(
        barrier, 2 + has_prev.astype(jnp.int32) + has_next.astype(jnp.int32)
    )

    across, onward = [], []
    for index in range(count):
        across.append(
            remote(
                chunks.at[index],
                plane.at[index, me],
                lat_send.at[0, index],
                lat_recv.at[0, index],
                "rows",
                far,
            )
        )
        onward.append(
            remote(
                plane.at[index, far],
                plane.at[index, far],
                lat_send.at[1, index],
                lat_recv.at[1, index],
                "rows",
                near,
            )
        )
        across[index].start()
    beside = remote(
        chunks, plane.at[:, me], lat_send.at[2, 0], lat_recv.at[2, 0], "rows", near
    )
    beside.start()
    for index in range(count):
        plane[index, me] = chunks[index]
    for load in loads[:2]:
        load.wait()
    beside.wait_recv()
    spatial = column(spatial_bias)
    for index in range(count):
        across[index].wait_recv()
        onward[index].start()
    here = me // 2
    depth_out = output_w.shape[1]
    early = depth_out * 4 // 16 // 16 * 16
    loads[10].wait()
    lent = []
    for index, rows in enumerate((pl.ds(0, early), pl.ds(early, depth_out - early))):
        lent.append(
            remote(
                output_w.at[here, rows],
                output_w.at[here, rows],
                lend_send.at[index],
                lend_recv.at[index],
                "rows",
                far,
            )
        )
    lent[0].start()
    for index in range(count):
        onward[index].wait_recv()
    for index in range(count):
        spatial = spatial + convolve_chunk(
            plane.at[index], shifted.at[index], spatial_w, index, width_cells
        )
    for load in loads[2:4]:
        load.wait()
    value = group_norm_silu(spatial, column(norm_gain), column(norm_shift), groups)
    half = act_rest.shape[2]
    act[...] = value[:main].T.astype(BF16)
    for pair in range(2):
        act_rest[pair] = value[main:, pair * half : (pair + 1) * half].astype(BF16)
    for copy in across + onward + [beside]:
        copy.wait_send()


    up, down = [], []
    for turn, pair in enumerate((1 - here, here)):
        rows = pl.ds(pl.multiple_of(pair * half, half), half)
        for side, (copies, peer) in enumerate(((up, later), (down, prev))):
            for index, (src, dst) in enumerate(
                ((act.at[rows], halo.at[side, rows]), (act_rest.at[pair], halo_rest.at[side, pair]))
            ):
                copies.append(
                    remote(
                        src,
                        dst,
                        halo_send.at[side, 2 * turn + index],
                        halo_recv.at[side, 2 * turn + index],
                        "frames",
                        peer,
                    )
                )

    sides = ((has_next, up), (has_prev, down))

    def launch(turn):
        for exists, copies in sides:

            @pl.when(exists)
            def _(part=copies[2 * turn : 2 * turn + 2]):
                for copy in part:
                    copy.start()

    def settle(turn):
        for exists, copies in sides:

            @pl.when(exists)
            def _(part=copies[2 * turn : 2 * turn + 2]):
                for copy in part:
                    copy.wait_send()

    launch(0)

    @pl.when(jnp.logical_not(has_prev))
    def _():
        halo[0] = jnp.zeros(halo.shape[1:], halo.dtype)
        halo_rest[0] = jnp.zeros(halo_rest.shape[1:], halo.dtype)

    @pl.when(jnp.logical_not(has_next))
    def _():
        halo[1] = jnp.zeros(halo.shape[1:], halo.dtype)
        halo_rest[1] = jnp.zeros(halo_rest.shape[1:], halo.dtype)

    settle(0)
    launch(1)
    for load in taps:
        load.wait()

    def temporal_term(pair, turn):
        rows = pl.ds(pl.multiple_of(pair * half, half), half)

        @pl.when(has_prev)
        def _():
            for copy in up[2 * turn : 2 * turn + 2]:
                copy.wait_recv()

        @pl.when(has_next)
        def _():
            for copy in down[2 * turn : 2 * turn + 2]:
                copy.wait_recv()

        left = jnp.concatenate([halo_rest[0, pair], act_rest[pair], halo_rest[1, pair]], axis=0)
        window = jnp.concatenate(
            [halo[0, rows, :], act[rows, :], halo[1, rows, :], left.astype(F32).T.astype(BF16)],
            axis=1,
        )
        return jnp.dot(window, temporal_w[...], preferred_element_type=F32)

    core = lax.rem(me, 2)
    step = size // PARTS
    spans = [slice(part * step, (part + 1) * step) for part in range(PARTS)]

    def share(slot, owner, part):
        start = pl.multiple_of(owner * size + part * step, step)
        return terms[slot, pl.ds(start, step), :]

    def hand(slot, pair):
        terms[slot] = temporal_term(pair, slot)
        for part, span in enumerate(spans):
            sent[slot, span, :] = share(slot, 1 - core, part).astype(BF16)
        copy = remote(
            sent.at[slot], got_near.at[slot], sum_send.at[slot], sum_recv.at[slot], "rows", near
        )
        copy.start()
        return copy

    first = hand(0, 1 - here)
    first.wait_recv()
    over = []
    for part, span in enumerate(spans):
        value = share(0, core, part) + got_near[0, span, :].astype(F32)
        partial[0, span, :] = value
        sent[2, span, :] = value.astype(BF16)
        copy = remote(
            sent.at[2, span],
            got_far.at[span],
            sum_send.at[2 + part],
            sum_recv.at[2 + part],
            "rows",
            far,
        )
        copy.start()
        over.append(copy)
    second = hand(1, here)
    second.wait_recv()
    for part, span in enumerate(spans):
        value = share(1, core, part) + got_near[1, span, :].astype(F32)
        partial[1, span, :] = value
        sent[3, span, :] = value.astype(BF16)
        copy = remote(
            sent.at[3, span],
            got_own.at[span],
            sum_send.at[2 + PARTS + part],
            sum_recv.at[2 + PARTS + part],
            "rows",
            far,
        )
        copy.start()
        over.append(copy)
    for load in loads[4:7]:
        load.wait()

    @pl.when(jnp.logical_and(has_prev, frame == frames - 3))
    def _():
        pl.semaphore_signal(ready, inc=1, device_id={"frames": prev}, device_id_type=MESH)

    @pl.when(jnp.logical_and(has_next, frame == 2))
    def _():
        pl.semaphore_signal(ready, inc=1, device_id={"frames": later}, device_id_type=MESH)

    settle(1)
    tokens = act.shape[0]
    moves = []
    order = sorted(range(1, frames), key=lambda turn: abs(2 * turn - frames))

    def project(pair, start, length, slot):
        slab = normed_all[pl.ds(2 * pair, 2), start : start + length, :]
        slab = slab.reshape(2 * length, slab.shape[2])
        span = pl.ds(start, length)
        for kind in range(3):
            cols = jnp.dot(slab, project_w[kind], preferred_element_type=F32)
            for owner in range(frames):
                head = cols[:, owner * HD : (owner + 1) * HD]
                outgoing[pair, owner, kind, span, :] = jnp.concatenate(
                    [head[:length], head[length:]], axis=1
                ).astype(BF16)
        for turn in order:
            peer = lax.rem(frame + turn, frames)
            copy = remote(
                outgoing.at[pair, peer, :, span],
                got.at[pair, frame, :, span],
                in_send.at[slot, turn],
                in_recv.at[slot, turn],
                "frames",
                peer,
            )
            copy.start()
            moves.append(copy)
        got[pair, frame, :, span, :] = outgoing[pair, frame, :, span, :]

    def normalise(slot, part, base, other):
        span = spans[part]
        total = partial[slot, span, :] + other[span, :].astype(F32) + row(temporal_bias)
        value = (base.astype(F32) + total).astype(BF16)
        flat = value.astype(F32)
        centred = flat - jnp.mean(flat, axis=-1, keepdims=True)
        var = jnp.mean(centred * centred, axis=-1, keepdims=True)
        return value, (centred / jnp.sqrt(var + 1e-05) * row(token_gain)).astype(BF16)

    gathers = []

    def give(block, slot, part, value):
        place = normed_all.at[block, spans[part]]
        normed_all[block, spans[part], :] = value
        copy = remote(
            place, place, gat_send.at[slot, part], gat_recv.at[slot, part], "rows", near
        )
        copy.start()
        gathers.append(copy)
        return copy

    def ready_part(index):
        slot, part = index // PARTS, index % PARTS
        span = spans[part]
        over[index].wait_recv()
        if slot == 0:
            hidden[span, :], value = normalise(1, part, latents[span, :], got_far)
            return give(me, 0, part, value)
        base = jnp.concatenate([plane[index, far, span, :] for index in range(count)], axis=1)
        _, value = normalise(0, part, base, got_own)
        return give(far, 1, part, value)

    pending = ready_part(0)
    for load in loads[7:10]:
        load.wait()

    @pl.when(jnp.logical_not(jnp.logical_and(has_prev, has_next)))
    def _():
        pl.semaphore_wait(ready, 1)

    for index in range(2 * PARTS):
        pending.wait_recv()
        project(here if index < PARTS else 1 - here, index % PARTS * step, step, index)
        if index == 1:
            lent[1].start()
        if index + 1 < 2 * PARTS:
            pending = ready_part(index + 1)

    for copy in moves:
        copy.wait_recv()
    scale = 1.0 / math.sqrt(HD)
    keys = got[:, :, 0].reshape(-1, LANES)
    values[...] = got[:, :, 2].reshape(-1, LANES).astype(F32).T.astype(BF16)
    sums = []
    for turn in range(1, frames + 1):
        peer = lax.rem(frame + turn, frames)
        pieces = []
        for pair in range(2):
            flipped = got[pair, peer, 1].astype(F32).T
            pieces += [flipped[:HD], flipped[HD:]]
        query = (jnp.concatenate(pieces, axis=1) * scale).astype(BF16)
        zero = jnp.zeros_like(query)
        block = jnp.concatenate(
            [jnp.concatenate([query, zero], axis=1), jnp.concatenate([zero, query], axis=1)],
            axis=0,
        )
        scores = jnp.dot(keys, block, preferred_element_type=F32)
        peak = jnp.max(scores, axis=0, keepdims=True)
        peak = jnp.maximum(peak[:, :tokens], peak[:, tokens:])
        weights = jnp.exp(scores - jnp.concatenate([peak, peak], axis=1))
        total = jnp.sum(weights, axis=0, keepdims=True)
        sums.append(total[:, :tokens] + total[:, tokens:])
        probs[turn - 1] = weights.astype(BF16)
    returns = []

    def give_back(turn):
        peer = lax.rem(frame + turn, frames)
        for side, (pair, target) in enumerate(((1 - here, far), (here, me))):
            if side == 1 and turn == frames:
                continue
            copy = pltpu.make_async_remote_copy(
                src_ref=done.at[pair, peer],
                dst_ref=back.at[here, frame],
                send_sem=out_send.at[side, turn],
                recv_sem=out_recv.at[side, turn],
                device_id={"rows": target, "frames": peer},
                device_id_type=MESH,
            )
            copy.start()
            returns.append(copy)

    for turn in order + [frames]:
        peer = lax.rem(frame + turn, frames)
        numerator = jnp.dot(
            values[:HD, :], probs[turn - 1, :, :tokens], preferred_element_type=F32
        ) + jnp.dot(values[HD:, :], probs[turn - 1, :, tokens:], preferred_element_type=F32)
        result = (numerator / sums[turn - 1]).astype(BF16)
        for pair in range(2):
            done[pair, peer] = result[:, pair * half : (pair + 1) * half]
        give_back(turn)
    back[here, frame] = done[here, frame]
    for copy in lent:
        copy.wait_recv()
    for copy in returns:
        copy.wait_recv()
    att[...] = back[...].reshape(-1, half).astype(F32).T.astype(BF16)
    mix = output_w[...].reshape(-1, output_w.shape[2])
    def mixed_term(owner):
        rows = pl.ds(pl.multiple_of(owner * size, size), size)
        return jnp.dot(att[rows, :], mix, preferred_element_type=F32)

    final[0] = mixed_term(1 - core).astype(BF16)
    swap = remote(
        final.at[0], final.at[1], sum_send.at[2 + 2 * PARTS], sum_recv.at[2 + 2 * PARTS], "rows", near
    )
    swap.start()
    mixed = mixed_term(core)
    swap.wait_recv()
    out_ref[...] = (hidden[...].astype(F32) + mixed + final[1].astype(F32)).astype(BF16)
    for copy in [first, second, swap] + over + gathers:
        copy.wait_send()
    for copy in lent + returns:
        copy.wait_send()
    for copy in moves:
        copy.wait_send()


def body_fast(
    latents,
    spatial_weight,
    spatial_bias,
    norm_gain,
    norm_shift,
    temporal_weight,
    temporal_bias,
    token_gain,
    query_weight,
    key_weight,
    value_weight,
    output_weight,
):
    channels = latents.shape[3]
    peers, frames = lax.axis_size("rows"), lax.axis_size("frames")
    block = latents.reshape(-1, channels)
    size = block.shape[0]
    tokens = size * peers
    width_cells = latents.shape[2]
    local_out = spatial_weight.shape[3]
    width = query_weight.shape[1] // frames
    main = local_out // LANES * LANES
    rest = local_out - main
    depth = CHUNK
    count = channels // depth
    denoised = pl.pallas_call(
        functools.partial(block_kernel, frames, width_cells, NORM_GROUPS // peers),
        out_shape=pltpu.VMEM(block.shape, BF16),
        in_specs=[ANY_SPEC] * 12,
        out_specs=VMEM_SPEC,
        scratch_shapes=[
            pltpu.VMEM((count, size, depth), BF16),
            pltpu.VMEM(block.shape, BF16),
            pltpu.VMEM(spatial_bias.shape, F32),
            pltpu.VMEM(norm_gain.shape, F32),
            pltpu.VMEM(norm_shift.shape, F32),
            pltpu.VMEM(temporal_bias.shape, F32),
            pltpu.VMEM(token_gain.shape, F32),
            pltpu.VMEM(spatial_weight.shape[:2] + (local_out, channels), BF16),
            pltpu.VMEM((3 * local_out, channels), BF16),
            pltpu.VMEM((3,) + query_weight.shape, BF16),
            pltpu.VMEM((2,) + output_weight.shape, BF16),
            pltpu.VMEM((count, peers, size, depth), BF16),
            pltpu.VMEM((count, 3, tokens + 2 * width_cells, depth), BF16),
            pltpu.VMEM((tokens, main), BF16),
            pltpu.VMEM((2, rest, tokens // 2), BF16),
            pltpu.VMEM((2, tokens, main), BF16),
            pltpu.VMEM((2, 2, rest, tokens // 2), BF16),
            pltpu.VMEM((2, tokens // 2, channels), F32),
            pltpu.VMEM(block.shape, BF16),
            pltpu.VMEM((peers,) + block.shape, BF16),
            pltpu.VMEM((2, frames, 3, size, LANES), BF16),
            pltpu.VMEM((2, frames, 3, size, LANES), BF16),
            pltpu.VMEM((LANES, 2 * frames * size), BF16),
            pltpu.VMEM((frames, 2 * frames * size, 2 * tokens), BF16),
            pltpu.VMEM((2, frames, width, tokens // 2), BF16),
            pltpu.VMEM((2, frames, width, tokens // 2), BF16),
            pltpu.VMEM((tokens // 2, 2 * frames * width), BF16),
            pltpu.VMEM((4,) + block.shape, BF16),
            pltpu.VMEM((2,) + block.shape, BF16),
            pltpu.VMEM(block.shape, BF16),
            pltpu.VMEM(block.shape, BF16),
            pltpu.VMEM((2,) + block.shape, F32),
            pltpu.VMEM((2,) + block.shape, BF16),
            DMA((11 + count,)),
            DMA((6,)),
            pltpu.SemaphoreType.REGULAR,
            DMA((3, count)),
            DMA((3, count)),
            DMA((2, peers)),
            DMA((2, peers)),
            DMA((2, PARTS)),
            DMA((2, PARTS)),
            DMA((2 * PARTS, frames)),
            DMA((2 * PARTS, frames)),
            DMA((2, frames + 1)),
            DMA((2, frames + 1)),
            DMA((3 + 2 * PARTS,)),
            DMA((3 + 2 * PARTS,)),
            DMA((2,)),
            DMA((2,)),
        ],
        compiler_params=pltpu.CompilerParams(
            collective_id=0, has_side_effects=True, vmem_limit_bytes=VMEM_LIMIT
        ),
    )(
        block,
        jnp.swapaxes(spatial_weight, 2, 3),
        spatial_bias,
        norm_gain,
        norm_shift,
        temporal_weight,
        temporal_bias,
        token_gain,
        query_weight,
        key_weight,
        value_weight,
        output_weight,
    )
    return denoised.reshape(latents.shape)


def fits(mesh):
    def choose(*args):
        latents, query_weight = args[0], args[8]
        peers, frames = mesh.shape["rows"], mesh.shape["frames"]
        heads = query_weight.shape[1] // HD
        tokens = latents.shape[0] * latents.shape[1] * latents.shape[2] * peers
        fast = (
            peers == 4
            and mesh.shape["frames"] == 4
            and latents.shape[3] % CHUNK == 0
            and args[1].shape[3] > LANES
            and args[1].shape[3] % LANES >= 16
            and args[1].shape[3] % 16 == 0
            and args[1].shape[3] % (8 * (NORM_GROUPS // peers)) == 0
            and latents.shape[1] == 1
            and heads == frames
            and 2 * HD == LANES
            and tokens % 256 == 0
            and latents.shape[2] % 16 == 0
            and latents.shape[0] * latents.shape[2] % (16 * PARTS) == 0
        )
        return (body_fast if fast else body)(*args)

    return choose


def solution(mesh):
    in_specs = (
        P("rows", ("groups", "frames"), None, None),
        P(None, None, None, "rows"),
        P("rows"),
        P("rows"),
        P("rows"),
        P(None, "rows", None),
        P(),
        P(),
        P(None, "rows"),
        P(None, "rows"),
        P(None, "rows"),
        P("rows", None),
    )
    out_specs = P("rows", ("groups", "frames"), None, None)
    return jax.shard_map(
        fits(mesh), mesh=mesh, in_specs=in_specs, out_specs=out_specs, check_vma=False
    )
```

```python
import functools
import math

import jax
import jax.numpy as jnp
from jax import lax
from jax.experimental import pallas as pl
from jax.experimental.pallas import tpu as pltpu
from jax.sharding import PartitionSpec as P

HD = 64
NORM_GROUPS = 32


def padded_2(array, sides, width):
    for axis, dim in sides:
        peers, length = (lax.axis_size(axis), array.shape[dim])
        up = [(i, (i + 1) % peers) for i in range(peers - 1)]
        down = [(j, i) for i, j in up]
        last = lax.slice_in_dim(array, length - width, length, axis=dim)
        leading = lax.slice_in_dim(array, 0, width, axis=dim)
        before = lax.ppermute(last, axis, up)
        after = lax.ppermute(leading, axis, down)
        array = jnp.concatenate([before, array, after], axis=dim)
    return array


def shifted_2(value, axis, steps):
    count = lax.axis_size(axis)
    pairs = [(source, (source + steps) % count) for source in range(count)]
    return lax.ppermute(value, axis, pairs)


def conv_plane(field, weight, bias):
    rows_n, frames_n, cols_n, chans = field.shape
    padded = jnp.pad(field, ((1, 1), (0, 0), (1, 1), (0, 0)))
    total = jnp.zeros((rows_n * frames_n * cols_n, weight.shape[3]), jnp.float32)
    for row_off in range(3):
        for col_off in range(3):
            window = padded[row_off : row_off + rows_n, :, col_off : col_off + cols_n, :].reshape(
                -1, chans
            )
            total = total + jnp.dot(
                window, weight[row_off, col_off], preferred_element_type=jnp.float32
            )
    return total.reshape(rows_n, frames_n, cols_n, -1) + bias


def layer_norm(field, token_gain):
    flat = field.astype(jnp.float32)
    token_mean = jnp.mean(flat, axis=-1, keepdims=True)
    shifted = flat - token_mean
    token_var = jnp.mean(shifted * shifted, axis=-1, keepdims=True)
    return (shifted / jnp.sqrt(token_var + 1e-05) * token_gain).astype(jnp.bfloat16)


def attend(queries, carried, keys, values):
    block = queries.shape[0]
    head_count = queries.shape[1]
    block_count = keys.shape[0] // block
    key_blocks = keys.reshape(block_count, block, head_count, HD)
    value_blocks = values.reshape(block_count, block, head_count, HD)
    scale = 1.0 / math.sqrt(HD)

    def visit_block(state, block_pair):
        running_max, denominator, numerator = state
        key_block, value_block = block_pair
        scores = (
            jnp.einsum("qhd,khd->qhk", queries, key_block, preferred_element_type=jnp.float32)
            * scale
        )
        new_max = jnp.maximum(running_max, jnp.max(scores, axis=-1))
        shrink = jnp.exp(running_max - new_max)
        weights = jnp.exp(scores - new_max[..., None])
        denominator = denominator * shrink + jnp.sum(weights, axis=-1)
        numerator = numerator * shrink[..., None] + jnp.einsum(
            "qhk,khd->qhd",
            weights.astype(jnp.bfloat16),
            value_block,
            preferred_element_type=jnp.float32,
        )
        return ((new_max, denominator, numerator), None)

    result, _ = lax.scan(visit_block, carried, (key_blocks, value_blocks))
    return result


def body(
    latents,
    spatial_weight,
    spatial_bias,
    norm_gain,
    norm_shift,
    temporal_weight,
    temporal_bias,
    token_gain,
    query_weight,
    key_weight,
    value_weight,
    output_weight,
):
    row_count, frame_count, width_cells, channels = latents.shape
    plane = lax.all_gather(latents, "rows", axis=0, tiled=True)
    plane_rows = plane.shape[0]
    local_out = spatial_weight.shape[3]
    spatial = conv_plane(plane, spatial_weight, spatial_bias)
    local_groups = NORM_GROUPS // lax.axis_size("rows")
    grouped = spatial.reshape(plane_rows, frame_count, width_cells, local_groups, -1)
    group_mean = jnp.mean(grouped, axis=(0, 2, 4), keepdims=True)
    centred = grouped - group_mean
    group_var = jnp.mean(centred * centred, axis=(0, 2, 4), keepdims=True)
    scaled = (centred / jnp.sqrt(group_var + 1e-05)).reshape(
        plane_rows, frame_count, width_cells, local_out
    ) * norm_gain + norm_shift
    activated = jax.nn.silu(scaled).astype(jnp.bfloat16)
    rim = padded_2(activated, (("frames", 1),), 1)
    row_total = row_count * lax.axis_size("rows")
    row_piece = rim
    total = jnp.zeros((row_total * frame_count * width_cells, channels), jnp.float32)
    for lag_index in range(3):
        window = row_piece[:, lag_index : lag_index + frame_count].reshape(-1, local_out)
        total = total + jnp.dot(
            window, temporal_weight[lag_index], preferred_element_type=jnp.float32
        )
    temporal = lax.psum_scatter(
        total.reshape(row_total, frame_count, width_cells, channels).astype(jnp.bfloat16),
        "rows",
        scatter_dimension=0,
        tiled=True,
    ).astype(jnp.float32)
    hidden = (latents.astype(jnp.float32) + temporal + temporal_bias).astype(jnp.bfloat16)
    normed_all = lax.all_gather(layer_norm(hidden, token_gain), "rows", axis=0, tiled=True)
    flat = normed_all.reshape(-1, channels)
    head_cols = query_weight.shape[1]
    head_count = head_cols // HD
    token_count = flat.shape[0]
    queries = jnp.dot(flat, query_weight, preferred_element_type=jnp.float32).astype(jnp.bfloat16)
    keys = jnp.dot(flat, key_weight, preferred_element_type=jnp.float32).astype(jnp.bfloat16)
    values = jnp.dot(flat, value_weight, preferred_element_type=jnp.float32).astype(jnp.bfloat16)
    start_state = (
        jnp.full((token_count, head_count), -1e30, jnp.float32),
        jnp.zeros((token_count, head_count), jnp.float32),
        jnp.zeros((token_count, head_count, HD), jnp.float32),
    )
    local_keys = keys.reshape(token_count, head_count, HD)
    local_values = values.reshape(token_count, head_count, HD)

    def travel(turn, state):
        query_moving, running_max, denominator, numerator = state
        running_max, denominator, numerator = attend(
            query_moving, (running_max, denominator, numerator), local_keys, local_values
        )
        return (
            shifted_2(query_moving, "frames", 1),
            shifted_2(running_max.astype(jnp.bfloat16), "frames", 1).astype(running_max.dtype),
            shifted_2(denominator.astype(jnp.bfloat16), "frames", 1).astype(denominator.dtype),
            shifted_2(numerator.astype(jnp.bfloat16), "frames", 1).astype(numerator.dtype),
        )

    start_moving = queries.reshape(token_count, head_count, HD)
    final = lax.fori_loop(0, lax.axis_size("frames"), travel, (start_moving,) + start_state)
    denominator, numerator = (final[2], final[3])
    attended = (
        (numerator / denominator[..., None])
        .astype(jnp.bfloat16)
        .reshape(plane_rows, frame_count, width_cells, head_cols)
    )
    row_piece = attended
    mixed = lax.psum_scatter(
        jnp.dot(row_piece.reshape(-1, head_cols), output_weight, preferred_element_type=jnp.float32)
        .reshape(row_count * lax.axis_size("rows"), frame_count, width_cells, channels)
        .astype(jnp.bfloat16),
        "rows",
        scatter_dimension=0,
        tiled=True,
    ).astype(jnp.float32)
    return (hidden.astype(jnp.float32) + mixed).astype(jnp.bfloat16)


MESH = pl.DeviceIdType.MESH
DMA = pltpu.SemaphoreType.DMA
VMEM_SPEC = pl.BlockSpec(memory_space=pltpu.VMEM)
ANY_SPEC = pl.BlockSpec(memory_space=pl.ANY)
BF16 = jnp.bfloat16
F32 = jnp.float32
VMEM_LIMIT = 54 << 20
PARTS = 2
CHUNK = 256
LANES = 128


def remote(src, dst, send, recv, axis, peer):
    return pltpu.make_async_remote_copy(
        src_ref=src,
        dst_ref=dst,
        send_sem=send,
        recv_sem=recv,
        device_id={axis: peer},
        device_id_type=MESH,
    )


def greet(barrier, axis, peer):
    pl.semaphore_signal(barrier, inc=1, device_id={axis: peer}, device_id_type=MESH)


def row(ref):
    return ref[...].reshape(1, -1)


def column(ref):
    value = jnp.broadcast_to(row(ref), (8, ref.shape[0]))
    return value.T[:, :1]


def convolve_chunk(plane, shifted, weight, chunk, width):
    blocks, size, depth = plane.shape
    tokens = blocks * size
    edge = jnp.zeros((width, depth), BF16)
    place = lax.broadcasted_iota(jnp.int32, (size, depth), 0) % width
    for offset in range(3):
        shifted[offset, :width, :] = edge
        shifted[offset, tokens + width :, :] = edge
    for block in range(blocks):
        rows = slice(width + block * size, width + (block + 1) * size)
        value = plane[block]
        wide = value.astype(F32)
        before = jnp.where(place == 0, 0.0, pltpu.roll(wide, 1, 0))
        after = jnp.where(place == width - 1, 0.0, pltpu.roll(wide, size - 1, 0))
        shifted[0, rows, :] = before.astype(BF16)
        shifted[1, rows, :] = value
        shifted[2, rows, :] = after.astype(BF16)
    total = None
    for row_off in range(3):
        for col_off in range(3):
            window = shifted[col_off, row_off * width : row_off * width + tokens, :]
            part = lax.dot_general(
                weight[row_off, col_off, :, chunk * depth : (chunk + 1) * depth],
                window,
                (((1,), (1,)), ((), ())),
                preferred_element_type=F32,
            )
            total = part if total is None else total + part
    return total


def group_norm_silu(spatial, gain, shift, groups):
    channels, tokens = spatial.shape

    def group_mean(value):
        return jnp.mean(value, axis=(1, 2), keepdims=True)

    grouped = spatial.reshape(groups, channels // groups, tokens)
    centred = grouped - group_mean(grouped)
    scale = 1.0 / jnp.sqrt(group_mean(centred * centred) + 1e-05)
    value = (centred * scale).reshape(channels, tokens) * gain + shift
    return value / (1.0 + jnp.exp(-value))


def block_kernel(
    frames,
    width_cells,
    groups,
    latents_hbm,
    spatial_hbm,
    bias_hbm,
    gain_hbm,
    shift_hbm,
    temporal_hbm,
    temporal_bias_hbm,
    token_gain_hbm,
    query_hbm,
    key_hbm,
    value_hbm,
    output_hbm,
    out_ref,
    chunks,
    latents,
    spatial_bias,
    norm_gain,
    norm_shift,
    temporal_bias,
    token_gain,
    spatial_w,
    temporal_w,
    project_w,
    output_w,
    plane,
    shifted,
    act,
    act_rest,
    halo,
    halo_rest,
    terms,
    hidden,
    normed_all,
    outgoing,
    got,
    values,
    probs,
    done,
    back,
    att,
    sent,
    got_near,
    got_far,
    got_own,
    partial,
    final,
    load_sem,
    tap_sem,
    ready,
    lat_send,
    lat_recv,
    halo_send,
    halo_recv,
    gat_send,
    gat_recv,
    in_send,
    in_recv,
    out_send,
    out_recv,
    sum_send,
    sum_recv,
    lend_send,
    lend_recv,
):
    me = lax.axis_index("rows")
    frame = lax.axis_index("frames")
    near, far = me ^ 1, me ^ 2
    has_prev, has_next = frame > 0, frame < frames - 1
    prev = jnp.maximum(frame - 1, 0)
    later = jnp.minimum(frame + 1, frames - 1)
    barrier = pltpu.get_barrier_semaphore()
    greet(barrier, "rows", far)

    @pl.when(has_next)
    def _():
        greet(barrier, "frames", later)

    @pl.when(has_prev)
    def _():
        greet(barrier, "frames", prev)

    greet(barrier, "rows", near)
    count, size, depth = chunks.shape
    main, rest = act.shape[1], act_rest.shape[1]
    loads, pieces = [], []
    for index in range(count):
        load = pltpu.make_async_copy(
            latents_hbm.at[:, index * depth : (index + 1) * depth],
            chunks.at[index],
            load_sem.at[index],
        )
        load.start()
        pieces.append(load)
    for index, (src, dst) in enumerate(
        (
            (bias_hbm, spatial_bias),
            (spatial_hbm, spatial_w),
            (gain_hbm, norm_gain),
            (shift_hbm, norm_shift),
            (latents_hbm, latents),
            (temporal_bias_hbm, temporal_bias),
            (token_gain_hbm, token_gain),
            (key_hbm, project_w.at[0]),
            (query_hbm, project_w.at[1]),
            (value_hbm, project_w.at[2]),
            (output_hbm, output_w.at[me // 2]),
        )
    ):
        load = pltpu.make_async_copy(src, dst, load_sem.at[count + index])
        load.start()
        loads.append(load)
        if index == 3:
            taps = []
            for tap in range(3):
                for start, stop, place in (
                    (0, main, tap * main),
                    (main, main + rest, 3 * main + tap * rest),
                ):
                    load = pltpu.make_async_copy(
                        temporal_hbm.at[tap, start:stop],
                        temporal_w.at[place : place + stop - start],
                        tap_sem.at[len(taps)],
                    )
                    load.start()
                    taps.append(load)
    for load in pieces:
        load.wait()
    pl.semaphore_wait(
        barrier, 2 + has_prev.astype(jnp.int32) + has_next.astype(jnp.int32)
    )

    across, onward = [], []
    for index in range(count):
        across.append(
            remote(
                chunks.at[index],
                plane.at[index, me],
                lat_send.at[0, index],
                lat_recv.at[0, index],
                "rows",
                far,
            )
        )
        onward.append(
            remote(
                plane.at[index, far],
                plane.at[index, far],
                lat_send.at[1, index],
                lat_recv.at[1, index],
                "rows",
                near,
            )
        )
        across[index].start()
    beside = remote(
        chunks, plane.at[:, me], lat_send.at[2, 0], lat_recv.at[2, 0], "rows", near
    )
    beside.start()
    for index in range(count):
        plane[index, me] = chunks[index]
    for load in loads[:2]:
        load.wait()
    beside.wait_recv()
    spatial = column(spatial_bias)
    for index in range(count):
        across[index].wait_recv()
        onward[index].start()
    here = me // 2
    depth_out = output_w.shape[1]
    early = depth_out * 4 // 16 // 16 * 16
    loads[10].wait()
    lent = []
    for index, rows in enumerate((pl.ds(0, early), pl.ds(early, depth_out - early))):
        lent.append(
            remote(
                output_w.at[here, rows],
                output_w.at[here, rows],
                lend_send.at[index],
                lend_recv.at[index],
                "rows",
                far,
            )
        )
    lent[0].start()
    for index in range(count):
        onward[index].wait_recv()
    for index in range(count):
        spatial = spatial + convolve_chunk(
            plane.at[index], shifted.at[index], spatial_w, index, width_cells
        )
    for load in loads[2:4]:
        load.wait()
    value = group_norm_silu(spatial, column(norm_gain), column(norm_shift), groups)
    half = act_rest.shape[2]
    act[...] = value[:main].T.astype(BF16)
    for pair in range(2):
        act_rest[pair] = value[main:, pair * half : (pair + 1) * half].astype(BF16)
    for copy in across + onward + [beside]:
        copy.wait_send()


    up, down = [], []
    for turn, pair in enumerate((1 - here, here)):
        rows = pl.ds(pl.multiple_of(pair * half, half), half)
        for side, (copies, peer) in enumerate(((up, later), (down, prev))):
            for index, (src, dst) in enumerate(
                ((act.at[rows], halo.at[side, rows]), (act_rest.at[pair], halo_rest.at[side, pair]))
            ):
                copies.append(
                    remote(
                        src,
                        dst,
                        halo_send.at[side, 2 * turn + index],
                        halo_recv.at[side, 2 * turn + index],
                        "frames",
                        peer,
                    )
                )

    sides = ((has_next, up), (has_prev, down))

    def launch(turn):
        for exists, copies in sides:

            @pl.when(exists)
            def _(part=copies[2 * turn : 2 * turn + 2]):
                for copy in part:
                    copy.start()

    def settle(turn):
        for exists, copies in sides:

            @pl.when(exists)
            def _(part=copies[2 * turn : 2 * turn + 2]):
                for copy in part:
                    copy.wait_send()

    launch(0)

    @pl.when(jnp.logical_not(has_prev))
    def _():
        halo[0] = jnp.zeros(halo.shape[1:], halo.dtype)
        halo_rest[0] = jnp.zeros(halo_rest.shape[1:], halo.dtype)

    @pl.when(jnp.logical_not(has_next))
    def _():
        halo[1] = jnp.zeros(halo.shape[1:], halo.dtype)
        halo_rest[1] = jnp.zeros(halo_rest.shape[1:], halo.dtype)

    settle(0)
    launch(1)
    for load in taps:
        load.wait()

    def temporal_term(pair, turn):
        rows = pl.ds(pl.multiple_of(pair * half, half), half)

        @pl.when(has_prev)
        def _():
            for copy in up[2 * turn : 2 * turn + 2]:
                copy.wait_recv()

        @pl.when(has_next)
        def _():
            for copy in down[2 * turn : 2 * turn + 2]:
                copy.wait_recv()

        left = jnp.concatenate([halo_rest[0, pair], act_rest[pair], halo_rest[1, pair]], axis=0)
        window = jnp.concatenate(
            [halo[0, rows, :], act[rows, :], halo[1, rows, :], left.astype(F32).T.astype(BF16)],
            axis=1,
        )
        return jnp.dot(window, temporal_w[...], preferred_element_type=F32)

    core = lax.rem(me, 2)
    step = size // PARTS
    spans = [slice(part * step, (part + 1) * step) for part in range(PARTS)]

    def share(slot, owner, part):
        start = pl.multiple_of(owner * size + part * step, step)
        return terms[slot, pl.ds(start, step), :]

    def hand(slot, pair):
        terms[slot] = temporal_term(pair, slot)
        for part, span in enumerate(spans):
            sent[slot, span, :] = share(slot, 1 - core, part).astype(BF16)
        copy = remote(
            sent.at[slot], got_near.at[slot], sum_send.at[slot], sum_recv.at[slot], "rows", near
        )
        copy.start()
        return copy

    first = hand(0, 1 - here)
    first.wait_recv()
    over = []
    for part, span in enumerate(spans):
        value = share(0, core, part) + got_near[0, span, :].astype(F32)
        partial[0, span, :] = value
        sent[2, span, :] = value.astype(BF16)
        copy = remote(
            sent.at[2, span],
            got_far.at[span],
            sum_send.at[2 + part],
            sum_recv.at[2 + part],
            "rows",
            far,
        )
        copy.start()
        over.append(copy)
    second = hand(1, here)
    second.wait_recv()
    for part, span in enumerate(spans):
        value = share(1, core, part) + got_near[1, span, :].astype(F32)
        partial[1, span, :] = value
        sent[3, span, :] = value.astype(BF16)
        copy = remote(
            sent.at[3, span],
            got_own.at[span],
            sum_send.at[2 + PARTS + part],
            sum_recv.at[2 + PARTS + part],
            "rows",
            far,
        )
        copy.start()
        over.append(copy)
    for load in loads[4:7]:
        load.wait()

    @pl.when(jnp.logical_and(has_prev, frame == frames - 3))
    def _():
        pl.semaphore_signal(ready, inc=1, device_id={"frames": prev}, device_id_type=MESH)

    @pl.when(jnp.logical_and(has_next, frame == 2))
    def _():
        pl.semaphore_signal(ready, inc=1, device_id={"frames": later}, device_id_type=MESH)

    settle(1)
    tokens = act.shape[0]
    moves = []
    order = sorted(range(1, frames), key=lambda turn: abs(2 * turn - frames))

    def project(pair, start, length, slot):
        slab = normed_all[pl.ds(2 * pair, 2), start : start + length, :]
        slab = slab.reshape(2 * length, slab.shape[2])
        span = pl.ds(start, length)
        for kind in range(3):
            cols = jnp.dot(slab, project_w[kind], preferred_element_type=F32)
            for owner in range(frames):
                head = cols[:, owner * HD : (owner + 1) * HD]
                outgoing[pair, owner, kind, span, :] = jnp.concatenate(
                    [head[:length], head[length:]], axis=1
                ).astype(BF16)
        for turn in order:
            peer = lax.rem(frame + turn, frames)
            copy = remote(
                outgoing.at[pair, peer, :, span],
                got.at[pair, frame, :, span],
                in_send.at[slot, turn],
                in_recv.at[slot, turn],
                "frames",
                peer,
            )
            copy.start()
            moves.append(copy)
        got[pair, frame, :, span, :] = outgoing[pair, frame, :, span, :]

    def normalise(slot, part, base, other):
        span = spans[part]
        total = partial[slot, span, :] + other[span, :].astype(F32) + row(temporal_bias)
        value = (base.astype(F32) + total).astype(BF16)
        flat = value.astype(F32)
        centred = flat - jnp.mean(flat, axis=-1, keepdims=True)
        var = jnp.mean(centred * centred, axis=-1, keepdims=True)
        return value, (centred / jnp.sqrt(var + 1e-05) * row(token_gain)).astype(BF16)

    gathers = []

    def give(block, slot, part, value):
        place = normed_all.at[block, spans[part]]
        normed_all[block, spans[part], :] = value
        copy = remote(
            place, place, gat_send.at[slot, part], gat_recv.at[slot, part], "rows", near
        )
        copy.start()
        gathers.append(copy)
        return copy

    def ready_part(index):
        slot, part = index // PARTS, index % PARTS
        span = spans[part]
        over[index].wait_recv()
        if slot == 0:
            hidden[span, :], value = normalise(1, part, latents[span, :], got_far)
            return give(me, 0, part, value)
        base = jnp.concatenate([plane[index, far, span, :] for index in range(count)], axis=1)
        _, value = normalise(0, part, base, got_own)
        return give(far, 1, part, value)

    pending = ready_part(0)
    for load in loads[7:10]:
        load.wait()

    @pl.when(jnp.logical_not(jnp.logical_and(has_prev, has_next)))
    def _():
        pl.semaphore_wait(ready, 1)

    for index in range(2 * PARTS):
        pending.wait_recv()
        eager = index >= PARTS
        if eager and index + 1 < 2 * PARTS:
            pending = ready_part(index + 1)
        project(here if index < PARTS else 1 - here, index % PARTS * step, step, index)
        if index == 1:
            lent[1].start()
        if not eager:
            pending = ready_part(index + 1)

    for copy in moves:
        copy.wait_recv()
    scale = 1.0 / math.sqrt(HD)
    keys = got[:, :, 0].reshape(-1, LANES)
    values[...] = got[:, :, 2].reshape(-1, LANES).astype(F32).T.astype(BF16)
    sums = []
    for turn in range(1, frames + 1):
        peer = lax.rem(frame + turn, frames)
        pieces = []
        for pair in range(2):
            flipped = got[pair, peer, 1].astype(F32).T
            pieces += [flipped[:HD], flipped[HD:]]
        query = (jnp.concatenate(pieces, axis=1) * scale).astype(BF16)
        zero = jnp.zeros_like(query)
        block = jnp.concatenate(
            [jnp.concatenate([query, zero], axis=1), jnp.concatenate([zero, query], axis=1)],
            axis=0,
        )
        scores = jnp.dot(keys, block, preferred_element_type=F32)
        peak = jnp.max(scores, axis=0, keepdims=True)
        peak = jnp.maximum(peak[:, :tokens], peak[:, tokens:])
        weights = jnp.exp(scores - jnp.concatenate([peak, peak], axis=1))
        total = jnp.sum(weights, axis=0, keepdims=True)
        sums.append(total[:, :tokens] + total[:, tokens:])
        probs[turn - 1] = weights.astype(BF16)
    returns = []

    def give_back(turn):
        peer = lax.rem(frame + turn, frames)
        for side, (pair, target) in enumerate(((1 - here, far), (here, me))):
            if side == 1 and turn == frames:
                continue
            copy = pltpu.make_async_remote_copy(
                src_ref=done.at[pair, peer],
                dst_ref=back.at[here, frame],
                send_sem=out_send.at[side, turn],
                recv_sem=out_recv.at[side, turn],
                device_id={"rows": target, "frames": peer},
                device_id_type=MESH,
            )
            copy.start()
            returns.append(copy)

    for turn in order + [frames]:
        peer = lax.rem(frame + turn, frames)
        numerator = jnp.dot(
            values[:HD, :], probs[turn - 1, :, :tokens], preferred_element_type=F32
        ) + jnp.dot(values[HD:, :], probs[turn - 1, :, tokens:], preferred_element_type=F32)
        result = (numerator / sums[turn - 1]).astype(BF16)
        for pair in range(2):
            done[pair, peer] = result[:, pair * half : (pair + 1) * half]
        give_back(turn)
    back[here, frame] = done[here, frame]
    for copy in lent:
        copy.wait_recv()
    for copy in returns:
        copy.wait_recv()
    att[...] = back[...].reshape(-1, half).astype(F32).T.astype(BF16)
    mix = output_w[...].reshape(-1, output_w.shape[2])
    def mixed_term(owner):
        rows = pl.ds(pl.multiple_of(owner * size, size), size)
        return jnp.dot(att[rows, :], mix, preferred_element_type=F32)

    final[0] = mixed_term(1 - core).astype(BF16)
    swap = remote(
        final.at[0], final.at[1], sum_send.at[2 + 2 * PARTS], sum_recv.at[2 + 2 * PARTS], "rows", near
    )
    swap.start()
    mixed = mixed_term(core)
    swap.wait_recv()
    out_ref[...] = (hidden[...].astype(F32) + mixed + final[1].astype(F32)).astype(BF16)
    for copy in [first, second, swap] + over + gathers:
        copy.wait_send()
    for copy in lent + returns:
        copy.wait_send()
    for copy in moves:
        copy.wait_send()


def body_fast(
    latents,
    spatial_weight,
    spatial_bias,
    norm_gain,
    norm_shift,
    temporal_weight,
    temporal_bias,
    token_gain,
    query_weight,
    key_weight,
    value_weight,
    output_weight,
):
    channels = latents.shape[3]
    peers, frames = lax.axis_size("rows"), lax.axis_size("frames")
    block = latents.reshape(-1, channels)
    size = block.shape[0]
    tokens = size * peers
    width_cells = latents.shape[2]
    local_out = spatial_weight.shape[3]
    width = query_weight.shape[1] // frames
    main = local_out // LANES * LANES
    rest = local_out - main
    depth = CHUNK
    count = channels // depth
    denoised = pl.pallas_call(
        functools.partial(block_kernel, frames, width_cells, NORM_GROUPS // peers),
        out_shape=pltpu.VMEM(block.shape, BF16),
        in_specs=[ANY_SPEC] * 12,
        out_specs=VMEM_SPEC,
        scratch_shapes=[
            pltpu.VMEM((count, size, depth), BF16),
            pltpu.VMEM(block.shape, BF16),
            pltpu.VMEM(spatial_bias.shape, F32),
            pltpu.VMEM(norm_gain.shape, F32),
            pltpu.VMEM(norm_shift.shape, F32),
            pltpu.VMEM(temporal_bias.shape, F32),
            pltpu.VMEM(token_gain.shape, F32),
            pltpu.VMEM(spatial_weight.shape[:2] + (local_out, channels), BF16),
            pltpu.VMEM((3 * local_out, channels), BF16),
            pltpu.VMEM((3,) + query_weight.shape, BF16),
            pltpu.VMEM((2,) + output_weight.shape, BF16),
            pltpu.VMEM((count, peers, size, depth), BF16),
            pltpu.VMEM((count, 3, tokens + 2 * width_cells, depth), BF16),
            pltpu.VMEM((tokens, main), BF16),
            pltpu.VMEM((2, rest, tokens // 2), BF16),
            pltpu.VMEM((2, tokens, main), BF16),
            pltpu.VMEM((2, 2, rest, tokens // 2), BF16),
            pltpu.VMEM((2, tokens // 2, channels), F32),
            pltpu.VMEM(block.shape, BF16),
            pltpu.VMEM((peers,) + block.shape, BF16),
            pltpu.VMEM((2, frames, 3, size, LANES), BF16),
            pltpu.VMEM((2, frames, 3, size, LANES), BF16),
            pltpu.VMEM((LANES, 2 * frames * size), BF16),
            pltpu.VMEM((frames, 2 * frames * size, 2 * tokens), BF16),
            pltpu.VMEM((2, frames, width, tokens // 2), BF16),
            pltpu.VMEM((2, frames, width, tokens // 2), BF16),
            pltpu.VMEM((tokens // 2, 2 * frames * width), BF16),
            pltpu.VMEM((4,) + block.shape, BF16),
            pltpu.VMEM((2,) + block.shape, BF16),
            pltpu.VMEM(block.shape, BF16),
            pltpu.VMEM(block.shape, BF16),
            pltpu.VMEM((2,) + block.shape, F32),
            pltpu.VMEM((2,) + block.shape, BF16),
            DMA((11 + count,)),
            DMA((6,)),
            pltpu.SemaphoreType.REGULAR,
            DMA((3, count)),
            DMA((3, count)),
            DMA((2, peers)),
            DMA((2, peers)),
            DMA((2, PARTS)),
            DMA((2, PARTS)),
            DMA((2 * PARTS, frames)),
            DMA((2 * PARTS, frames)),
            DMA((2, frames + 1)),
            DMA((2, frames + 1)),
            DMA((3 + 2 * PARTS,)),
            DMA((3 + 2 * PARTS,)),
            DMA((2,)),
            DMA((2,)),
        ],
        compiler_params=pltpu.CompilerParams(
            collective_id=0, has_side_effects=True, vmem_limit_bytes=VMEM_LIMIT
        ),
    )(
        block,
        jnp.swapaxes(spatial_weight, 2, 3),
        spatial_bias,
        norm_gain,
        norm_shift,
        temporal_weight,
        temporal_bias,
        token_gain,
        query_weight,
        key_weight,
        value_weight,
        output_weight,
    )
    return denoised.reshape(latents.shape)


def fits(mesh):
    def choose(*args):
        latents, query_weight = args[0], args[8]
        peers, frames = mesh.shape["rows"], mesh.shape["frames"]
        heads = query_weight.shape[1] // HD
        tokens = latents.shape[0] * latents.shape[1] * latents.shape[2] * peers
        fast = (
            peers == 4
            and mesh.shape["frames"] == 4
            and latents.shape[3] % CHUNK == 0
            and args[1].shape[3] > LANES
            and args[1].shape[3] % LANES >= 16
            and args[1].shape[3] % 16 == 0
            and args[1].shape[3] % (8 * (NORM_GROUPS // peers)) == 0
            and latents.shape[1] == 1
            and heads == frames
            and 2 * HD == LANES
            and tokens % 256 == 0
            and latents.shape[2] % 16 == 0
            and latents.shape[0] * latents.shape[2] % (16 * PARTS) == 0
        )
        return (body_fast if fast else body)(*args)

    return choose


def solution(mesh):
    in_specs = (
        P("rows", ("groups", "frames"), None, None),
        P(None, None, None, "rows"),
        P("rows"),
        P("rows"),
        P("rows"),
        P(None, "rows", None),
        P(),
        P(),
        P(None, "rows"),
        P(None, "rows"),
        P(None, "rows"),
        P("rows", None),
    )
    out_specs = P("rows", ("groups", "frames"), None, None)
    return jax.shard_map(
        fits(mesh), mesh=mesh, in_specs=in_specs, out_specs=out_specs, check_vma=False
    )
```
